32 devices in a mesh: grp: 2 (over y), seq: 4 (over z), head: 2 (over x), rep: 2 (over core).
Axes of the slice: x: 2, y: 2, z: 4, core: 2. Of those that a mesh axis runs over, the one named last changes fastest.
Arguments:
- spectrum: float32 [4, 3, 128, 4096], P('grp', None, ('seq', 'head', 'rep')), parts along dimension 0, may hold values from -6 to 6
- src_amp: float32 [32, 3], P('grp'), parts along dimension 0, may hold values from -6 to 6
- src_phase: float32 [32], P('grp'), parts along dimension 0, may hold values from -3.140625 to 3.140625
- src_mode: int32 [32], P('grp'), parts along dimension 0, may hold values from 1 to 4
- src_delay: int32 [32], P('grp'), parts along dimension 0, may hold values from 0 to 511
- src_bins: int32 [32, 2], P('grp'), parts along dimension 0, may hold values from 0 to 524287, as said below
- w_embed: bfloat16 [384, 1024], replicated, may hold values from -0.3125 to 0.3125
- norm_in: bfloat16 [1024], replicated, may hold values from 0.5 to 1.5
- w_z: bfloat16 [1024, 2048], P(None, ('head', 'rep')), may hold values from -0.1875 to 0.1875
- w_x: bfloat16 [1024, 2048], P(None, ('head', 'rep')), may hold values from -0.1875 to 0.1875
- w_bc: bfloat16 [1024, 256], replicated, may hold values from -0.1875 to 0.1875
- w_dt: bfloat16 [1024, 32], P(None, ('head', 'rep')), may hold values from -0.5625 to 0.5625
- dt_bias: float32 [32], P(('head', 'rep')), may hold values from -4 to -2
- a_log: float32 [32], P(('head', 'rep')), may hold values from -11 to -1.5
- conv_x: float32 [4, 2048], P(None, ('head', 'rep')), may hold values from -3 to 3
- conv_bc: float32 [4, 256], replicated, may hold values from -3 to 3
- norm_out: bfloat16 [2048], replicated, may hold values from 0.5 to 1.5
- w_out: bfloat16 [2048, 1024], replicated, may hold values from -0.125 to 0.125
Outputs:
- summary: bfloat16 [16384, 1024], P(('grp', 'seq', 'head', 'rep')), parts along dimension 0
The draws below stay inside these ranges and needn't reach their ends.
There are 2 independent parts, one for each index of `grp`. The reference program is written for one: setup_inputs(seed, part) draws one part's arguments, and reference() takes and returns one part's arrays. A program takes and returns all parts, laid end to end along the dimension named above; an argument that names none is the same for every part. Nothing has to cross between parts.
Inputs may be any that keep to these rules, and one draw needn't show every extreme that they name: src_bins[s, 0] is the first frequency bin of source s and src_bins[s, 1] one past its last; the first is smaller than the second; some source starts at bin 0 and some has src_bins[s, 1] = 524287.
All inputs are finite; a program needn't handle non-finite values.
Results may differ from the reference program's by a relative error of at most 0.0065.
Values may be sent and summed in bfloat16 or wider, within the bound.
No kernel may reach another device: no remote copies, remote signals or barrier semaphores. Data moves between devices by JAX's collectives and lax.ppermute only.
A program may use at most 128 MiB of HBM per device.

```python
import math
import jax
import jax.numpy as jnp
from jax import lax

D = 1024
HEADS = 32
HEADDIM = 64
STATE = 128
SPAN = 256
CONV = 4
CHANS = 3
PATCH = 64
SOURCES = 16
TOK_DEV = 2048
DIN = 2048
TOKENS = 8192
SAMPLES = 524288
ROWS_FT = 128
COLS_FT = 4096


def draw_src_bins(key, part):
    first_key = jax.random.fold_in(key, 11)
    second_key = jax.random.fold_in(key, 12)
    lower_bin = jax.random.randint(first_key, (SOURCES,), 0, SAMPLES // 2)
    band_width = jax.random.randint(second_key, (SOURCES,), SAMPLES // 32, SAMPLES // 2 + 1)
    source_ids = jnp.arange(SOURCES, dtype=jnp.int32)
    lower_bin = jnp.where(source_ids == 0, 0, lower_bin)
    upper_bin = lower_bin + band_width
    upper_bin = jnp.where(source_ids == SOURCES - 1, SAMPLES - 1, upper_bin)
    return jnp.stack([lower_bin, upper_bin], axis=1).astype(jnp.int32)


def draw_a_log(key, part):
    unit = jax.random.uniform(jax.random.fold_in(key, 21), (HEADS,), jnp.float32)
    low_end = jnp.log(jnp.float32(0.03))
    high_end = jnp.log(jnp.float32(3.0))
    target = low_end + unit * (high_end - low_end)
    return (target - jnp.log(jnp.float32(0.6 * TOK_DEV))).astype(jnp.float32)


def with_ends(array, stream_key, low, high):
    longest = array.shape.index(max(array.shape))
    spots = []
    for shift in (0, 1):
        where = [jax.random.randint(jax.random.fold_in(stream_key, axis), (), 0, length) for axis, length in enumerate(array.shape)]
        where[longest] = (where[longest] + shift) % array.shape[longest]
        spots.append(tuple(where))
    return array.at[spots[0]].set(low).at[spots[1]].set(high)


def level_of(own_key, dims, split, least, high):
    def one(dim, parts):
        draws = jax.random.uniform(jax.random.fold_in(jax.random.fold_in(own_key, 6), dim), (parts,), jnp.float32, least / len(split), high / len(split))
        return jnp.repeat(jnp.exp(draws), dims[dim] // parts).reshape((-1,) + (1,) * (len(dims) - dim - 1))

    factor_of = one(*split[0])
    for cut in split[1:]:
        factor_of = factor_of * one(*cut)
    return factor_of


def noise(key, dims, deviation, bound, shards=(), kind=jnp.bfloat16):
    entries = jax.random.normal(key, dims, jnp.float32) * deviation
    if len(shards) > 0:
        entries = level_of(key, dims, shards, -0.22, 0.18) * entries
    return jnp.clip(entries, min=-bound, max=bound).astype(kind)


def setup_inputs(seed: int = 0, part: int = 0) -> dict:
    arg_keys = jax.random.split(jax.random.key(seed), 19)
    part_keys = jax.random.split(jax.random.fold_in(arg_keys[18], part), 19)
    spectrum = noise(part_keys[0], (2, CHANS, ROWS_FT, COLS_FT), 1.0, 6.0, ((2, 16),), jnp.float32)
    src_amp = noise(part_keys[1], (SOURCES, CHANS), 1.5, 6.0, (), jnp.float32)
    src_phase = jnp.clip(jax.random.uniform(part_keys[2], (SOURCES,), jnp.float32, -3.140625, 3.140625), -3.140625, 3.140625)
    src_mode = with_ends(jax.random.randint(part_keys[3], (SOURCES,), 1, 5), jax.random.fold_in(part_keys[3], 1), 1, 4).astype(jnp.int32)
    src_delay = with_ends(jax.random.randint(part_keys[4], (SOURCES,), 0, 512), jax.random.fold_in(part_keys[4], 1), 0, 511).astype(jnp.int32)
    src_bins = draw_src_bins(jax.random.fold_in(jax.random.fold_in(arg_keys[18], part), 71), part)
    w_embed = noise(arg_keys[6], (2 * CHANS * PATCH, D), (2 * CHANS * PATCH) ** -0.5, 0.3125)
    norm_in = jnp.clip(1.0 + 0.1 * jax.random.normal(arg_keys[7], (D,), jnp.float32), 0.5, 1.5).astype(jnp.bfloat16)
    w_z = noise(arg_keys[8], (D, DIN), D ** -0.5, 0.1875, ((1, 4),))
    w_x = noise(arg_keys[9], (D, DIN), D ** -0.5, 0.1875, ((1, 4),))
    w_bc = noise(arg_keys[10], (D, 2 * STATE), D ** -0.5, 0.1875)
    w_dt = noise(arg_keys[11], (D, HEADS), (3.0 * D ** -0.5), 0.5625, ((1, 4),))
    dt_bias = jnp.clip(-4.0 + 2.0 * jax.random.uniform(arg_keys[12], (HEADS,), jnp.float32) ** level_of(arg_keys[12], (HEADS,), ((0, 4),), -0.2, 0.2), -4.0, -2.0)
    a_log = draw_a_log(jax.random.fold_in(arg_keys[18], 71), part)
    conv_x = noise(arg_keys[14], (CONV, DIN), 0.5, 3.0, ((1, 4),), jnp.float32)
    conv_bc = noise(arg_keys[15], (CONV, 2 * STATE), 0.5, 3.0, (), jnp.float32)
    norm_out = jnp.clip(1.0 + 0.1 * jax.random.normal(arg_keys[16], (DIN,), jnp.float32), 0.5, 1.5).astype(jnp.bfloat16)
    w_out = noise(arg_keys[17], (DIN, D), DIN ** -0.5, 0.125)
    return {"spectrum": spectrum, "src_amp": src_amp, "src_phase": src_phase, "src_mode": src_mode, "src_delay": src_delay, "src_bins": src_bins, "w_embed": w_embed, "norm_in": norm_in, "w_z": w_z, "w_x": w_x, "w_bc": w_bc, "w_dt": w_dt, "dt_bias": dt_bias, "a_log": a_log, "conv_x": conv_x, "conv_bc": conv_bc, "norm_out": norm_out, "w_out": w_out}


EPSILON = 1e-05

def harmonic_angle(position, harmonic, lag_bins, phase_shift, length):
    turn_count = position * lag_bins % length * harmonic % length
    return harmonic.astype(phase_shift.dtype) * phase_shift + turn_count.astype(phase_shift.dtype) * (2.0 * math.pi / length)

def rms_scale(values):
    return lax.rsqrt(lax.optimization_barrier(jnp.mean(values * values, axis=-1, keepdims=True)) + EPSILON)

def causal_conv(padded, kernel, row_count):
    accumulated = kernel[0][None, :] * padded[0:row_count].astype(jnp.float32)
    for tap_index in range(1, kernel.shape[0]):
        accumulated = accumulated + kernel[tap_index][None, :] * padded[tap_index:tap_index + row_count].astype(jnp.float32)
    return jax.nn.silu(accumulated).astype(jnp.bfloat16)

def reference(spectrum, src_amp, src_phase, src_mode, src_delay, src_bins, w_embed, norm_in, w_z, w_x, w_bc, w_dt, dt_bias, a_log, conv_x, conv_bc, norm_out, w_out):
    float_kind = spectrum.dtype
    length = SAMPLES
    spectra = jnp.transpose(spectrum, (0, 1, 3, 2)).reshape(2, CHANS, length)
    position = jnp.arange(length, dtype=jnp.int32)

    def add_source(source, accumulated):
        lower_bin = src_bins[source, 0]
        upper_bin = src_bins[source, 1]
        inside = jnp.where((position >= lower_bin) & (position < upper_bin), 1.0, 0.0).astype(float_kind)
        angle_now = harmonic_angle(position, src_mode[source], src_delay[source], src_phase[source], length)
        wave_pair = jnp.stack([inside * jnp.cos(angle_now), inside * jnp.sin(angle_now)])
        return accumulated + src_amp[source][None, :, None] * wave_pair[:, None, :]
    spectra = lax.fori_loop(0, SOURCES, add_source, spectra)
    complex_series = jnp.fft.ifft(spectra[0] + 1j * spectra[1], axis=-1) * math.sqrt(length)
    series = jnp.stack([jnp.real(complex_series), jnp.imag(complex_series)]).astype(float_kind)
    patches = series.reshape(2, CHANS, TOKENS, PATCH).transpose(2, 0, 1, 3).reshape(TOKENS, 2 * CHANS * PATCH).astype(jnp.bfloat16)
    embedded = jnp.dot(patches, w_embed, preferred_element_type=jnp.float32).astype(jnp.bfloat16)
    embedded_f = embedded.astype(jnp.float32)
    normed_in = (embedded_f * rms_scale(embedded_f) * norm_in.astype(jnp.float32)).astype(jnp.bfloat16)
    gate_in = jnp.dot(normed_in, w_z, preferred_element_type=jnp.float32).astype(jnp.bfloat16)
    x_raw = jnp.dot(normed_in, w_x, preferred_element_type=jnp.float32).astype(jnp.bfloat16)
    bc_raw = jnp.dot(normed_in, w_bc, preferred_element_type=jnp.float32).astype(jnp.bfloat16)
    dt_raw = jnp.dot(normed_in, w_dt, preferred_element_type=jnp.float32)
    x_conv = causal_conv(jnp.concatenate([jnp.zeros((CONV - 1, DIN), jnp.bfloat16), x_raw], 0), conv_x, TOKENS)
    bc_conv = causal_conv(jnp.concatenate([jnp.zeros((CONV - 1, 2 * STATE), jnp.bfloat16), bc_raw], 0), conv_bc, TOKENS)
    step_size = jax.nn.softplus(dt_raw + dt_bias[None, :])
    decay_rate = -jnp.exp(a_log)
    blocks = TOKENS // SPAN
    x_blocks = x_conv.reshape(blocks, SPAN, HEADS, HEADDIM)
    b_blocks = bc_conv[:, :STATE].reshape(blocks, SPAN, STATE)
    c_blocks = bc_conv[:, STATE:].reshape(blocks, SPAN, STATE)
    step_blocks = step_size.reshape(blocks, SPAN, HEADS)
    causal_mask = jnp.arange(SPAN)[:, None] >= jnp.arange(SPAN)[None, :]

    def block_step(carried, block_data):
        x_block, b_block, c_block, step_block = block_data
        cumulative = jnp.cumsum(step_block * decay_rate[None, :], axis=0)
        by_head = cumulative.T
        spread = by_head[:, :, None] - by_head[:, None, :]
        segment = jnp.exp(jnp.where(causal_mask[None], spread, -jnp.inf))
        gram_matrix = jnp.dot(c_block, b_block.T, preferred_element_type=jnp.float32)
        scores = (gram_matrix[None] * segment * step_block.T[:, None, :]).astype(jnp.bfloat16)
        x_float = x_block.astype(jnp.float32)
        y_diag = jnp.einsum('htk,khp->thp', scores.astype(jnp.float32), x_float)
        weights_in = jnp.exp(cumulative[-1][None, :] - cumulative) * step_block
        weighted = (b_block.astype(jnp.float32)[:, None, :] * weights_in[:, :, None]).astype(jnp.bfloat16)
        states = jnp.einsum('khs,khp->hsp', weighted.astype(jnp.float32), x_float)
        y_off = jnp.einsum('ts,hsp->thp', c_block.astype(jnp.float32), carried, precision=lax.Precision.HIGHEST) * jnp.exp(cumulative)[:, :, None]
        following = jnp.exp(cumulative[-1])[:, None, None] * carried + states
        return (following, y_diag + y_off)
    _, outputs = lax.scan(block_step, jnp.zeros((HEADS, STATE, HEADDIM), float_kind), (x_blocks, b_blocks, c_blocks, step_blocks))
    y_all = outputs.reshape(TOKENS, DIN)
    gated_out = (y_all * jax.nn.silu(gate_in.astype(jnp.float32))).astype(jnp.bfloat16)
    gated_f = gated_out.astype(jnp.float32)
    normed = (gated_f * rms_scale(gated_f) * norm_out.astype(jnp.float32)).astype(jnp.bfloat16)
    mixed_out = jnp.dot(normed, w_out, preferred_element_type=jnp.float32)
    return (embedded_f + mixed_out).astype(jnp.bfloat16)
```

```python
import functools
import math

import jax
import jax.numpy as jnp
import ml_dtypes
import numpy as np
from jax import lax
from jax.experimental import pallas as pl
from jax.experimental.pallas import tpu as pltpu
from jax.sharding import PartitionSpec as P

SPAN = 256
EPSILON = 1e-05
LANES = 128
PATCH = 64
ALL = ("seq", "head", "rep")
HR = ("head", "rep")
F32 = jnp.float32
BF16 = jnp.bfloat16
VMEM = pl.BlockSpec(memory_space=pltpu.VMEM)
SMEM = pl.BlockSpec(memory_space=pltpu.SMEM)
PARAMS = pltpu.CompilerParams(vmem_limit_bytes=56 * 1024 * 1024)


def two_halves(table):
    high = table.astype(ml_dtypes.bfloat16)
    return high, (table - high.astype(np.float64)).astype(ml_dtypes.bfloat16)


def mm(a, b):
    return jnp.dot(a, b, preferred_element_type=F32)


def split(a):
    high = a.astype(BF16)
    return high, (a - high.astype(F32)).astype(BF16)


def lane_bins(inner):
    parts = PATCH // inner
    lane = np.arange(LANES)
    width = LANES // parts
    return lane // width + parts * (lane % width)


def inverse_fft(real, imag):
    count = len(real)
    if count == 1:
        return real, imag
    even_r, even_i = inverse_fft(real[0::2], imag[0::2])
    odd_r, odd_i = inverse_fft(real[1::2], imag[1::2])
    half = count // 2
    out_r, out_i = [None] * count, [None] * count
    for k in range(half):
        angle = 2.0 * math.pi * k / count
        c, s = math.cos(angle), math.sin(angle)
        if k == 0:
            r, i = odd_r[k], odd_i[k]
        elif 4 * k == count:
            r, i = -odd_i[k], odd_r[k]
        else:
            r = odd_r[k] * c - odd_i[k] * s
            i = odd_r[k] * s + odd_i[k] * c
        out_r[k], out_i[k] = even_r[k] + r, even_i[k] + i
        out_r[k + half], out_i[k + half] = even_r[k] - r, even_i[k] - i
    return out_r, out_i


def first_section(
    rows_all, length, pos, amp, phase, mode, delay, bins, turn_ref, x_ref, twist_ref, high_ref, low_ref,
    out_ref, base, acc, lhs,
):
    channels = amp.shape[1]
    sources = amp.shape[0]
    inner = x_ref.shape[2]
    row_block = x_ref.shape[3]
    shape = (row_block, LANES)
    row = pos[0] * row_block + lax.broadcasted_iota(jnp.int32, shape, 0)
    lane = lax.broadcasted_iota(jnp.int32, shape, 1)
    first_bin = row + rows_all * lane
    unit = 2.0 * math.pi / length

    def make_base(s, _):
        turn = ((((first_bin * delay[s]) & (length - 1)) * mode[s]) & (length - 1)).astype(F32)
        angle = mode[s].astype(F32) * phase[s] + turn * unit
        base[0, s] = jnp.cos(angle)
        base[1, s] = jnp.sin(angle)
        return 0

    lax.fori_loop(0, sources, make_base, 0)

    def add_sources(v, _):
        here = first_bin + (rows_all * LANES) * v
        total = [x_ref[r, c, v] for r in range(2) for c in range(channels)]
        for s in range(sources):
            which = (delay[s] * mode[s] * v) & (inner - 1)
            tr, ti = turn_ref[0, which], turn_ref[1, which]
            inside = (here >= bins[s, 0]) & (here < bins[s, 1])
            br, bi = base[0, s], base[1, s]
            real = jnp.where(inside, br * tr - bi * ti, 0.0)
            imag = jnp.where(inside, br * ti + bi * tr, 0.0)
            for c in range(channels):
                total[c] = total[c] + amp[s, c] * real
                total[channels + c] = total[channels + c] + amp[s, c] * imag
        for n in range(2 * channels):
            acc[n, v] = total[n]
        return 0

    lax.fori_loop(0, inner, add_sources, 0)

    def transform(c, _):
        real, imag = inverse_fft(
            [acc[c, v] for v in range(inner)], [acc[channels + c, v] for v in range(inner)]
        )
        for q in range(inner):
            tc, ts = twist_ref[0, q : q + 1, :], twist_ref[1, q : q + 1, :]
            lhs[c, q, :, 0:LANES] = real[q] * tc - imag[q] * ts
            lhs[c, q, :, LANES : 2 * LANES] = real[q] * ts + imag[q] * tc
        return 0

    lax.fori_loop(0, channels, transform, 0)

    wide = (inner, row_block, LANES)
    parts = PATCH // inner
    width = LANES // parts
    lanes = lax.broadcasted_iota(jnp.int32, wide, 2)
    outer = lax.div(lanes, width) + parts * lax.rem(lanes, width)
    column = lax.broadcasted_iota(jnp.int32, wide, 0) + inner * outer
    rows = pos[0] * row_block + lax.broadcasted_iota(jnp.int32, wide, 1)
    angle = ((rows * column) & (length - 1)).astype(F32) * unit
    cos, sin = jnp.cos(angle), jnp.sin(angle)
    for c in range(channels):
        high, low = split(lhs[c].reshape(inner * row_block, 2 * LANES))
        got = mm(high, high_ref[...]) + mm(low, high_ref[...]) + mm(high, low_ref[...])
        real = got[:, 0:LANES].reshape(wide)
        imag = got[:, LANES : 2 * LANES].reshape(wide)
        out_ref[:, c] = (real * cos - imag * sin).astype(BF16)
        out_ref[:, channels + c] = (real * sin + imag * cos).astype(BF16)


def run_first(spectrum, amp, phase, mode, delay, bins, pos, rows_all, length):
    _, channels, row_block, columns = spectrum.shape
    inner = columns // LANES
    grid_in = spectrum.reshape(2, channels, row_block, inner, LANES).transpose(0, 1, 3, 2, 4)
    steps = np.arange(inner)
    turn = 2.0 * np.pi * steps / inner
    turns = np.stack([np.cos(turn), np.sin(turn)]).astype(np.float32)
    lane = np.arange(LANES)
    twist = 2.0 * np.pi * (steps[:, None] * lane[None, :] % columns) / columns
    twists = np.stack([np.cos(twist), np.sin(twist)]).astype(np.float32)
    angle = 2.0 * np.pi * (lane[:, None] * lane_bins(inner)[None, :] % LANES) / LANES
    cos, sin = np.cos(angle), np.sin(angle)
    high, low = two_halves(np.block([[cos, sin], [-sin, cos]]))
    return pl.pallas_call(
        functools.partial(first_section, rows_all, length),
        out_shape=jax.ShapeDtypeStruct((inner, 2 * channels, row_block, LANES), BF16),
        in_specs=[SMEM] * 7 + [VMEM] * 4,
        out_specs=VMEM,
        scratch_shapes=[
            pltpu.VMEM((2, amp.shape[0], row_block, LANES), F32),
            pltpu.VMEM((2 * channels, inner, row_block, LANES), F32),
            pltpu.VMEM((channels, inner, row_block, 2 * LANES), F32),
        ],
        compiler_params=PARAMS,
        name="first_section",
    )(pos, amp, phase, mode, delay, bins, turns, grid_in, twists, high, low)


def second_section(z_ref, high_ref, low_ref, out_ref):
    devices, own, pairs, row_block, _ = z_ref.shape
    channels = pairs // 2
    rows = devices * row_block
    for q in range(own):
        for c in range(channels):
            right = jnp.concatenate(
                [z_ref[:, q, r * channels + c].astype(F32).reshape(rows, LANES) for r in range(2)], axis=0
            ).astype(BF16)
            got = mm(high_ref[...], right) + mm(low_ref[...], right)
            for r in range(2):
                out_ref[:, q * pairs + r * channels + c] = (
                    got[r * rows : (r + 1) * rows].reshape(devices, row_block, LANES).astype(BF16)
                )


def run_second(z, length):
    devices, own, pairs, row_block, _ = z.shape
    rows = devices * row_block
    counter = np.arange(rows)
    angle = 2.0 * np.pi * (counter[:, None] * counter[None, :] % rows) / rows
    cos, sin = np.cos(angle), np.sin(angle)
    high, low = two_halves(np.block([[cos, -sin], [sin, cos]]) / math.sqrt(length))
    return pl.pallas_call(
        second_section,
        out_shape=jax.ShapeDtypeStruct((devices, own * pairs, row_block, LANES), BF16),
        in_specs=[VMEM] * 3,
        out_specs=VMEM,
        compiler_params=PARAMS,
        name="second_section",
    )(z, high, low)


def order_patches(x_ref, perm_ref, out_ref, wide):
    devices, own, row_block, _ = x_ref.shape
    parts = perm_ref.shape[0]
    width = LANES // parts
    wide[...] = x_ref[...].astype(F32).reshape(devices * own * row_block, LANES)
    for m in range(row_block):
        rows = wide[pl.ds(m, devices * own, stride=row_block), :]
        across = rows.T.astype(BF16)
        total = mm(across[0:width], perm_ref[0])
        for n in range(1, parts):
            total = total + mm(across[n * width : (n + 1) * width], perm_ref[n])
        out_ref[m * width : (m + 1) * width, :] = total.astype(BF16)


def run_order(x, inner, channels):
    devices, own, row_block, _ = x.shape
    parts = PATCH // inner
    each = own // (2 * channels)
    perm = np.zeros((parts, devices * own, 2 * channels * PATCH), ml_dtypes.bfloat16)
    for n in range(parts):
        for j in range(devices):
            for q in range(each):
                for rc in range(2 * channels):
                    perm[n, j * own + q * 2 * channels + rc, rc * PATCH + n * inner + j * each + q] = 1
    return pl.pallas_call(
        order_patches,
        out_shape=jax.ShapeDtypeStruct((row_block * LANES // parts, 2 * channels * PATCH), BF16),
        in_specs=[VMEM] * 2,
        out_specs=VMEM,
        scratch_shapes=[pltpu.VMEM((devices * own * row_block, LANES), F32)],
        compiler_params=PARAMS,
        name="order_patches",
    )(x, perm)


def dft_table(order):
    counter = jnp.arange(order, dtype=jnp.int32)
    turn_count = counter[:, None] * counter[None, :] % order
    radians = turn_count.astype(F32) * (2.0 * math.pi / order)
    return jnp.stack([jnp.cos(radians), jnp.sin(radians)])


def make_patches(first, length):
    devices = lax.axis_size(ALL)
    inner, pairs, row_block, _ = first.shape
    channels = pairs // 2
    if inner % devices == 0:
        own = inner // devices
        moved = lax.all_to_all(
            first.reshape(devices, own, pairs, row_block, LANES), ALL, 0, 0, tiled=True
        )
        moved = lax.all_to_all(run_second(moved, length), ALL, 0, 0, tiled=True)
        return run_order(moved, inner, channels)
    flat = first.transpose(1, 2, 0, 3).reshape(2, channels, row_block, inner * LANES)
    flat = lax.all_to_all(flat, ALL, split_axis=3, concat_axis=2, tiled=True).astype(F32)
    mixed = jnp.einsum(
        "rcuq,kum->krcqm", flat, dft_table(row_block * devices), precision=lax.Precision.HIGHEST
    )
    series = jnp.stack([mixed[0, 0] - mixed[1, 1], mixed[1, 0] + mixed[0, 1]])
    series = (series * (1.0 / math.sqrt(length))).astype(BF16)
    series = lax.all_to_all(series, ALL, split_axis=4 - 1, concat_axis=2, tiled=True)
    parts = PATCH // inner
    series = series.reshape(2, channels, inner, parts, LANES // parts, row_block)
    return series.transpose(5, 4, 0, 1, 3, 2).reshape(
        row_block * LANES // parts, 2 * channels * PATCH
    )


def norm_rows(values, total):
    return lax.rsqrt(jnp.sum(values * values, axis=-1, keepdims=True) * (1.0 / total) + EPSILON)


def silu(values):
    return values * (1.0 / (1.0 + jnp.exp(-values)))


def scan_tokens(
    heads, per, me_ref, *refs,
):
    count = len(refs) - 23
    pats = refs[:count]
    (halo, we, nin, wz, wx, wbc, wdt, dtb, alog, cx, cbc, spread, yg_ref, fac_ref, c_ref, st_ref,
     xs, bcs, carried, total, y_acc, low_tri, pad) = refs[count:]
    block = pl.program_id(0)
    inner = wx.shape[1]
    head_dim = inner // heads
    state = wbc.shape[1] // 2
    taps = cx.shape[0]

    def features(p):
        embedded = mm(p, we[...]).astype(BF16).astype(F32)
        scale = norm_rows(embedded, embedded.shape[-1])
        return (embedded * scale * nin[...].astype(F32)).astype(BF16)

    @pl.when(block == 0)
    def _():
        carried[...] = jnp.zeros_like(carried)
        total[...] = jnp.zeros_like(total)
        before = features(halo[...])
        xs[0:8] = mm(before, wx[...]).astype(BF16).astype(F32)
        bcs[0:8] = mm(before, wbc[...]).astype(BF16).astype(F32)
        ri = lax.broadcasted_iota(jnp.int32, (SPAN, SPAN), 0)
        ci = lax.broadcasted_iota(jnp.int32, (SPAN, SPAN), 1)
        low_tri[...] = jnp.where(ri >= ci, 1.0, 0.0)

    @pl.when(block > 0)
    def _():
        xs[0:8] = xs[SPAN : SPAN + 8]
        bcs[0:8] = bcs[SPAN : SPAN + 8]

    which = (block // per) ^ me_ref[0]
    patch = pats[0][...]
    for d in range(1, count):
        patch = jnp.where(which == d, pats[d][...], patch)
    normed = features(patch)
    xs[8 : SPAN + 8] = mm(normed, wx[...]).astype(BF16).astype(F32)
    bcs[8 : SPAN + 8] = mm(normed, wbc[...]).astype(BF16).astype(F32)
    gate = silu(mm(normed, wz[...]).astype(BF16).astype(F32))
    step = mm(normed, wdt[...]) + dtb[...]
    step = jnp.maximum(step, 0.0) + jnp.log1p(jnp.exp(-jnp.abs(step)))

    def conv(buffer, kernel):
        out = kernel[0:1] * buffer[9 - taps : 9 - taps + SPAN]
        for i in range(1, taps):
            out = out + kernel[i : i + 1] * buffer[9 - taps + i : 9 - taps + i + SPAN]
        return silu(out)

    xc = conv(xs, cx).astype(BF16)
    bc = conv(bcs, cbc)
    bt = bc[:, :state].T.astype(BF16)
    cm = bc[:, state:].astype(BF16)
    c_ref[...] = cm
    cum = jnp.dot(
        low_tri[...], step * (-jnp.exp(alog[...])), precision=lax.Precision.HIGHEST,
        preferred_element_type=F32,
    )
    last = cum[SPAN - 1 : SPAN]
    cum_t = cum.T
    step_t = step.T
    gram = mm(cm, bt)
    inside = low_tri[...] > 0.5

    def expand(values):
        high, low = split(values)
        return mm(jnp.concatenate([high, low], axis=1), spread[...])

    for h in range(heads):
        gap = cum[:, h : h + 1] - cum_t[h : h + 1, :]
        seg = jnp.exp(jnp.where(inside, gap, -jnp.inf))
        scores = (gram * seg * step_t[h : h + 1, :]).astype(BF16)
        cols = slice(h * head_dim, (h + 1) * head_dim)
        y_acc[:, cols] = mm(scores, xc[:, cols])
    grown = expand(jnp.exp(cum))
    weights = expand(jnp.exp(last - cum) * step)
    rows8 = expand(jnp.concatenate(
        [jnp.exp(jnp.broadcast_to(last, (8, LANES))), jnp.exp(total[...])], axis=0))
    c_twice = jnp.concatenate([cm, cm], axis=1)
    high, low = split(carried[...])
    off = mm(c_twice, jnp.concatenate([high, low], axis=0))
    y = y_acc[...] + off * grown
    yg_ref[...] = (y * gate).astype(BF16)
    fac_ref[...] = (grown * rows8[8:9] * gate).astype(BF16)
    weighted = (xc.astype(F32) * weights).astype(BF16)
    carried[...] = carried[...] * rows8[0:1] + mm(bt, weighted)
    total[...] = total[...] + last

    @pl.when(block == pl.num_programs(0) - 1)
    def _():
        st_ref[0:state] = carried[...].astype(BF16)
        st_ref[state : state + 8] = (rows8[8:16] * rows8[0:8]).astype(BF16)


def run_scan(pats, halo, me, we, nin, wz, wx, wbc, wdt, dtb, alog, cx, cbc):
    own, width = pats[0].shape
    heads = dtb.shape[0]
    inner = wx.shape[1]
    state = wbc.shape[1] // 2
    tokens = own * len(pats)
    per = own // SPAN
    spread = np.zeros((2 * LANES, inner), ml_dtypes.bfloat16)
    for h in range(heads):
        spread[h, h * (inner // heads) : (h + 1) * (inner // heads)] = 1
    spread[LANES:] = spread[:LANES]
    more = LANES - heads
    wdt = jnp.pad(wdt, ((0, 0), (0, more)))
    dtb = jnp.pad(dtb, (0, more))[None]
    alog = jnp.pad(alog, (0, more))[None]
    consts = [halo, we, nin[None], wz, wx, wbc, wdt, dtb, alog, cx, cbc, spread]
    rows = lambda n: pl.BlockSpec((SPAN, n), lambda b, me: (b, 0))
    return pl.pallas_call(
        functools.partial(scan_tokens, heads, per),
        grid_spec=pltpu.PrefetchScalarGridSpec(
            num_scalar_prefetch=1,
            grid=(tokens // SPAN,),
            in_specs=[pl.BlockSpec((SPAN, width), lambda b, me: (b % per, 0))] * len(pats)
            + [VMEM] * len(consts),
            out_specs=[rows(inner), rows(inner), rows(state),
                       pl.BlockSpec((state + 8, inner), lambda b, me: (0, 0))],
            scratch_shapes=[
                pltpu.VMEM((SPAN + 8, inner), F32),
                pltpu.VMEM((SPAN + 8, 2 * state), F32),
                pltpu.VMEM((state, inner), F32),
                pltpu.VMEM((8, LANES), F32),
                pltpu.VMEM((SPAN, inner), F32),
                pltpu.VMEM((SPAN, SPAN), F32),
                pltpu.VMEM((8, LANES), F32),
            ],
        ),
        out_shape=[
            jax.ShapeDtypeStruct((tokens, inner), BF16),
            jax.ShapeDtypeStruct((tokens, inner), BF16),
            jax.ShapeDtypeStruct((tokens, state), BF16),
            jax.ShapeDtypeStruct((state + 8, inner), BF16),
        ],
        compiler_params=PARAMS,
        name="scan_tokens",
    )(me, *pats, *consts)


def correct(steps, me_ref, yg_ref, fac_ref, c_ref, *refs):
    earlier = refs[: len(refs) - steps - 1]
    outs = refs[len(earlier) : -1]
    start = refs[-1]
    step = pl.program_id(0)
    state = c_ref.shape[1]

    @pl.when(step == 0)
    def _():
        entering = jnp.zeros((state, yg_ref.shape[1]), F32)
        for part in reversed(earlier):
            entering = part[0:state].astype(F32) + part[state : state + 1].astype(F32) * entering
        high, low = split(entering)
        start[0:state] = high
        start[state : 2 * state] = low

    cm = c_ref[...]
    added = mm(jnp.concatenate([cm, cm], axis=1), start[...])
    value = (yg_ref[...].astype(F32) + fac_ref[...].astype(F32) * added).astype(BF16)
    for n in range(steps):
        @pl.when(step == n)
        def _(n=n):
            outs[n][...] = value


def run_correct(which, me, yg, fac, cm, earlier, own):
    inner, state = yg.shape[1], cm.shape[1]
    steps = len(which)
    first, stride = which[0], (which[1] - which[0] if steps > 1 else 0)
    block = lambda d, me: (me[0] ^ (first + stride * d), 0)
    return pl.pallas_call(
        functools.partial(correct, steps),
        grid_spec=pltpu.PrefetchScalarGridSpec(
            num_scalar_prefetch=1,
            grid=(steps,),
            in_specs=[pl.BlockSpec((own, inner), block)] * 2 + [pl.BlockSpec((own, state), block)]
            + [VMEM] * len(earlier),
            out_specs=[pl.BlockSpec((own, inner), lambda d, me: (0, 0))] * steps,
            scratch_shapes=[pltpu.VMEM((2 * state, inner), BF16)],
        ),
        out_shape=[jax.ShapeDtypeStruct((own, inner), BF16)] * steps,
        compiler_params=PARAMS,
        name="correct",
    )(me, yg, fac, cm, *earlier)


def finish(count, me_ref, pat_ref, we_ref, *refs):
    parts, norms, weights, out_ref = refs[:count], refs[count : 2 * count], refs[2 * count : -1], refs[-1]
    values = [p[...].astype(F32) for p in parts]
    square = values[0] * values[0]
    for v in values[1:]:
        square = square + v * v
    inner = values[0].shape[1]
    scale = lax.rsqrt(
        jnp.sum(square, axis=-1, keepdims=True) * (1.0 / (count * inner)) + EPSILON
    )
    out = mm(pat_ref[...], we_ref[...]).astype(BF16).astype(F32)
    mixed = None
    for v, n, w in zip(values, norms, weights):
        part = mm((v * scale * n[0].astype(F32)).astype(BF16), w[0])
        mixed = part if mixed is None else mixed + part
    out_ref[...] = (out + mixed).astype(BF16)


def run_finish(me, patches, we, parts, norm_out, w_out):
    count = len(parts)
    own, inner = parts[0].shape
    width = w_out.shape[1]
    tile = min(own, SPAN)
    norms = norm_out.reshape(count, 1, inner)
    weights = w_out.reshape(count, inner, width)
    pick = lambda shape: [
        pl.BlockSpec((1,) + shape, lambda i, me, d=d: (me[0] ^ d, 0, 0)) for d in range(count)
    ]
    return pl.pallas_call(
        functools.partial(finish, count),
        grid_spec=pltpu.PrefetchScalarGridSpec(
            num_scalar_prefetch=1,
            grid=(own // tile,),
            in_specs=[pl.BlockSpec((tile, patches.shape[1]), lambda i, me: (i, 0)), VMEM]
            + [pl.BlockSpec((tile, inner), lambda i, me: (i, 0))] * count
            + pick((1, inner)) + pick((inner, width)),
            out_specs=pl.BlockSpec((tile, width), lambda i, me: (i, 0)),
        ),
        out_shape=jax.ShapeDtypeStruct((own, width), BF16),
        compiler_params=PARAMS,
        name="finish",
    )(me, patches, we, *parts, *([norms] * count), *([weights] * count))


def swap(value, flip):
    count = lax.axis_size(HR)
    return lax.ppermute(value, HR, [(i, i ^ flip) for i in range(count)])


def shift(value, by):
    count = lax.axis_size("seq")
    return lax.ppermute(value, "seq", [(i, i + by) for i in range(count - by)])


def on_device(
    spectrum, src_amp, src_phase, src_mode, src_delay, src_bins, w_embed, norm_in, w_z, w_x, w_bc, w_dt,
    dt_bias, a_log, conv_x, conv_bc, norm_out, w_out,
):
    devices = lax.axis_size(ALL)
    share = lax.axis_size(HR)
    rows_all = spectrum.shape[2] * devices
    length = rows_all * spectrum.shape[3]
    pos = lax.axis_index(ALL).astype(jnp.int32).reshape(1)
    me = lax.axis_index(HR).astype(jnp.int32).reshape(1)
    first = run_first(
        spectrum, src_amp, src_phase, src_mode, src_delay, src_bins, pos, rows_all, length
    )
    patches = make_patches(first, length)
    own = patches.shape[0]
    pats = [patches]
    for d in range(1, share):
        pats.append(swap(pats[2], 1) if d == 3 else swap(patches, d))
    tail = pats[0][own - 8 :]
    for d in range(1, share):
        tail = jnp.where(me[0] ^ d == share - 1, pats[d][own - 8 :], tail)
    halo = shift(tail, 1)
    yg, fac, cm, ends = run_scan(
        pats, halo, me, w_embed, norm_in, w_z, w_x, w_bc, w_dt, dt_bias, a_log, conv_x, conv_bc
    )
    earlier = [shift(ends, d) for d in range(1, lax.axis_size("seq"))]
    far = run_correct(list(range(share // 2, share)), me, yg, fac, cm, earlier, own)
    near = run_correct(list(range(share // 2)), me, yg, fac, cm, earlier, own)
    gated = list(near) + list(far)
    parts = [gated[0]] + [swap(gated[d], d) for d in range(1, share)]
    return run_finish(me, patches, w_embed, parts, norm_out, w_out)


def solution(mesh):
    in_specs = (
        P("grp", None, ("seq", "head", "rep"), None),
        P("grp", None),
        P("grp"),
        P("grp"),
        P("grp"),
        P("grp", None),
        P(),
        P(),
        P(None, ("head", "rep")),
        P(None, ("head", "rep")),
        P(),
        P(None, ("head", "rep")),
        P(("head", "rep")),
        P(("head", "rep")),
        P(None, ("head", "rep")),
        P(),
        P(),
        P(),
    )
    out_specs = P(("grp", "seq", "head", "rep"), None)
    return jax.shard_map(
        on_device, mesh=mesh, in_specs=in_specs, out_specs=out_specs, check_vma=False
    )
```

```python
import functools
import math

import jax
import jax.numpy as jnp
import ml_dtypes
import numpy as np
from jax import lax
from jax.experimental import pallas as pl
from jax.experimental.pallas import tpu as pltpu
from jax.sharding import PartitionSpec as P

SPAN = 256
EPSILON = 1e-05
LANES = 128
PATCH = 64
ALL = ("seq", "head", "rep")
HR = ("head", "rep")
F32 = jnp.float32
BF16 = jnp.bfloat16
VMEM = pl.BlockSpec(memory_space=pltpu.VMEM)
SMEM = pl.BlockSpec(memory_space=pltpu.SMEM)


def cost(micros):
    return pl.CostEstimate(
        flops=int(micros * 1e9), transcendentals=0, bytes_accessed=int(micros * 3e6)
    )


PARAMS = pltpu.CompilerParams(vmem_limit_bytes=56 * 1024 * 1024)


def two_halves(table):
    high = table.astype(ml_dtypes.bfloat16)
    return high, (table - high.astype(np.float64)).astype(ml_dtypes.bfloat16)


def mm(a, b):
    return jnp.dot(a, b, preferred_element_type=F32)


def split(a):
    high = a.astype(BF16)
    return high, (a - high.astype(F32)).astype(BF16)


def lane_bins(inner):
    parts = PATCH // inner
    lane = np.arange(LANES)
    width = LANES // parts
    return lane // width + parts * (lane % width)


def inverse_fft(real, imag):
    count = len(real)
    if count == 1:
        return real, imag
    even_r, even_i = inverse_fft(real[0::2], imag[0::2])
    odd_r, odd_i = inverse_fft(real[1::2], imag[1::2])
    half = count // 2
    out_r, out_i = [None] * count, [None] * count
    for k in range(half):
        angle = 2.0 * math.pi * k / count
        c, s = math.cos(angle), math.sin(angle)
        if k == 0:
            r, i = odd_r[k], odd_i[k]
        elif 4 * k == count:
            r, i = -odd_i[k], odd_r[k]
        else:
            r = odd_r[k] * c - odd_i[k] * s
            i = odd_r[k] * s + odd_i[k] * c
        out_r[k], out_i[k] = even_r[k] + r, even_i[k] + i
        out_r[k + half], out_i[k + half] = even_r[k] - r, even_i[k] - i
    return out_r, out_i


def first_section(
    rows_all, length, pos, amp, phase, mode, delay, bins, turn_ref, x_ref, twist_ref, high_ref, low_ref,
    out_ref, base, acc, lhs,
):
    channels = x_ref.shape[1]
    sources = phase.shape[0]
    inner = x_ref.shape[2]
    row_block = x_ref.shape[3]
    shape = (row_block, LANES)
    row = pos[0] * row_block + lax.broadcasted_iota(jnp.int32, shape, 0)
    lane = lax.broadcasted_iota(jnp.int32, shape, 1)
    first_bin = row + rows_all * lane
    unit = 2.0 * math.pi / length

    def make_base(s, _):
        turn = ((((first_bin * delay[s]) & (length - 1)) * mode[s]) & (length - 1)).astype(F32)
        angle = mode[s].astype(F32) * phase[s] + turn * unit
        base[0, s] = jnp.cos(angle)
        base[1, s] = jnp.sin(angle)
        return 0

    lax.fori_loop(0, sources, make_base, 0)

    def add_sources(v, _):
        here = first_bin + (rows_all * LANES) * v
        total = [x_ref[r, c, v] for r in range(2) for c in range(channels)]
        for s in range(sources):
            which = (delay[s] * mode[s] * v) & (inner - 1)
            tr, ti = turn_ref[0, which], turn_ref[1, which]
            inside = (here >= bins[0, s]) & (here < bins[1, s])
            br, bi = base[0, s], base[1, s]
            real = jnp.where(inside, br * tr - bi * ti, 0.0)
            imag = jnp.where(inside, br * ti + bi * tr, 0.0)
            for c in range(channels):
                total[c] = total[c] + amp[c, s] * real
                total[channels + c] = total[channels + c] + amp[c, s] * imag
        for n in range(2 * channels):
            acc[n, v] = total[n]
        return 0

    lax.fori_loop(0, inner, add_sources, 0)

    def transform(c, _):
        real, imag = inverse_fft(
            [acc[c, v] for v in range(inner)], [acc[channels + c, v] for v in range(inner)]
        )
        for q in range(inner):
            tc, ts = twist_ref[0, q : q + 1, :], twist_ref[1, q : q + 1, :]
            lhs[c, q, :, 0:LANES] = real[q] * tc - imag[q] * ts
            lhs[c, q, :, LANES : 2 * LANES] = real[q] * ts + imag[q] * tc
        return 0

    lax.fori_loop(0, channels, transform, 0)

    wide = (inner, row_block, LANES)
    parts = PATCH // inner
    width = LANES // parts
    lanes = lax.broadcasted_iota(jnp.int32, wide, 2)
    outer = lax.div(lanes, width) + parts * lax.rem(lanes, width)
    column = lax.broadcasted_iota(jnp.int32, wide, 0) + inner * outer
    rows = pos[0] * row_block + lax.broadcasted_iota(jnp.int32, wide, 1)
    angle = ((rows * column) & (length - 1)).astype(F32) * unit
    cos, sin = jnp.cos(angle), jnp.sin(angle)
    for c in range(channels):
        high, low = split(lhs[c].reshape(inner * row_block, 2 * LANES))
        got = mm(high, high_ref[...]) + mm(low, high_ref[...]) + mm(high, low_ref[...])
        real = got[:, 0:LANES].reshape(wide)
        imag = got[:, LANES : 2 * LANES].reshape(wide)
        out_ref[:, c] = (real * cos - imag * sin).astype(BF16)
        out_ref[:, channels + c] = (real * sin + imag * cos).astype(BF16)


def run_first(spectrum, amp, phase, mode, delay, bins, pos, rows_all, length):
    _, channels, row_block, columns = spectrum.shape
    inner = columns // LANES
    grid_in = spectrum.reshape(2, channels, row_block, inner, LANES).transpose(0, 1, 3, 2, 4)
    steps = np.arange(inner)
    turn = 2.0 * np.pi * steps / inner
    turns = np.stack([np.cos(turn), np.sin(turn)]).astype(np.float32)
    lane = np.arange(LANES)
    twist = 2.0 * np.pi * (steps[:, None] * lane[None, :] % columns) / columns
    twists = np.stack([np.cos(twist), np.sin(twist)]).astype(np.float32)
    angle = 2.0 * np.pi * (lane[:, None] * lane_bins(inner)[None, :] % LANES) / LANES
    cos, sin = np.cos(angle), np.sin(angle)
    high, low = two_halves(np.block([[cos, sin], [-sin, cos]]))
    return pl.pallas_call(
        functools.partial(first_section, rows_all, length),
        out_shape=jax.ShapeDtypeStruct((inner, 2 * channels, row_block, LANES), BF16),
        in_specs=[SMEM] * 7 + [VMEM] * 4,
        out_specs=VMEM,
        scratch_shapes=[
            pltpu.VMEM((2, amp.shape[0], row_block, LANES), F32),
            pltpu.VMEM((2 * channels, inner, row_block, LANES), F32),
            pltpu.VMEM((channels, inner, row_block, 2 * LANES), F32),
        ],
        compiler_params=PARAMS,
        cost_estimate=cost(7),
        name="first_section",
    )(pos, amp.T, phase, mode, delay, bins.T, turns, grid_in, twists, high, low)


def second_section(reps, z_ref, high_ref, low_ref, out_ref):
    devices, own, pairs, row_block, _ = z_ref.shape
    channels = pairs // 2
    rows = devices * row_block
    tiles = own * pairs
    half = (tiles + 1) // 2
    lane = lax.broadcasted_iota(jnp.int32, (rows, LANES), 1)
    sub = lax.rem(lax.broadcasted_iota(jnp.int32, (rows, LANES), 0), row_block)
    upper = (lane & 32) != 0
    rim = jnp.zeros((rows, LANES), F32)
    for q in range(own):
        for c in range(channels):
            right = jnp.concatenate(
                [z_ref[:, q, r * channels + c].astype(F32).reshape(rows, LANES) for r in range(2)], axis=0
            ).astype(BF16)
            got = mm(high_ref[...], right) + mm(low_ref[...], right)
            for r in range(2):
                tile = q * pairs + r * channels + c
                part = got[r * rows : (r + 1) * rows]
                out_ref[:, tile] = part.reshape(devices, row_block, LANES).astype(BF16)
                ends = jnp.broadcast_to(
                    part.reshape(devices, row_block, LANES)[:, row_block - 1 :, :],
                    (devices, row_block, LANES),
                ).reshape(rows, LANES)
                if tile < half:
                    rim = jnp.where(upper & (sub == tile), ends, rim)
                else:
                    ends = pltpu.roll(ends, LANES - 32, 1)
                    rim = jnp.where(jnp.logical_not(upper) & (sub == tile - half), ends, rim)
    rim = rim.reshape(devices, row_block, LANES).astype(BF16)
    for d in range(devices):
        source = d - d % reps - 1
        out_ref[d, tiles] = rim[source] if source >= 0 else jnp.zeros((row_block, LANES), BF16)


def run_second(z, length):
    devices, own, pairs, row_block, _ = z.shape
    rows = devices * row_block
    counter = np.arange(rows)
    angle = 2.0 * np.pi * (counter[:, None] * counter[None, :] % rows) / rows
    cos, sin = np.cos(angle), np.sin(angle)
    high, low = two_halves(np.block([[cos, -sin], [sin, cos]]) / math.sqrt(length))
    return pl.pallas_call(
        functools.partial(second_section, lax.axis_size("rep")),
        out_shape=jax.ShapeDtypeStruct((devices, own * pairs + 1, row_block, LANES), BF16),
        in_specs=[VMEM] * 3,
        out_specs=VMEM,
        compiler_params=PARAMS,
        cost_estimate=cost(3),
        name="second_section",
    )(z, high, low)


def order_patches(x_ref, perm_ref, rim_ref, out_ref, wide):
    devices, tiles, row_block, _ = x_ref.shape
    parts = perm_ref.shape[0]
    width = LANES // parts
    half = tiles // 2
    wide[...] = x_ref[...].astype(F32).reshape(devices * tiles * row_block, LANES)
    for m in range(row_block):
        rows = wide[pl.ds(m, devices * tiles, stride=row_block), :]
        across = rows.T.astype(BF16)
        total = mm(across[0:width], perm_ref[0])
        for n in range(1, parts):
            total = total + mm(across[n * width : (n + 1) * width], perm_ref[n])
        out_ref[m * width : (m + 1) * width, :] = total.astype(BF16)
    rows = jnp.concatenate(
        [wide[pl.ds((tiles - 1) * row_block + n, devices, stride=tiles * row_block), :] for n in range(half)],
        axis=0,
    )
    across = jnp.concatenate([rows, pltpu.roll(rows, 32, 1)], axis=0).T.astype(BF16)
    total = mm(across[width - 8 : width], rim_ref[0])
    for n in range(1, parts):
        total = total + mm(across[(n + 1) * width - 8 : (n + 1) * width], rim_ref[n])
    out_ref[row_block * width :, :] = total.astype(BF16)


def run_order(x, inner, channels):
    devices, tiles, row_block, _ = x.shape
    parts = PATCH // inner
    own = tiles - 1
    pairs = 2 * channels
    each = own // pairs
    perm = np.zeros((parts, devices * tiles, pairs * PATCH), ml_dtypes.bfloat16)
    rim = np.zeros((parts, own * devices, pairs * PATCH), ml_dtypes.bfloat16)
    for n in range(parts):
        for j in range(devices):
            for q in range(each):
                for rc in range(pairs):
                    to = rc * PATCH + n * inner + j * each + q
                    perm[n, j * tiles + q * pairs + rc, to] = 1
                    rim[n, (q * pairs + rc) * devices + j, to] = 1
    return pl.pallas_call(
        order_patches,
        out_shape=jax.ShapeDtypeStruct((row_block * LANES // parts + 8, pairs * PATCH), BF16),
        in_specs=[VMEM] * 3,
        out_specs=VMEM,
        scratch_shapes=[pltpu.VMEM((devices * tiles * row_block, LANES), F32)],
        compiler_params=PARAMS,
        cost_estimate=cost(3),
        name="order_patches",
    )(x, perm, rim)


def dft_table(order):
    counter = jnp.arange(order, dtype=jnp.int32)
    turn_count = counter[:, None] * counter[None, :] % order
    radians = turn_count.astype(F32) * (2.0 * math.pi / order)
    return jnp.stack([jnp.cos(radians), jnp.sin(radians)])


def make_patches(first, length):
    devices = lax.axis_size(ALL)
    inner, pairs, row_block, _ = first.shape
    channels = pairs // 2
    if inner % devices == 0 and 2 * inner == PATCH and inner // devices * pairs in range(2, 17, 2):
        own = inner // devices
        moved = lax.all_to_all(
            first.reshape(devices, own, pairs, row_block, LANES), ALL, 0, 0, tiled=True
        )
        moved = lax.all_to_all(run_second(moved, length), ALL, 0, 0, tiled=True)
        return run_order(moved, inner, channels)
    flat = first.transpose(1, 2, 0, 3).reshape(2, channels, row_block, inner * LANES)
    flat = lax.all_to_all(flat, ALL, split_axis=3, concat_axis=2, tiled=True).astype(F32)
    mixed = jnp.einsum(
        "rcuq,kum->krcqm", flat, dft_table(row_block * devices), precision=lax.Precision.HIGHEST
    )
    series = jnp.stack([mixed[0, 0] - mixed[1, 1], mixed[1, 0] + mixed[0, 1]])
    series = (series * (1.0 / math.sqrt(length))).astype(BF16)
    series = lax.all_to_all(series, ALL, split_axis=4 - 1, concat_axis=2, tiled=True)
    parts = PATCH // inner
    series = series.reshape(2, channels, inner, parts, LANES // parts, row_block)
    patches = series.transpose(5, 4, 0, 1, 3, 2).reshape(
        row_block * LANES // parts, 2 * channels * PATCH
    )
    reps = lax.axis_size("rep")
    tail = patches[patches.shape[0] - 8 :]
    rim = jnp.zeros_like(tail)
    for r in range(reps):
        pairs = [(i - 1, i + r) for i in range(reps, devices, reps)]
        rim = rim + lax.ppermute(tail, ALL, pairs)
    return jnp.concatenate([patches, rim], 0)


def norm_rows(values, total):
    return lax.rsqrt(jnp.sum(values * values, axis=-1, keepdims=True) * (1.0 / total) + EPSILON)


def silu(values):
    return values * (1.0 / (1.0 + jnp.exp(-values)))


def fold(ends, count, head, entering, upto=None):
    state = entering.shape[0]
    for i in range(count):
        part, decay = ends[0][0:state], ends[0][state : state + 1]
        for j in range(1, len(ends)):
            here = (head ^ i) == j
            part = jnp.where(here, ends[j][0:state], part)
            decay = jnp.where(here, ends[j][state : state + 1], decay)
        after = decay * entering + part
        entering = after if upto is None else jnp.where(i < upto, after, entering)
    return entering


def expand(values, spread):
    high, low = split(values)
    return mm(jnp.concatenate([high, low], axis=1), spread[...])


def block_states(heads, per, before, final, me_ref, *refs):
    pats, refs = refs[:2], refs[2:]
    halo, we, nin, wx, wbc, wdt, dtb, alog, cx, cbc, spread = refs[:11]
    earlier, refs = refs[11 : 11 + before], refs[11 + before :]
    normed_ref, x_ref, b_ref, c_ref, cum_ref, step_ref, local_ref, grown_ref, st_ref = refs[:9]
    xs, bcs, carried, total, low_tri, dts, rows = refs[-7:]
    block = pl.program_id(0)
    state = wbc.shape[1] // 2
    taps = cx.shape[0]

    def features(p):
        embedded = mm(p, we[...]).astype(BF16).astype(F32)
        scale = norm_rows(embedded, embedded.shape[-1])
        return (embedded * scale * nin[...].astype(F32)).astype(BF16)

    @pl.when(block == 0)
    def _():
        carried[...] = jnp.zeros_like(carried)
        total[...] = jnp.zeros_like(total)
        past = features(halo[...])
        xs[0:8] = mm(past, wx[...]).astype(BF16).astype(F32)
        bcs[0:8] = mm(past, wbc[...]).astype(BF16).astype(F32)
        ri = lax.broadcasted_iota(jnp.int32, (SPAN, SPAN), 0)
        ci = lax.broadcasted_iota(jnp.int32, (SPAN, SPAN), 1)
        low_tri[...] = jnp.where(ri >= ci, 1.0, 0.0).astype(BF16)
        dts[...] = jnp.zeros_like(dts)
        rows[...] = jnp.zeros_like(rows)
        rows[0:1, 0:heads] = dtb[...]
        rows[1:2, 0:heads] = -jnp.exp(alog[...])

    @pl.when(block > 0)
    def _():
        xs[0:8] = xs[SPAN : SPAN + 8]
        bcs[0:8] = bcs[SPAN : SPAN + 8]

    here = ((block // per) ^ me_ref[1]) == 0
    normed = features(jnp.where(here, pats[0][...], pats[1][...]))
    normed_ref[...] = normed
    dts[:, 0:heads] = lax.dot_general(
        normed, wdt[...], (((1,), (1,)), ((), ())), preferred_element_type=F32
    )
    bcs[8 : SPAN + 8] = mm(normed, wbc[...]).astype(BF16).astype(F32)
    xs[8 : SPAN + 8] = mm(normed, wx[...]).astype(BF16).astype(F32)
    step = dts[...] + rows[0:1]
    step = jnp.maximum(step, 0.0) + jnp.log1p(jnp.exp(-jnp.abs(step)))
    step_ref[...] = step
    rated = step * rows[1:2]
    one = rated.astype(BF16).astype(F32)
    two = (rated - one).astype(BF16).astype(F32)
    three = rated - one - two
    packed = one + pltpu.roll(two, heads, 1) + pltpu.roll(three, 2 * heads, 1)
    sums = mm(low_tri[...], packed.astype(BF16))
    cum = sums + pltpu.roll(sums, LANES - heads, 1) + pltpu.roll(sums, LANES - 2 * heads, 1)
    cum_ref[...] = cum
    last = cum[SPAN - 1 : SPAN]
    weights = expand(jnp.exp(last - cum) * step, spread)
    grow = expand(
        jnp.exp(jnp.concatenate([jnp.broadcast_to(last, (8, LANES)), total[...]], axis=0)), spread
    )

    def conv(buffer, kernel):
        out = kernel[0:1] * buffer[9 - taps : 9 - taps + SPAN]
        for i in range(1, taps):
            out = out + kernel[i : i + 1] * buffer[9 - taps + i : 9 - taps + i + SPAN]
        return silu(out)

    bc = conv(bcs, cbc)
    b_ref[...] = bc[:, :state].astype(BF16)
    c_ref[...] = bc[:, state:].astype(BF16)
    bt = bc[:, :state].T.astype(BF16)
    xc = conv(xs, cx).astype(BF16)
    x_ref[...] = xc
    weighted = (xc.astype(F32) * weights).astype(BF16)
    local_ref[0] = carried[...]
    grown_ref[0] = grow[8:16]
    carried[...] = carried[...] * grow[0:1] + mm(bt, weighted)
    total[...] = total[...] + last

    @pl.when(block == pl.num_programs(0) - 1)
    def _():
        st_ref[0:state] = carried[...]
        st_ref[state : state + 8] = grow[8:16] * grow[0:8]
        if final:
            everything = [e[...] for e in earlier] + [st_ref[...]]
            count = len(everything)
            send = refs[9]
            send[0:state] = fold(everything, count, me_ref[0], jnp.zeros((state, xc.shape[1]), F32)).astype(BF16)
            decay = everything[0][state : state + 8]
            for e in everything[1:]:
                decay = decay * e[state : state + 8]
            send[state : state + 8] = decay.astype(BF16)


def run_states(me, pats, halo, consts, heads, inner, state, own, earlier, final):
    rows_in, width = pats[0].shape
    model = consts[0].shape[1]
    tokens = own * len(pats)
    per = own // SPAN
    blocks = tokens // SPAN
    row = lambda n: pl.BlockSpec((SPAN, n), lambda b, me: (b, 0))
    fixed = pl.BlockSpec((state + 8, inner), lambda b, me: (0, 0))
    shape = lambda *d, t=F32: jax.ShapeDtypeStruct(d, t)
    return pl.pallas_call(
        functools.partial(block_states, heads, per, len(earlier), final),
        grid_spec=pltpu.PrefetchScalarGridSpec(
            num_scalar_prefetch=1,
            grid=(blocks,),
            in_specs=[pl.BlockSpec((SPAN, width), lambda b, me: (b % per, 0))] * len(pats)
            + [pl.BlockSpec((8, width), lambda b, me: (own // 8, 0))]
            + [VMEM] * (len(consts) + len(earlier)),
            out_specs=[row(model), row(inner), row(state), row(state), row(LANES), row(LANES),
                       pl.BlockSpec((1, state, inner), lambda b, me: (b, 0, 0)),
                       pl.BlockSpec((1, 8, inner), lambda b, me: (b, 0, 0)), fixed]
            + [fixed] * final,
            scratch_shapes=[
                pltpu.VMEM((SPAN + 8, inner), F32),
                pltpu.VMEM((SPAN + 8, 2 * state), F32),
                pltpu.VMEM((state, inner), F32),
                pltpu.VMEM((8, LANES), F32),
                pltpu.VMEM((SPAN, SPAN), BF16),
                pltpu.VMEM((SPAN, LANES), F32),
                pltpu.VMEM((8, LANES), F32),
            ],
        ),
        out_shape=[
            shape(tokens, model, t=BF16), shape(tokens, inner, t=BF16), shape(tokens, state, t=BF16),
            shape(tokens, state, t=BF16), shape(tokens, LANES), shape(tokens, LANES),
            shape(blocks, state, inner), shape(blocks, 8, inner), shape(state + 8, inner),
        ] + [shape(state + 8, inner, t=BF16)] * final,
        compiler_params=PARAMS,
        cost_estimate=cost(13),
        name="block_states",
    )(me, *pats, halo, *consts, *earlier)


def local_part(heads, normed_ref, x_ref, b_ref, c_ref, cum_ref, step_ref, wz, spread, yg_ref, fac_ref, y_acc):
    gate = silu(mm(normed_ref[...], wz[...]).astype(BF16).astype(F32))
    cum = cum_ref[...]
    cum_t = cum.T
    step_t = step_ref[...].T
    gram = lax.dot_general(
        c_ref[...], b_ref[...], (((1,), (1,)), ((), ())), preferred_element_type=F32
    )
    ri = lax.broadcasted_iota(jnp.int32, (SPAN, SPAN), 0)
    ci = lax.broadcasted_iota(jnp.int32, (SPAN, SPAN), 1)
    inside = ri >= ci
    head_dim = x_ref.shape[1] // heads
    for h in range(heads):
        gap = cum[:, h : h + 1] - cum_t[h : h + 1, :]
        seg = jnp.exp(jnp.where(inside, gap, -jnp.inf))
        scores = (gram * seg * step_t[h : h + 1, :]).astype(BF16)
        cols = slice(h * head_dim, (h + 1) * head_dim)
        y_acc[:, cols] = mm(scores, x_ref[:, cols])
    fac_ref[...] = (expand(jnp.exp(cum), spread) * gate).astype(BF16)
    yg_ref[...] = (y_acc[...] * gate).astype(BF16)


def run_local(micros, heads, normed, xc, bm, cm, cum, step, wz, spread):
    tokens, inner = xc.shape
    row = lambda n: pl.BlockSpec((SPAN, n), lambda b: (b, 0))
    return pl.pallas_call(
        functools.partial(local_part, heads),
        grid=(tokens // SPAN,),
        in_specs=[row(a.shape[1]) for a in (normed, xc, bm, cm, cum, step)] + [VMEM] * 2,
        out_specs=[row(inner)] * 2,
        scratch_shapes=[pltpu.VMEM((SPAN, inner), F32)],
        out_shape=[jax.ShapeDtypeStruct((tokens, inner), BF16)] * 2,
        compiler_params=PARAMS,
        cost_estimate=cost(micros),
        name="local_part",
    )(normed, xc, bm, cm, cum, step, wz, spread)


def correct(chip, chips, reps, me_ref, yg_ref, fac_ref, c_ref, local_ref, grown_ref, *refs):
    ends, earlier = refs[:chips], refs[chips : -reps - 1]
    outs, start = refs[-reps - 1 : -1], refs[-1]
    state = c_ref.shape[1]
    block = pl.program_id(0)
    per = pl.num_programs(0) // reps

    @pl.when(block == 0)
    def _():
        entering = jnp.zeros((state, yg_ref.shape[1]), F32)
        for part in reversed(earlier):
            entering = part[0:state].astype(F32) + part[state : state + 1].astype(F32) * entering
        start[...] = fold([e[...] for e in ends], chips - 1, me_ref[0], entering, me_ref[0] ^ chip)

    cm = c_ref[...]
    high, low = split(local_ref[0] + grown_ref[0, 0:1] * start[...])
    added = mm(jnp.concatenate([cm, cm], axis=1), jnp.concatenate([high, low], axis=0))
    value = (yg_ref[...].astype(F32) + fac_ref[...].astype(F32) * added).astype(BF16)
    for r in range(reps):
        @pl.when((block // per) == (me_ref[1] ^ r))
        def _(r=r):
            outs[r][pl.ds(pl.multiple_of((block % per) * SPAN, SPAN), SPAN), :] = value


def run_correct(chip, reps, me, yg, fac, cm, local, grown, ends, earlier, own):
    tokens, inner = yg.shape
    state = cm.shape[1]
    block = lambda b, me: (b, 0)
    block3 = lambda b, me: (b, 0, 0)
    return pl.pallas_call(
        functools.partial(correct, chip, len(ends), reps),
        grid_spec=pltpu.PrefetchScalarGridSpec(
            num_scalar_prefetch=1,
            grid=(tokens // SPAN,),
            in_specs=[pl.BlockSpec((SPAN, inner), block)] * 2 + [pl.BlockSpec((SPAN, state), block),
                      pl.BlockSpec((1, state, inner), block3), pl.BlockSpec((1, 8, inner), block3)]
            + [VMEM] * (len(earlier) + len(ends)),
            out_specs=[pl.BlockSpec((own, inner), lambda b, me: (0, 0))] * reps,
            scratch_shapes=[pltpu.VMEM((state, inner), F32)],
        ),
        out_shape=[jax.ShapeDtypeStruct((own, inner), BF16)] * reps,
        compiler_params=PARAMS,
        cost_estimate=cost(5 if chip else 0.05),
        name="correct",
    )(me, yg, fac, cm, local, grown, *ends, *earlier)


def finish(count, me_ref, pat_ref, we_ref, *refs):
    parts, norms, weights, out_ref = refs[:count], refs[count : 2 * count], refs[2 * count : -1], refs[-1]
    values = [p[...].astype(F32) for p in parts]
    square = values[0] * values[0]
    for v in values[1:]:
        square = square + v * v
    inner = values[0].shape[1]
    scale = lax.rsqrt(
        jnp.sum(square, axis=-1, keepdims=True) * (1.0 / (count * inner)) + EPSILON
    )
    out = mm(pat_ref[...], we_ref[...]).astype(BF16).astype(F32)
    mixed = None
    for v, n, w in zip(values, norms, weights):
        part = mm((v * scale * n[...].astype(F32)).astype(BF16), w[0])
        mixed = part if mixed is None else mixed + part
    out_ref[...] = (out + mixed).astype(BF16)


def run_finish(me, patches, we, parts, norm_out, w_out):
    count = len(parts)
    own, inner = parts[0].shape
    width = w_out.shape[1]
    tile = min(own, SPAN)
    norms = norm_out[None]
    weights = w_out.reshape(count, inner, width)
    picks = [
        pl.BlockSpec((1, inner), lambda i, me, d=d: (0, me[0] ^ d)) for d in range(count)
    ] + [
        pl.BlockSpec((1, inner, width), lambda i, me, d=d: (me[0] ^ d, 0, 0)) for d in range(count)
    ]
    return pl.pallas_call(
        functools.partial(finish, count),
        grid_spec=pltpu.PrefetchScalarGridSpec(
            num_scalar_prefetch=1,
            grid=(own // tile,),
            in_specs=[pl.BlockSpec((tile, patches.shape[1]), lambda i, me: (i, 0)), VMEM]
            + [pl.BlockSpec((tile, inner), lambda i, me: (i, 0))] * count
            + picks,
            out_specs=pl.BlockSpec((tile, width), lambda i, me: (i, 0)),
        ),
        out_shape=jax.ShapeDtypeStruct((own, width), BF16),
        compiler_params=PARAMS,
        cost_estimate=cost(7),
        name="finish",
    )(me, patches, we, *parts, *([norms] * count), *([weights] * count))


def swap(value, flip):
    count = lax.axis_size(HR)
    return lax.ppermute(value, HR, [(i, i ^ flip) for i in range(count)])


def shift(value, by):
    count = lax.axis_size("seq")
    return lax.ppermute(value, "seq", [(i, i + by) for i in range(count - by)])


def on_device(
    spectrum, src_amp, src_phase, src_mode, src_delay, src_bins, w_embed, norm_in, w_z, w_x, w_bc, w_dt,
    dt_bias, a_log, conv_x, conv_bc, norm_out, w_out,
):
    devices = lax.axis_size(ALL)
    share = lax.axis_size(HR)
    rows_all = spectrum.shape[2] * devices
    length = rows_all * spectrum.shape[3]
    pos = lax.axis_index(ALL).astype(jnp.int32).reshape(1)
    me = lax.axis_index(HR).astype(jnp.int32).reshape(1)
    first = run_first(
        spectrum, src_amp, src_phase, src_mode, src_delay, src_bins, pos, rows_all, length
    )
    patches = make_patches(first, length)
    own = patches.shape[0] - 8
    reps, chips = lax.axis_size("rep"), lax.axis_size("head")
    place = jnp.stack([lax.axis_index("head"), lax.axis_index("rep")]).astype(jnp.int32)
    heads, inner, state = dt_bias.shape[0], w_x.shape[1], w_bc.shape[1] // 2
    spread = np.zeros((2 * LANES, inner), ml_dtypes.bfloat16)
    for h in range(heads):
        spread[h, h * (inner // heads) : (h + 1) * (inner // heads)] = 1
    spread[LANES:] = spread[:LANES]
    consts = (
        w_embed, norm_in[None], w_x, w_bc, w_dt.T, dt_bias[None], a_log[None], conv_x, conv_bc,
        jnp.asarray(spread),
    )
    done, ends = [], []
    base = [patches] + [swap(patches, c * reps) for c in range(1, chips)]
    for c in range(chips):
        start = base[c]
        if ends:
            start, ends[-1] = lax.optimization_barrier((start, ends[-1]))
        group = [start] + [swap(start, r) for r in range(1, reps)]
        got = run_states(
            place, group, start, consts, heads, inner, state, own, ends, c == chips - 1
        )
        done.append(got[:8])
        ends.append(got[8])
    send = got[9]
    earlier = [shift(send, d) for d in range(1, lax.axis_size("seq"))]
    parts = [None] * share
    gate = None
    for c in list(range(1, chips)) + [0]:
        normed, xc, bm, cm, cum, step, local, grown = done[c]
        if gate is not None:
            normed, gate = lax.optimization_barrier((normed, gate))
        yg, fac = run_local(7 if c else 0.05, heads, normed, xc, bm, cm, cum, step, w_z, spread)
        values = run_correct(c, reps, place, yg, fac, cm, local, grown, ends, earlier, own)
        gate = values[0]
        for r in reversed(range(reps)):
            d = c * reps + r
            parts[d] = swap(values[r], d) if d else values[r]
    return run_finish(me, patches, w_embed, parts, norm_out, w_out)


def solution(mesh):
    in_specs = (
        P("grp", None, ("seq", "head", "rep"), None),
        P("grp", None),
        P("grp"),
        P("grp"),
        P("grp"),
        P("grp", None),
        P(),
        P(),
        P(None, ("head", "rep")),
        P(None, ("head", "rep")),
        P(),
        P(None, ("head", "rep")),
        P(("head", "rep")),
        P(("head", "rep")),
        P(None, ("head", "rep")),
        P(),
        P(),
        P(),
    )
    out_specs = P(("grp", "seq", "head", "rep"), None)
    return jax.shard_map(
        on_device, mesh=mesh, in_specs=in_specs, out_specs=out_specs, check_vma=False
    )
```

```python
import functools
import math

import jax
import jax.numpy as jnp
import ml_dtypes
import numpy as np
from jax import lax
from jax.experimental import pallas as pl
from jax.experimental.pallas import tpu as pltpu
from jax.sharding import PartitionSpec as P

SPAN = 256
LOG2E = math.log2(math.e)
TILE = 512
EPSILON = 1e-05
LANES = 128
PATCH = 64
ALL = ("seq", "head", "rep")
HR = ("head", "rep")
F32 = jnp.float32
BF16 = jnp.bfloat16
VMEM = pl.BlockSpec(memory_space=pltpu.VMEM)
SMEM = pl.BlockSpec(memory_space=pltpu.SMEM)


def cost(micros):
    return pl.CostEstimate(
        flops=int(micros * 1e9), transcendentals=0, bytes_accessed=int(micros * 3e6)
    )


PARAMS = pltpu.CompilerParams(vmem_limit_bytes=56 * 1024 * 1024)


def two_halves(table):
    high = table.astype(ml_dtypes.bfloat16)
    return high, (table - high.astype(np.float64)).astype(ml_dtypes.bfloat16)


def mm(a, b):
    return jnp.dot(a, b, preferred_element_type=F32)


def split(a):
    high = a.astype(BF16)
    return high, (a - high.astype(F32)).astype(BF16)


def lane_bins(inner):
    parts = PATCH // inner
    lane = np.arange(LANES)
    width = LANES // parts
    return lane // width + parts * (lane % width)


def inverse_fft(real, imag):
    count = len(real)
    if count == 1:
        return real, imag
    even_r, even_i = inverse_fft(real[0::2], imag[0::2])
    odd_r, odd_i = inverse_fft(real[1::2], imag[1::2])
    half = count // 2
    out_r, out_i = [None] * count, [None] * count
    for k in range(half):
        angle = 2.0 * math.pi * k / count
        c, s = math.cos(angle), math.sin(angle)
        if k == 0:
            r, i = odd_r[k], odd_i[k]
        elif 4 * k == count:
            r, i = -odd_i[k], odd_r[k]
        else:
            r = odd_r[k] * c - odd_i[k] * s
            i = odd_r[k] * s + odd_i[k] * c
        out_r[k], out_i[k] = even_r[k] + r, even_i[k] + i
        out_r[k + half], out_i[k + half] = even_r[k] - r, even_i[k] - i
    return out_r, out_i


def first_section(
    rows_all, length, pos, amp, phase, mode, delay, bins, turn_ref, x_ref, twist_ref, near_ref, high_ref, low_ref,
    out_ref, base, acc, lhs,
):
    channels = x_ref.shape[1]
    sources = phase.shape[0]
    inner = x_ref.shape[2]
    row_block = x_ref.shape[3]
    shape = (row_block, LANES)
    row = pos[0] * row_block + lax.broadcasted_iota(jnp.int32, shape, 0)
    lane = lax.broadcasted_iota(jnp.int32, shape, 1)
    first_bin = row + rows_all * lane
    unit = 2.0 * math.pi / length

    def make_base(s, _):
        turn = ((((first_bin * delay[s]) & (length - 1)) * mode[s]) & (length - 1)).astype(F32)
        angle = mode[s].astype(F32) * phase[s] + turn * unit
        base[0, s] = jnp.cos(angle)
        base[1, s] = jnp.sin(angle)
        return 0

    lax.fori_loop(0, sources, make_base, 0)

    def add_sources(v, _):
        here = first_bin + (rows_all * LANES) * v
        total = [x_ref[r, c, v] for r in range(2) for c in range(channels)]
        for s in range(sources):
            which = (delay[s] * mode[s] * v) & (inner - 1)
            tr, ti = turn_ref[0, which], turn_ref[1, which]
            inside = (here >= bins[0, s]) & (here < bins[1, s])
            br, bi = base[0, s], base[1, s]
            real = jnp.where(inside, br * tr - bi * ti, 0.0)
            imag = jnp.where(inside, br * ti + bi * tr, 0.0)
            for c in range(channels):
                total[c] = total[c] + amp[c, s] * real
                total[channels + c] = total[channels + c] + amp[c, s] * imag
        for n in range(2 * channels):
            acc[n, v] = total[n]
        return 0

    lax.fori_loop(0, inner, add_sources, 0)

    def transform(c, _):
        real, imag = inverse_fft(
            [acc[c, v] for v in range(inner)], [acc[channels + c, v] for v in range(inner)]
        )
        for q in range(inner):
            tc, ts = twist_ref[0, q : q + 1, :], twist_ref[1, q : q + 1, :]
            lhs[c, q, :, 0:LANES] = real[q] * tc - imag[q] * ts
            lhs[c, q, :, LANES : 2 * LANES] = real[q] * ts + imag[q] * tc
        return 0

    lax.fori_loop(0, channels, transform, 0)

    wide = (inner, row_block, LANES)
    parts = PATCH // inner
    width = LANES // parts
    flat = (inner, LANES)
    lanes = lax.broadcasted_iota(jnp.int32, flat, 1)
    outer = lax.div(lanes, width) + parts * lax.rem(lanes, width)
    column = lax.broadcasted_iota(jnp.int32, flat, 0) + inner * outer
    angle = ((pos[0] * row_block * column) & (length - 1)).astype(F32) * unit
    turn_cos, turn_sin = jnp.cos(angle)[:, None, :], jnp.sin(angle)[:, None, :]
    near_cos, near_sin = near_ref[0], near_ref[1]
    cos = turn_cos * near_cos - turn_sin * near_sin
    sin = turn_sin * near_cos + turn_cos * near_sin
    for c in range(channels):
        high, low = split(lhs[c].reshape(inner * row_block, 2 * LANES))
        got = mm(high, high_ref[...]) + mm(low, high_ref[...]) + mm(high, low_ref[...])
        real = got[:, 0:LANES].reshape(wide)
        imag = got[:, LANES : 2 * LANES].reshape(wide)
        out_ref[:, c] = (real * cos - imag * sin).astype(BF16)
        out_ref[:, channels + c] = (real * sin + imag * cos).astype(BF16)


def run_first(spectrum, amp, phase, mode, delay, bins, pos, rows_all, length):
    _, channels, row_block, columns = spectrum.shape
    inner = columns // LANES
    grid_in = spectrum.reshape(2, channels, row_block, inner, LANES).transpose(0, 1, 3, 2, 4)
    steps = np.arange(inner)
    turn = 2.0 * np.pi * steps / inner
    turns = np.stack([np.cos(turn), np.sin(turn)]).astype(np.float32)
    lane = np.arange(LANES)
    twist = 2.0 * np.pi * (steps[:, None] * lane[None, :] % columns) / columns
    twists = np.stack([np.cos(twist), np.sin(twist)]).astype(np.float32)
    column = steps[:, None] + inner * lane_bins(inner)[None, :]
    near = 2.0 * np.pi * np.arange(row_block)[None, :, None] * column[:, None, :] / length
    nears = np.stack([np.cos(near), np.sin(near)]).astype(np.float32)
    angle = 2.0 * np.pi * (lane[:, None] * lane_bins(inner)[None, :] % LANES) / LANES
    cos, sin = np.cos(angle), np.sin(angle)
    high, low = two_halves(np.block([[cos, sin], [-sin, cos]]))
    return pl.pallas_call(
        functools.partial(first_section, rows_all, length),
        out_shape=jax.ShapeDtypeStruct((inner, 2 * channels, row_block, LANES), BF16),
        in_specs=[SMEM] * 7 + [VMEM] * 5,
        out_specs=VMEM,
        scratch_shapes=[
            pltpu.VMEM((2, amp.shape[0], row_block, LANES), F32),
            pltpu.VMEM((2 * channels, inner, row_block, LANES), F32),
            pltpu.VMEM((channels, inner, row_block, 2 * LANES), F32),
        ],
        compiler_params=PARAMS,
        cost_estimate=cost(7),
        name="first_section",
    )(pos, amp.T, phase, mode, delay, bins.T, turns, grid_in, twists, nears, high, low)


def second_section(reps, z_ref, high_ref, low_ref, out_ref):
    devices, own, pairs, row_block, _ = z_ref.shape
    channels = pairs // 2
    rows = devices * row_block
    tiles = own * pairs
    half = (tiles + 1) // 2
    lane = lax.broadcasted_iota(jnp.int32, (rows, LANES), 1)
    sub = lax.rem(lax.broadcasted_iota(jnp.int32, (rows, LANES), 0), row_block)
    upper = (lane & 32) != 0
    rim = jnp.zeros((rows, LANES), F32)
    for q in range(own):
        for c in range(channels):
            right = jnp.concatenate(
                [z_ref[:, q, r * channels + c].astype(F32).reshape(rows, LANES) for r in range(2)], axis=0
            ).astype(BF16)
            got = mm(high_ref[...], right) + mm(low_ref[...], right)
            for r in range(2):
                tile = q * pairs + r * channels + c
                part = got[r * rows : (r + 1) * rows]
                out_ref[:, tile] = part.reshape(devices, row_block, LANES).astype(BF16)
                ends = jnp.broadcast_to(
                    part.reshape(devices, row_block, LANES)[:, row_block - 1 :, :],
                    (devices, row_block, LANES),
                ).reshape(rows, LANES)
                if tile < half:
                    rim = jnp.where(upper & (sub == tile), ends, rim)
                else:
                    ends = pltpu.roll(ends, LANES - 32, 1)
                    rim = jnp.where(jnp.logical_not(upper) & (sub == tile - half), ends, rim)
    rim = rim.reshape(devices, row_block, LANES).astype(BF16)
    for d in range(devices):
        source = d - d % reps - 1
        out_ref[d, tiles] = rim[source] if source >= 0 else jnp.zeros((row_block, LANES), BF16)


def run_second(z, length):
    devices, own, pairs, row_block, _ = z.shape
    rows = devices * row_block
    counter = np.arange(rows)
    angle = 2.0 * np.pi * (counter[:, None] * counter[None, :] % rows) / rows
    cos, sin = np.cos(angle), np.sin(angle)
    high, low = two_halves(np.block([[cos, -sin], [sin, cos]]) / math.sqrt(length))
    return pl.pallas_call(
        functools.partial(second_section, lax.axis_size("rep")),
        out_shape=jax.ShapeDtypeStruct((devices, own * pairs + 1, row_block, LANES), BF16),
        in_specs=[VMEM] * 3,
        out_specs=VMEM,
        compiler_params=PARAMS,
        cost_estimate=cost(3),
        name="second_section",
    )(z, high, low)


def order_patches(x_ref, perm_ref, rim_ref, out_ref, wide):
    devices, tiles, row_block, _ = x_ref.shape
    parts = perm_ref.shape[0]
    width = LANES // parts
    half = tiles // 2
    wide[...] = x_ref[...].astype(F32).reshape(devices * tiles * row_block, LANES)
    for m in range(row_block):
        rows = wide[pl.ds(m, devices * tiles, stride=row_block), :]
        across = rows.T.astype(BF16)
        total = mm(across[0:width], perm_ref[0])
        for n in range(1, parts):
            total = total + mm(across[n * width : (n + 1) * width], perm_ref[n])
        out_ref[m * width : (m + 1) * width, :] = total.astype(BF16)
    rows = jnp.concatenate(
        [wide[pl.ds((tiles - 1) * row_block + n, devices, stride=tiles * row_block), :] for n in range(half)],
        axis=0,
    )
    across = jnp.concatenate([rows, pltpu.roll(rows, 32, 1)], axis=0).T.astype(BF16)
    total = mm(across[width - 8 : width], rim_ref[0])
    for n in range(1, parts):
        total = total + mm(across[(n + 1) * width - 8 : (n + 1) * width], rim_ref[n])
    out_ref[row_block * width :, :] = total.astype(BF16)


def run_order(x, inner, channels):
    devices, tiles, row_block, _ = x.shape
    parts = PATCH // inner
    own = tiles - 1
    pairs = 2 * channels
    each = own // pairs
    perm = np.zeros((parts, devices * tiles, pairs * PATCH), ml_dtypes.bfloat16)
    rim = np.zeros((parts, own * devices, pairs * PATCH), ml_dtypes.bfloat16)
    for n in range(parts):
        for j in range(devices):
            for q in range(each):
                for rc in range(pairs):
                    to = rc * PATCH + n * inner + j * each + q
                    perm[n, j * tiles + q * pairs + rc, to] = 1
                    rim[n, (q * pairs + rc) * devices + j, to] = 1
    return pl.pallas_call(
        order_patches,
        out_shape=jax.ShapeDtypeStruct((row_block * LANES // parts + 8, pairs * PATCH), BF16),
        in_specs=[VMEM] * 3,
        out_specs=VMEM,
        scratch_shapes=[pltpu.VMEM((devices * tiles * row_block, LANES), F32)],
        compiler_params=PARAMS,
        cost_estimate=cost(3),
        name="order_patches",
    )(x, perm, rim)


def dft_table(order):
    counter = jnp.arange(order, dtype=jnp.int32)
    turn_count = counter[:, None] * counter[None, :] % order
    radians = turn_count.astype(F32) * (2.0 * math.pi / order)
    return jnp.stack([jnp.cos(radians), jnp.sin(radians)])


def make_patches(first, length):
    devices = lax.axis_size(ALL)
    inner, pairs, row_block, _ = first.shape
    channels = pairs // 2
    if inner % devices == 0 and 2 * inner == PATCH and inner // devices * pairs in range(2, 17, 2):
        own = inner // devices
        moved = lax.all_to_all(
            first.reshape(devices, own, pairs, row_block, LANES), ALL, 0, 0, tiled=True
        )
        moved = lax.all_to_all(run_second(moved, length), ALL, 0, 0, tiled=True)
        return run_order(moved, inner, channels)
    flat = first.transpose(1, 2, 0, 3).reshape(2, channels, row_block, inner * LANES)
    flat = lax.all_to_all(flat, ALL, split_axis=3, concat_axis=2, tiled=True).astype(F32)
    mixed = jnp.einsum(
        "rcuq,kum->krcqm", flat, dft_table(row_block * devices), precision=lax.Precision.HIGHEST
    )
    series = jnp.stack([mixed[0, 0] - mixed[1, 1], mixed[1, 0] + mixed[0, 1]])
    series = (series * (1.0 / math.sqrt(length))).astype(BF16)
    series = lax.all_to_all(series, ALL, split_axis=4 - 1, concat_axis=2, tiled=True)
    parts = PATCH // inner
    series = series.reshape(2, channels, inner, parts, LANES // parts, row_block)
    patches = series.transpose(5, 4, 0, 1, 3, 2).reshape(
        row_block * LANES // parts, 2 * channels * PATCH
    )
    reps = lax.axis_size("rep")
    tail = patches[patches.shape[0] - 8 :]
    rim = jnp.zeros_like(tail)
    for r in range(reps):
        pairs = [(i - 1, i + r) for i in range(reps, devices, reps)]
        rim = rim + lax.ppermute(tail, ALL, pairs)
    return jnp.concatenate([patches, rim], 0)


def norm_rows(values, total):
    return lax.rsqrt(jnp.sum(values * values, axis=-1, keepdims=True) * (1.0 / total) + EPSILON)


def silu(values):
    half = 0.5 * values
    return half + half * jnp.tanh(half)


def fold(ends, count, head, entering, upto=None):
    state = entering.shape[0]
    for i in range(count):
        part, decay = ends[0][0:state], ends[0][state : state + 1]
        for j in range(1, len(ends)):
            here = (head ^ i) == j
            part = jnp.where(here, ends[j][0:state], part)
            decay = jnp.where(here, ends[j][state : state + 1], decay)
        after = decay * entering + part
        entering = after if upto is None else jnp.where(i < upto, after, entering)
    return entering


def expand(values, spread):
    high, low = split(values)
    return mm(jnp.concatenate([high, low], axis=1), spread[...])


def block_states(heads, per, reps, before, final, me_ref, *refs):
    pats, refs = refs[:2], refs[2:]
    halo, we, nin, wx, wbc, wdt, dtb, alog, cx, cbc, spread = refs[:11]
    earlier, refs = refs[11 : 11 + before], refs[11 + before :]
    normed_ref, x_ref, b_ref, c_ref, cum_ref, step_ref, local_ref, grown_ref, st_ref = refs[:9]
    xs, bcs, carried, total, low_tri, dts, rows, tail = refs[-8:]
    block = pl.program_id(0)
    state = wbc.shape[1] // 2
    taps = cx.shape[0]

    gains = nin[...].astype(F32)
    gains = jnp.concatenate([gains[i : i + 1] for i in range(gains.shape[0])], axis=1)

    def features(p):
        embedded = mm(p, we[...]).astype(BF16).astype(F32)
        scale = norm_rows(embedded, embedded.shape[-1])
        return (embedded * scale * gains).astype(BF16)

    @pl.when(block == 0)
    def _():
        carried[...] = jnp.zeros_like(carried)
        total[...] = jnp.zeros_like(total)
        tail[...] = halo[...].astype(F32)
        ri = lax.broadcasted_iota(jnp.int32, (SPAN, SPAN), 0)
        ci = lax.broadcasted_iota(jnp.int32, (SPAN, SPAN), 1)
        low_tri[...] = jnp.where(ri >= ci, 1.0, 0.0).astype(BF16)
        dts[...] = jnp.zeros_like(dts)
        rows[...] = jnp.zeros_like(rows)
        rows[0:1, 0:heads] = dtb[...]
        rows[1:2, 0:heads] = -jnp.exp(alog[...])

    here = ((block // per) ^ lax.rem(me_ref[0], reps)) == 0
    span = pats[0].shape[0]
    patch = jnp.where(here, pats[0][...], pats[1][...]).astype(F32)
    joined = features(jnp.concatenate([tail[...], patch], axis=0).astype(BF16))
    tail[...] = patch[span - 8 :]
    normed = joined[8:]
    normed_ref[...] = normed
    dts[:, 0:heads] = lax.dot_general(
        normed, wdt[...], (((1,), (1,)), ((), ())), preferred_element_type=F32
    )
    bcs[...] = mm(joined, wbc[...]).astype(BF16).astype(F32)
    xs[...] = mm(joined, wx[...]).astype(BF16).astype(F32)
    step_all = dts[...] + rows[0:1]
    step_all = jnp.maximum(step_all, 0.0) + jnp.log1p(jnp.exp(-jnp.abs(step_all)))
    step_ref[...] = step_all

    def conv(buffer, kernel, at):
        out = kernel[0:1] * buffer[at + 9 - taps : at + 9 - taps + SPAN]
        for i in range(1, taps):
            out = out + kernel[i : i + 1] * buffer[at + 9 - taps + i : at + 9 - taps + i + SPAN]
        return silu(out)

    for n in range(span // SPAN):
        at = n * SPAN
        step = step_all[at : at + SPAN]
        rated = step * rows[1:2]
        one = rated.astype(BF16).astype(F32)
        two = (rated - one).astype(BF16).astype(F32)
        three = rated - one - two
        packed = one + pltpu.roll(two, heads, 1) + pltpu.roll(three, 2 * heads, 1)
        sums = mm(low_tri[...], packed.astype(BF16))
        cum = sums + pltpu.roll(sums, LANES - heads, 1) + pltpu.roll(sums, LANES - 2 * heads, 1)
        cum_ref[at : at + SPAN] = cum
        last = cum[SPAN - 1 : SPAN]
        weights = expand(jnp.exp(last - cum) * step, spread)
        grow = expand(
            jnp.exp(jnp.concatenate([jnp.broadcast_to(last, (8, LANES)), total[...]], axis=0)), spread
        )
        bc = conv(bcs, cbc, at)
        b_ref[at : at + SPAN] = bc[:, :state].astype(BF16)
        c_ref[at : at + SPAN] = bc[:, state:].astype(BF16)
        bt = bc[:, :state].T.astype(BF16)
        xc = conv(xs, cx, at).astype(BF16)
        x_ref[at : at + SPAN] = xc
        weighted = (xc.astype(F32) * weights).astype(BF16)
        local_ref[n] = carried[...]
        grown_ref[n] = grow[8:16]
        carried[...] = carried[...] * grow[0:1] + mm(bt, weighted)
        total[...] = total[...] + last

    @pl.when(block == pl.num_programs(0) - 1)
    def _():
        st_ref[0:state] = carried[...]
        st_ref[state : state + 8] = grow[8:16] * grow[0:8]
        if final:
            everything = [e[...] for e in earlier] + [st_ref[...]]
            count = len(everything)
            send = refs[9]
            zero = jnp.zeros((state, xs.shape[1]), F32)
            send[0:state] = fold(everything, count, lax.div(me_ref[0], reps), zero).astype(BF16)
            decay = everything[0][state : state + 8]
            for e in everything[1:]:
                decay = decay * e[state : state + 8]
            send[state : state + 8] = decay.astype(BF16)


def run_states(me, pats, halo, consts, heads, inner, state, own, earlier, final):
    rows_in, width = pats[0].shape
    model = consts[0].shape[1]
    tokens = own * len(pats)
    span = min(own, TILE)
    per = own // span
    blocks = tokens // SPAN
    subs = span // SPAN
    row = lambda n: pl.BlockSpec((span, n), lambda b, me: (b, 0))
    fixed = pl.BlockSpec((state + 8, inner), lambda b, me: (0, 0))
    shape = lambda *d, t=F32: jax.ShapeDtypeStruct(d, t)
    return pl.pallas_call(
        functools.partial(block_states, heads, per, len(pats), len(earlier), final),
        grid_spec=pltpu.PrefetchScalarGridSpec(
            num_scalar_prefetch=1,
            grid=(tokens // span,),
            in_specs=[pl.BlockSpec((span, width), lambda b, me: (b % per, 0))] * len(pats)
            + [pl.BlockSpec((8, width), lambda b, me: (own // 8, 0))]
            + [VMEM] * (len(consts) + len(earlier)),
            out_specs=[row(model), row(inner), row(state), row(state), row(LANES), row(LANES),
                       pl.BlockSpec((subs, state, inner), lambda b, me: (b, 0, 0)),
                       pl.BlockSpec((subs, 8, inner), lambda b, me: (b, 0, 0)), fixed]
            + [fixed] * final,
            scratch_shapes=[
                pltpu.VMEM((span + 8, inner), F32),
                pltpu.VMEM((span + 8, 2 * state), F32),
                pltpu.VMEM((state, inner), F32),
                pltpu.VMEM((8, LANES), F32),
                pltpu.VMEM((SPAN, SPAN), BF16),
                pltpu.VMEM((span, LANES), F32),
                pltpu.VMEM((8, LANES), F32),
                pltpu.VMEM((8, width), F32),
            ],
        ),
        out_shape=[
            shape(tokens, model, t=BF16), shape(tokens, inner, t=BF16), shape(tokens, state, t=BF16),
            shape(tokens, state, t=BF16), shape(tokens, LANES), shape(tokens, LANES),
            shape(blocks, state, inner), shape(blocks, 8, inner), shape(state + 8, inner),
        ] + [shape(state + 8, inner, t=BF16)] * final,
        compiler_params=PARAMS,
        cost_estimate=cost(13),
        name="block_states",
    )(me, *pats, halo, *consts, *earlier)


def outputs(
    heads, chip, chips, reps, me_ref, normed_ref, x_ref, b_ref, c_ref, cum_ref, step_ref, local_ref, grown_ref,
    wz, spread, *refs,
):
    ends, earlier = refs[:chips], refs[chips : -reps - 2]
    outs, start, y_acc = refs[-reps - 2 : -2], refs[-2], refs[-1]
    state = c_ref.shape[1]
    block = pl.program_id(0)
    per = pl.num_programs(0) // reps

    @pl.when(block == 0)
    def _():
        entering = jnp.zeros((state, x_ref.shape[1]), F32)
        for part in reversed(earlier):
            entering = part[0:state].astype(F32) + part[state : state + 1].astype(F32) * entering
        place = lax.div(me_ref[0], reps)
        start[...] = fold([e[...] for e in ends], chips - 1, place, entering, place ^ chip)

    cum = cum_ref[...]
    log_cum = cum * LOG2E
    back = (log_cum - jnp.log2(step_ref[...])).T
    gram = lax.dot_general(
        c_ref[...], b_ref[...], (((1,), (1,)), ((), ())), preferred_element_type=F32
    )
    gate = silu(mm(normed_ref[...], wz[...]).astype(BF16).astype(F32))
    half = SPAN // 2
    ri = lax.broadcasted_iota(jnp.int32, (half, half), 0)
    ci = lax.broadcasted_iota(jnp.int32, (half, half), 1)
    inside = ri >= ci
    head_dim = x_ref.shape[1] // heads
    for h in range(heads):
        cols = slice(h * head_dim, (h + 1) * head_dim)
        upper, lower = log_cum[:half, h : h + 1], log_cum[half:, h : h + 1]
        early, late = back[h : h + 1, :half], back[h : h + 1, half:]
        first = jnp.where(inside, jnp.exp2(upper - early), 0.0) * gram[:half, :half]
        cross = jnp.exp2(lower - early) * gram[half:, :half]
        second = jnp.where(inside, jnp.exp2(lower - late), 0.0) * gram[half:, half:]
        y_acc[:half, cols] = mm(first.astype(BF16), x_ref[:half, cols])
        y_acc[half:, cols] = mm(
            jnp.concatenate([cross.astype(BF16), second.astype(BF16)], axis=1), x_ref[:, cols]
        )
    cm = c_ref[...]
    high, low = split(local_ref[0] + grown_ref[0, 0:1] * start[...])
    added = mm(jnp.concatenate([cm, cm], axis=1), jnp.concatenate([high, low], axis=0))
    value = ((y_acc[...] + expand(jnp.exp(cum), spread) * added) * gate).astype(BF16)
    for r in range(reps):
        @pl.when((block // per) == (lax.rem(me_ref[0], reps) ^ r))
        def _(r=r):
            outs[r][pl.ds(pl.multiple_of((block % per) * SPAN, SPAN), SPAN), :] = value


def run_outputs(heads, chip, reps, me, normed, xc, bm, cm, cum, step, local, grown, wz, spread, ends, earlier, own):
    tokens, inner = xc.shape
    state = cm.shape[1]
    row = lambda n: pl.BlockSpec((SPAN, n), lambda b, me: (b, 0))
    block3 = lambda b, me: (b, 0, 0)
    return pl.pallas_call(
        functools.partial(outputs, heads, chip, len(ends), reps),
        grid_spec=pltpu.PrefetchScalarGridSpec(
            num_scalar_prefetch=1,
            grid=(tokens // SPAN,),
            in_specs=[row(a.shape[1]) for a in (normed, xc, bm, cm, cum, step)]
            + [pl.BlockSpec((1, state, inner), block3), pl.BlockSpec((1, 8, inner), block3)]
            + [VMEM] * (2 + len(earlier) + len(ends)),
            out_specs=[pl.BlockSpec((own, inner), lambda b, me: (0, 0))] * reps,
            scratch_shapes=[pltpu.VMEM((state, inner), F32), pltpu.VMEM((SPAN, inner), F32)],
        ),
        out_shape=[jax.ShapeDtypeStruct((own, inner), BF16)] * reps,
        compiler_params=PARAMS,
        cost_estimate=cost(9 if chip else 0.05),
        name="outputs",
    )(me, normed, xc, bm, cm, cum, step, local, grown, wz, spread, *ends, *earlier)


def mix_most(count, me_ref, pat_ref, we_ref, *refs):
    parts, (norm, weight, embed_ref, mixed_ref, square_ref) = refs[:count], refs[count:]
    step = pl.program_id(0)

    @pl.when(step == 0)
    def _():
        embed_ref[...] = mm(pat_ref[...], we_ref[...]).astype(BF16)
        square = None
        for part in parts:
            v = part[...].astype(F32)
            square = v * v if square is None else square + v * v
        square_ref[...] = jnp.broadcast_to(jnp.sum(square, axis=-1, keepdims=True), square_ref.shape)

    for n in range(count):
        @pl.when(step == n)
        def _(n=n):
            left = (parts[n][...].astype(F32) * norm[...].astype(F32)).astype(BF16)
            got = mm(left, weight[0])
            mixed_ref[...] = got if n == 0 else mixed_ref[...] + got


def mix_last(total, me_ref, embed_ref, mixed_ref, square_ref, part_ref, norm, weight, out_ref):
    v = part_ref[...].astype(F32)
    got = mm((v * norm[...].astype(F32)).astype(BF16), weight[0])
    square = square_ref[:, 0:1] + jnp.sum(v * v, axis=-1, keepdims=True)
    scale = lax.rsqrt(square * (1.0 / total) + EPSILON)
    out_ref[...] = (embed_ref[...].astype(F32) + scale * (mixed_ref[...] + got)).astype(BF16)


def run_mix(me, patches, we, parts, norm_out, w_out):
    share = len(parts)
    count = share - 1
    own, inner = parts[0].shape
    width = w_out.shape[1]
    norms = norm_out[None]
    weights = w_out.reshape(share, inner, width)
    full = pl.BlockSpec((own, width), lambda d, me: (0, 0))
    embed, mixed, square = pl.pallas_call(
        functools.partial(mix_most, count),
        grid_spec=pltpu.PrefetchScalarGridSpec(
            num_scalar_prefetch=1,
            grid=(count,),
            in_specs=[pl.BlockSpec((own, patches.shape[1]), lambda d, me: (0, 0)), VMEM] + [VMEM] * count
            + [pl.BlockSpec((1, inner), lambda d, me: (0, me[0] ^ d)),
               pl.BlockSpec((1, inner, width), lambda d, me: (me[0] ^ d, 0, 0))],
            out_specs=[full, full, pl.BlockSpec((own, LANES), lambda d, me: (0, 0))],
        ),
        out_shape=[jax.ShapeDtypeStruct((own, width), BF16), jax.ShapeDtypeStruct((own, width), F32),
                   jax.ShapeDtypeStruct((own, LANES), F32)],
        compiler_params=PARAMS,
        cost_estimate=cost(0.05),
        name="mix_most",
    )(me, patches, we, *parts[:count], norms, weights)
    tile = SPAN
    row = lambda n: pl.BlockSpec((tile, n), lambda i, me: (i, 0))
    return pl.pallas_call(
        functools.partial(mix_last, share * inner),
        grid_spec=pltpu.PrefetchScalarGridSpec(
            num_scalar_prefetch=1,
            grid=(own // tile,),
            in_specs=[row(width), row(width), row(LANES), row(inner),
                      pl.BlockSpec((1, inner), lambda i, me: (0, me[0] ^ count)),
                      pl.BlockSpec((1, inner, width), lambda i, me: (me[0] ^ count, 0, 0))],
            out_specs=row(width),
        ),
        out_shape=jax.ShapeDtypeStruct((own, width), BF16),
        compiler_params=PARAMS,
        cost_estimate=cost(3),
        name="mix_last",
    )(me, embed, mixed, square, parts[count], norms, weights)


def swap(value, flip):
    count = lax.axis_size(HR)
    return lax.ppermute(value, HR, [(i, i ^ flip) for i in range(count)])


def shift(value, by):
    count = lax.axis_size("seq")
    return lax.ppermute(value, "seq", [(i, i + by) for i in range(count - by)])


def on_device(
    spectrum, src_amp, src_phase, src_mode, src_delay, src_bins, w_embed, norm_in, w_z, w_x, w_bc, w_dt,
    dt_bias, a_log, conv_x, conv_bc, norm_out, w_out,
):
    devices = lax.axis_size(ALL)
    share = lax.axis_size(HR)
    rows_all = spectrum.shape[2] * devices
    length = rows_all * spectrum.shape[3]
    pos = lax.axis_index(ALL).astype(jnp.int32).reshape(1)
    me = lax.axis_index(HR).astype(jnp.int32).reshape(1)
    first = run_first(
        spectrum, src_amp, src_phase, src_mode, src_delay, src_bins, pos, rows_all, length
    )
    patches = make_patches(first, length)
    own = patches.shape[0] - 8
    reps, chips = lax.axis_size("rep"), lax.axis_size("head")
    heads, inner, state = dt_bias.shape[0], w_x.shape[1], w_bc.shape[1] // 2
    spread = np.zeros((2 * LANES, inner), ml_dtypes.bfloat16)
    for h in range(heads):
        spread[h, h * (inner // heads) : (h + 1) * (inner // heads)] = 1
    spread[LANES:] = spread[:LANES]
    consts = (
        w_embed, norm_in.reshape(-1, LANES), w_x, w_bc, w_dt.T, dt_bias[None], a_log[None], conv_x, conv_bc,
        jnp.asarray(spread),
    )
    done, ends = [], []
    base = [patches] + [swap(patches, c * reps) for c in range(1, chips)]
    for c in range(chips):
        start = base[c]
        if ends:
            start, ends[-1] = lax.optimization_barrier((start, ends[-1]))
        group = [start] + [swap(start, r) for r in range(1, reps)]
        got = run_states(
            me, group, start, consts, heads, inner, state, own, ends, c == chips - 1
        )
        done.append(got[:8])
        ends.append(got[8])
    send = got[9]
    earlier = [shift(send, d) for d in range(1, lax.axis_size("seq"))]
    parts = [None] * share
    gate = None
    for c in list(range(1, chips)) + [0]:
        normed, xc, bm, cm, cum, step, local, grown = done[c]
        if gate is not None:
            normed, gate = lax.optimization_barrier((normed, gate))
        values = run_outputs(
            heads, c, reps, me, normed, xc, bm, cm, cum, step, local, grown, w_z, spread, ends, earlier, own
        )
        gate = values[0]
        for r in reversed(range(reps)):
            d = c * reps + r
            if d == 1:
                half = own // 2
                parts[d] = jnp.concatenate([swap(values[r][:half], d), swap(values[r][half:], d)], 0)
            else:
                parts[d] = swap(values[r], d) if d else values[r]
    return run_mix(me, patches, w_embed, parts, norm_out, w_out)


def solution(mesh):
    in_specs = (
        P("grp", None, ("seq", "head", "rep"), None),
        P("grp", None),
        P("grp"),
        P("grp"),
        P("grp"),
        P("grp", None),
        P(),
        P(),
        P(None, ("head", "rep")),
        P(None, ("head", "rep")),
        P(),
        P(None, ("head", "rep")),
        P(("head", "rep")),
        P(("head", "rep")),
        P(None, ("head", "rep")),
        P(),
        P(),
        P(),
    )
    out_specs = P(("grp", "seq", "head", "rep"), None)
    return jax.shard_map(
        on_device, mesh=mesh, in_specs=in_specs, out_specs=out_specs, check_vma=False
    )
```

```python
import functools
import math

import jax
import jax.numpy as jnp
import ml_dtypes
import numpy as np
from jax import lax
from jax.experimental import pallas as pl
from jax.experimental.pallas import tpu as pltpu
from jax.sharding import PartitionSpec as P

SPAN = 256
LOG2E = math.log2(math.e)
TILE = 512
EPSILON = 1e-05
LANES = 128
PATCH = 64
ALL = ("seq", "head", "rep")
HR = ("head", "rep")
F32 = jnp.float32
BF16 = jnp.bfloat16
VMEM = pl.BlockSpec(memory_space=pltpu.VMEM)
SMEM = pl.BlockSpec(memory_space=pltpu.SMEM)


def cost(micros):
    return pl.CostEstimate(
        flops=int(micros * 1e9), transcendentals=0, bytes_accessed=int(micros * 3e6)
    )


PARAMS = pltpu.CompilerParams(vmem_limit_bytes=56 * 1024 * 1024)


def two_halves(table):
    high = table.astype(ml_dtypes.bfloat16)
    return high, (table - high.astype(np.float64)).astype(ml_dtypes.bfloat16)


def mm(a, b):
    return jnp.dot(a, b, preferred_element_type=F32)


def split(a):
    high = a.astype(BF16)
    return high, (a - high.astype(F32)).astype(BF16)


def lane_bins(inner):
    parts = PATCH // inner
    lane = np.arange(LANES)
    width = LANES // parts
    return lane // width + parts * (lane % width)


def inverse_fft(real, imag):
    count = len(real)
    if count == 1:
        return real, imag
    even_r, even_i = inverse_fft(real[0::2], imag[0::2])
    odd_r, odd_i = inverse_fft(real[1::2], imag[1::2])
    half = count // 2
    out_r, out_i = [None] * count, [None] * count
    for k in range(half):
        angle = 2.0 * math.pi * k / count
        c, s = math.cos(angle), math.sin(angle)
        if k == 0:
            r, i = odd_r[k], odd_i[k]
        elif 4 * k == count:
            r, i = -odd_i[k], odd_r[k]
        else:
            r = odd_r[k] * c - odd_i[k] * s
            i = odd_r[k] * s + odd_i[k] * c
        out_r[k], out_i[k] = even_r[k] + r, even_i[k] + i
        out_r[k + half], out_i[k + half] = even_r[k] - r, even_i[k] - i
    return out_r, out_i


def first_section(
    rows_all, length, pos, amp, phase, mode, delay, bins, turn_ref, x_ref, twist_ref, near_ref, high_ref, low_ref,
    out_ref, base, acc, lhs,
):
    channels = x_ref.shape[1]
    sources = phase.shape[0]
    inner = x_ref.shape[2]
    row_block = x_ref.shape[3]
    shape = (row_block, LANES)
    row = pos[0] * row_block + lax.broadcasted_iota(jnp.int32, shape, 0)
    lane = lax.broadcasted_iota(jnp.int32, shape, 1)
    first_bin = row + rows_all * lane
    unit = 2.0 * math.pi / length

    def make_base(s, _):
        turn = ((((first_bin * delay[s]) & (length - 1)) * mode[s]) & (length - 1)).astype(F32)
        angle = mode[s].astype(F32) * phase[s] + turn * unit
        base[0, s] = jnp.cos(angle)
        base[1, s] = jnp.sin(angle)
        return 0

    lax.fori_loop(0, sources, make_base, 0)

    def add_sources(v, _):
        here = first_bin + (rows_all * LANES) * v
        total = [x_ref[r, c, v] for r in range(2) for c in range(channels)]
        for s in range(sources):
            which = (delay[s] * mode[s] * v) & (inner - 1)
            tr, ti = turn_ref[0, which], turn_ref[1, which]
            inside = (here >= bins[0, s]) & (here < bins[1, s])
            br, bi = base[0, s], base[1, s]
            real = jnp.where(inside, br * tr - bi * ti, 0.0)
            imag = jnp.where(inside, br * ti + bi * tr, 0.0)
            for c in range(channels):
                total[c] = total[c] + amp[c, s] * real
                total[channels + c] = total[channels + c] + amp[c, s] * imag
        for n in range(2 * channels):
            acc[n, v] = total[n]
        return 0

    lax.fori_loop(0, inner, add_sources, 0)

    def transform(c, _):
        real, imag = inverse_fft(
            [acc[c, v] for v in range(inner)], [acc[channels + c, v] for v in range(inner)]
        )
        for q in range(inner):
            tc, ts = twist_ref[0, q : q + 1, :], twist_ref[1, q : q + 1, :]
            lhs[c, q, :, 0:LANES] = real[q] * tc - imag[q] * ts
            lhs[c, q, :, LANES : 2 * LANES] = real[q] * ts + imag[q] * tc
        return 0

    lax.fori_loop(0, channels, transform, 0)

    wide = (inner, row_block, LANES)
    parts = PATCH // inner
    width = LANES // parts
    flat = (inner, LANES)
    lanes = lax.broadcasted_iota(jnp.int32, flat, 1)
    outer = lax.div(lanes, width) + parts * lax.rem(lanes, width)
    column = lax.broadcasted_iota(jnp.int32, flat, 0) + inner * outer
    angle = ((pos[0] * row_block * column) & (length - 1)).astype(F32) * unit
    turn_cos, turn_sin = jnp.cos(angle)[:, None, :], jnp.sin(angle)[:, None, :]
    near_cos, near_sin = near_ref[0], near_ref[1]
    cos = turn_cos * near_cos - turn_sin * near_sin
    sin = turn_sin * near_cos + turn_cos * near_sin
    for c in range(channels):
        high, low = split(lhs[c].reshape(inner * row_block, 2 * LANES))
        got = mm(high, high_ref[...]) + mm(low, high_ref[...]) + mm(high, low_ref[...])
        real = got[:, 0:LANES].reshape(wide)
        imag = got[:, LANES : 2 * LANES].reshape(wide)
        out_ref[:, c] = (real * cos - imag * sin).astype(BF16)
        out_ref[:, channels + c] = (real * sin + imag * cos).astype(BF16)


def run_first(spectrum, amp, phase, mode, delay, bins, pos, rows_all, length):
    _, channels, row_block, columns = spectrum.shape
    inner = columns // LANES
    grid_in = spectrum.reshape(2, channels, row_block, inner, LANES).transpose(0, 1, 3, 2, 4)
    steps = np.arange(inner)
    turn = 2.0 * np.pi * steps / inner
    turns = np.stack([np.cos(turn), np.sin(turn)]).astype(np.float32)
    lane = np.arange(LANES)
    twist = 2.0 * np.pi * (steps[:, None] * lane[None, :] % columns) / columns
    twists = np.stack([np.cos(twist), np.sin(twist)]).astype(np.float32)
    column = steps[:, None] + inner * lane_bins(inner)[None, :]
    near = 2.0 * np.pi * np.arange(row_block)[None, :, None] * column[:, None, :] / length
    nears = np.stack([np.cos(near), np.sin(near)]).astype(np.float32)
    angle = 2.0 * np.pi * (lane[:, None] * lane_bins(inner)[None, :] % LANES) / LANES
    cos, sin = np.cos(angle), np.sin(angle)
    high, low = two_halves(np.block([[cos, sin], [-sin, cos]]))
    return pl.pallas_call(
        functools.partial(first_section, rows_all, length),
        out_shape=jax.ShapeDtypeStruct((inner, 2 * channels, row_block, LANES), BF16),
        in_specs=[SMEM] * 7 + [VMEM] * 5,
        out_specs=VMEM,
        scratch_shapes=[
            pltpu.VMEM((2, amp.shape[0], row_block, LANES), F32),
            pltpu.VMEM((2 * channels, inner, row_block, LANES), F32),
            pltpu.VMEM((channels, inner, row_block, 2 * LANES), F32),
        ],
        compiler_params=PARAMS,
        cost_estimate=cost(7),
        name="first_section",
    )(pos, amp.T, phase, mode, delay, bins.T, turns, grid_in, twists, nears, high, low)


def second_section(reps, z_ref, high_ref, low_ref, out_ref):
    devices, own, pairs, row_block, _ = z_ref.shape
    channels = pairs // 2
    rows = devices * row_block
    tiles = own * pairs
    half = (tiles + 1) // 2
    lane = lax.broadcasted_iota(jnp.int32, (rows, LANES), 1)
    sub = lax.rem(lax.broadcasted_iota(jnp.int32, (rows, LANES), 0), row_block)
    upper = (lane & 32) != 0
    rim = jnp.zeros((rows, LANES), F32)
    for q in range(own):
        for c in range(channels):
            right = jnp.concatenate(
                [z_ref[:, q, r * channels + c].astype(F32).reshape(rows, LANES) for r in range(2)], axis=0
            ).astype(BF16)
            got = mm(high_ref[...], right) + mm(low_ref[...], right)
            for r in range(2):
                tile = q * pairs + r * channels + c
                part = got[r * rows : (r + 1) * rows]
                out_ref[:, tile] = part.reshape(devices, row_block, LANES).astype(BF16)
                ends = jnp.broadcast_to(
                    part.reshape(devices, row_block, LANES)[:, row_block - 1 :, :],
                    (devices, row_block, LANES),
                ).reshape(rows, LANES)
                if tile < half:
                    rim = jnp.where(upper & (sub == tile), ends, rim)
                else:
                    ends = pltpu.roll(ends, LANES - 32, 1)
                    rim = jnp.where(jnp.logical_not(upper) & (sub == tile - half), ends, rim)
    rim = rim.reshape(devices, row_block, LANES).astype(BF16)
    for d in range(devices):
        source = d - d % reps - 1
        out_ref[d, tiles] = rim[source] if source >= 0 else jnp.zeros((row_block, LANES), BF16)


def run_second(z, length):
    devices, own, pairs, row_block, _ = z.shape
    rows = devices * row_block
    counter = np.arange(rows)
    angle = 2.0 * np.pi * (counter[:, None] * counter[None, :] % rows) / rows
    cos, sin = np.cos(angle), np.sin(angle)
    high, low = two_halves(np.block([[cos, -sin], [sin, cos]]) / math.sqrt(length))
    return pl.pallas_call(
        functools.partial(second_section, lax.axis_size("rep")),
        out_shape=jax.ShapeDtypeStruct((devices, own * pairs + 1, row_block, LANES), BF16),
        in_specs=[VMEM] * 3,
        out_specs=VMEM,
        compiler_params=PARAMS,
        cost_estimate=cost(3),
        name="second_section",
    )(z, high, low)


def order_patches(x_ref, perm_ref, rim_ref, out_ref, wide):
    devices, tiles, row_block, _ = x_ref.shape
    parts = perm_ref.shape[0]
    width = LANES // parts
    half = tiles // 2
    wide[...] = x_ref[...].astype(F32).reshape(devices * tiles * row_block, LANES)
    for m in range(row_block):
        rows = wide[pl.ds(m, devices * tiles, stride=row_block), :]
        across = rows.T.astype(BF16)
        total = mm(across[0:width], perm_ref[0])
        for n in range(1, parts):
            total = total + mm(across[n * width : (n + 1) * width], perm_ref[n])
        out_ref[m * width : (m + 1) * width, :] = total.astype(BF16)
    rows = jnp.concatenate(
        [wide[pl.ds((tiles - 1) * row_block + n, devices, stride=tiles * row_block), :] for n in range(half)],
        axis=0,
    )
    across = jnp.concatenate([rows, pltpu.roll(rows, 32, 1)], axis=0).T.astype(BF16)
    total = mm(across[width - 8 : width], rim_ref[0])
    for n in range(1, parts):
        total = total + mm(across[(n + 1) * width - 8 : (n + 1) * width], rim_ref[n])
    out_ref[row_block * width :, :] = total.astype(BF16)


def run_order(x, inner, channels):
    devices, tiles, row_block, _ = x.shape
    parts = PATCH // inner
    own = tiles - 1
    pairs = 2 * channels
    each = own // pairs
    perm = np.zeros((parts, devices * tiles, pairs * PATCH), ml_dtypes.bfloat16)
    rim = np.zeros((parts, own * devices, pairs * PATCH), ml_dtypes.bfloat16)
    for n in range(parts):
        for j in range(devices):
            for q in range(each):
                for rc in range(pairs):
                    to = rc * PATCH + n * inner + j * each + q
                    perm[n, j * tiles + q * pairs + rc, to] = 1
                    rim[n, (q * pairs + rc) * devices + j, to] = 1
    return pl.pallas_call(
        order_patches,
        out_shape=jax.ShapeDtypeStruct((row_block * LANES // parts + 8, pairs * PATCH), BF16),
        in_specs=[VMEM] * 3,
        out_specs=VMEM,
        scratch_shapes=[pltpu.VMEM((devices * tiles * row_block, LANES), F32)],
        compiler_params=PARAMS,
        cost_estimate=cost(3),
        name="order_patches",
    )(x, perm, rim)


def dft_table(order):
    counter = jnp.arange(order, dtype=jnp.int32)
    turn_count = counter[:, None] * counter[None, :] % order
    radians = turn_count.astype(F32) * (2.0 * math.pi / order)
    return jnp.stack([jnp.cos(radians), jnp.sin(radians)])


def make_patches(first, length):
    devices = lax.axis_size(ALL)
    inner, pairs, row_block, _ = first.shape
    channels = pairs // 2
    if inner % devices == 0 and 2 * inner == PATCH and inner // devices * pairs in range(2, 17, 2):
        own = inner // devices
        moved = lax.all_to_all(
            first.reshape(devices, own, pairs, row_block, LANES), ALL, 0, 0, tiled=True
        )
        moved = lax.all_to_all(run_second(moved, length), ALL, 0, 0, tiled=True)
        return run_order(moved, inner, channels)
    flat = first.transpose(1, 2, 0, 3).reshape(2, channels, row_block, inner * LANES)
    flat = lax.all_to_all(flat, ALL, split_axis=3, concat_axis=2, tiled=True).astype(F32)
    mixed = jnp.einsum(
        "rcuq,kum->krcqm", flat, dft_table(row_block * devices), precision=lax.Precision.HIGHEST
    )
    series = jnp.stack([mixed[0, 0] - mixed[1, 1], mixed[1, 0] + mixed[0, 1]])
    series = (series * (1.0 / math.sqrt(length))).astype(BF16)
    series = lax.all_to_all(series, ALL, split_axis=4 - 1, concat_axis=2, tiled=True)
    parts = PATCH // inner
    series = series.reshape(2, channels, inner, parts, LANES // parts, row_block)
    patches = series.transpose(5, 4, 0, 1, 3, 2).reshape(
        row_block * LANES // parts, 2 * channels * PATCH
    )
    reps = lax.axis_size("rep")
    tail = patches[patches.shape[0] - 8 :]
    rim = jnp.zeros_like(tail)
    for r in range(reps):
        pairs = [(i - 1, i + r) for i in range(reps, devices, reps)]
        rim = rim + lax.ppermute(tail, ALL, pairs)
    return jnp.concatenate([patches, rim], 0)


def norm_rows(values, total):
    return lax.rsqrt(jnp.sum(values * values, axis=-1, keepdims=True) * (1.0 / total) + EPSILON)


def silu(values):
    half = 0.5 * values
    return half + half * jnp.tanh(half)


def fold(ends, count, head, entering, upto=None):
    state = entering.shape[0]
    for i in range(count):
        part, decay = ends[0][0:state], ends[0][state : state + 1]
        for j in range(1, len(ends)):
            here = (head ^ i) == j
            part = jnp.where(here, ends[j][0:state], part)
            decay = jnp.where(here, ends[j][state : state + 1], decay)
        after = decay * entering + part
        entering = after if upto is None else jnp.where(i < upto, after, entering)
    return entering


def expand(values, spread):
    high, low = split(values)
    return mm(jnp.concatenate([high, low], axis=1), spread[...])


def block_states(heads, per, reps, before, final, me_ref, *refs):
    pats, refs = refs[:2], refs[2:]
    halo, we, nin, wx, wbc, wdt, dtb, alog, cx, cbc, spread = refs[:11]
    earlier, refs = refs[11 : 11 + before], refs[11 + before :]
    normed_ref, x_ref, b_ref, c_ref, cum_ref, step_ref, local_ref, grown_ref, st_ref = refs[:9]
    xs, bcs, carried, total, low_tri, dts, rows, tail = refs[-8:]
    block = pl.program_id(0)
    state = wbc.shape[1] // 2
    taps = cx.shape[0]

    gains = nin[...].astype(F32)
    gains = jnp.concatenate([gains[i : i + 1] for i in range(gains.shape[0])], axis=1)

    def features(p):
        embedded = mm(p, we[...]).astype(BF16).astype(F32)
        scale = norm_rows(embedded, embedded.shape[-1])
        return (embedded * scale * gains).astype(BF16)

    @pl.when(block == 0)
    def _():
        carried[...] = jnp.zeros_like(carried)
        total[...] = jnp.zeros_like(total)
        tail[...] = halo[...].astype(F32)
        ri = lax.broadcasted_iota(jnp.int32, (SPAN, SPAN), 0)
        ci = lax.broadcasted_iota(jnp.int32, (SPAN, SPAN), 1)
        low_tri[...] = jnp.where(ri >= ci, 1.0, 0.0).astype(BF16)
        dts[...] = jnp.zeros_like(dts)
        rows[...] = jnp.zeros_like(rows)
        rows[0:1, 0:heads] = dtb[...]
        rows[1:2, 0:heads] = -jnp.exp(alog[...])

    here = ((block // per) ^ lax.rem(me_ref[0], reps)) == 0
    span = pats[0].shape[0]
    patch = jnp.where(here, pats[0][...], pats[1][...]).astype(F32)
    joined = features(jnp.concatenate([tail[...], patch], axis=0).astype(BF16))
    tail[...] = patch[span - 8 :]
    normed = joined[8:]
    normed_ref[...] = normed
    dts[:, 0:heads] = lax.dot_general(
        normed, wdt[...], (((1,), (1,)), ((), ())), preferred_element_type=F32
    )
    bcs[...] = mm(joined, wbc[...]).astype(BF16).astype(F32)
    xs[...] = mm(joined, wx[...]).astype(BF16).astype(F32)
    step_all = dts[...] + rows[0:1]
    step_all = jnp.maximum(step_all, 0.0) + jnp.log1p(jnp.exp(-jnp.abs(step_all)))
    step_ref[...] = step_all

    def conv(buffer, kernel, at):
        out = kernel[0:1] * buffer[at + 9 - taps : at + 9 - taps + SPAN]
        for i in range(1, taps):
            out = out + kernel[i : i + 1] * buffer[at + 9 - taps + i : at + 9 - taps + i + SPAN]
        return silu(out)

    for n in range(span // SPAN):
        at = n * SPAN
        step = step_all[at : at + SPAN]
        rated = step * rows[1:2]
        one = rated.astype(BF16).astype(F32)
        two = (rated - one).astype(BF16).astype(F32)
        three = rated - one - two
        packed = one + pltpu.roll(two, heads, 1) + pltpu.roll(three, 2 * heads, 1)
        sums = mm(low_tri[...], packed.astype(BF16))
        cum = sums + pltpu.roll(sums, LANES - heads, 1) + pltpu.roll(sums, LANES - 2 * heads, 1)
        cum_ref[at : at + SPAN] = cum
        last = cum[SPAN - 1 : SPAN]
        weights = expand(jnp.exp(last - cum) * step, spread)
        grow = expand(
            jnp.exp(jnp.concatenate([jnp.broadcast_to(last, (8, LANES)), total[...]], axis=0)), spread
        )
        bc = conv(bcs, cbc, at)
        b_ref[at : at + SPAN] = bc[:, :state].astype(BF16)
        c_ref[at : at + SPAN] = bc[:, state:].astype(BF16)
        bt = bc[:, :state].T.astype(BF16)
        xc = conv(xs, cx, at).astype(BF16)
        x_ref[at : at + SPAN] = xc
        weighted = (xc.astype(F32) * weights).astype(BF16)
        local_ref[n] = carried[...]
        grown_ref[n] = grow[8:16]
        carried[...] = carried[...] * grow[0:1] + mm(bt, weighted)
        total[...] = total[...] + last

    @pl.when(block == pl.num_programs(0) - 1)
    def _():
        st_ref[0:state] = carried[...]
        st_ref[state : state + 8] = grow[8:16] * grow[0:8]
        if final:
            everything = [e[...] for e in earlier] + [st_ref[...]]
            count = len(everything)
            send = refs[9]
            zero = jnp.zeros((state, xs.shape[1]), F32)
            send[0:state] = fold(everything, count, lax.div(me_ref[0], reps), zero).astype(BF16)
            decay = everything[0][state : state + 8]
            for e in everything[1:]:
                decay = decay * e[state : state + 8]
            send[state : state + 8] = decay.astype(BF16)


def run_states(me, pats, halo, consts, heads, inner, state, own, earlier, final):
    rows_in, width = pats[0].shape
    model = consts[0].shape[1]
    tokens = own * len(pats)
    span = min(own, TILE)
    per = own // span
    blocks = tokens // SPAN
    subs = span // SPAN
    row = lambda n: pl.BlockSpec((span, n), lambda b, me: (b, 0))
    fixed = pl.BlockSpec((state + 8, inner), lambda b, me: (0, 0))
    shape = lambda *d, t=F32: jax.ShapeDtypeStruct(d, t)
    return pl.pallas_call(
        functools.partial(block_states, heads, per, len(pats), len(earlier), final),
        grid_spec=pltpu.PrefetchScalarGridSpec(
            num_scalar_prefetch=1,
            grid=(tokens // span,),
            in_specs=[pl.BlockSpec((span, width), lambda b, me: (b % per, 0))] * len(pats)
            + [pl.BlockSpec((8, width), lambda b, me: (own // 8, 0))]
            + [VMEM] * (len(consts) + len(earlier)),
            out_specs=[row(model), row(inner), row(state), row(state), row(LANES), row(LANES),
                       pl.BlockSpec((subs, state, inner), lambda b, me: (b, 0, 0)),
                       pl.BlockSpec((subs, 8, inner), lambda b, me: (b, 0, 0)), fixed]
            + [fixed] * final,
            scratch_shapes=[
                pltpu.VMEM((span + 8, inner), F32),
                pltpu.VMEM((span + 8, 2 * state), F32),
                pltpu.VMEM((state, inner), F32),
                pltpu.VMEM((8, LANES), F32),
                pltpu.VMEM((SPAN, SPAN), BF16),
                pltpu.VMEM((span, LANES), F32),
                pltpu.VMEM((8, LANES), F32),
                pltpu.VMEM((8, width), F32),
            ],
        ),
        out_shape=[
            shape(tokens, model, t=BF16), shape(tokens, inner, t=BF16), shape(tokens, state, t=BF16),
            shape(tokens, state, t=BF16), shape(tokens, LANES), shape(tokens, LANES),
            shape(blocks, state, inner), shape(blocks, 8, inner), shape(state + 8, inner),
        ] + [shape(state + 8, inner, t=BF16)] * final,
        compiler_params=PARAMS,
        cost_estimate=cost(13),
        name="block_states",
    )(me, *pats, halo, *consts, *earlier)


def gate_tokens(normed_ref, wz, gate_ref):
    gate_ref[...] = silu(mm(normed_ref[...], wz[...]).astype(BF16).astype(F32)).astype(BF16)


def run_gate(normed, wz):
    tokens, width = normed.shape
    inner = wz.shape[1]
    span = min(tokens, TILE)
    return pl.pallas_call(
        gate_tokens,
        grid=(tokens // span,),
        in_specs=[pl.BlockSpec((span, width), lambda b: (b, 0)), VMEM],
        out_specs=pl.BlockSpec((span, inner), lambda b: (b, 0)),
        out_shape=jax.ShapeDtypeStruct((tokens, inner), BF16),
        compiler_params=PARAMS,
        cost_estimate=cost(4),
        name="gate_tokens",
    )(normed, wz)


def outputs(
    heads, chip, chips, seqs, reps, which, gated, opening, me_ref, normed_ref, x_ref, b_ref, c_ref, cum_ref, step_ref, local_ref, grown_ref,
    *refs,
):
    if not gated:
        wz, refs = refs[0], refs[1:]
    spread, refs = refs[0], refs[1:]
    if opening:
        ends, earlier, refs = refs[:chips], refs[chips : chips + seqs], refs[chips + seqs :]
        entries, refs = refs[:chips], refs[chips:]
        start = entries[chip]
    else:
        start, refs = refs[0], refs[1:]
    outs, y_acc = refs[:-1], refs[-1]
    state = c_ref.shape[1]
    block = pl.program_id(0)
    per = pl.num_programs(0) // len(which)

    if opening:
        @pl.when(block == 0)
        def _():
            entering = jnp.zeros((state, x_ref.shape[1]), F32)
            for part in reversed(earlier):
                entering = part[0:state].astype(F32) + part[state : state + 1].astype(F32) * entering
            place = lax.div(me_ref[0], reps)
            known = [e[...] for e in ends]
            for c in range(chips):
                entries[c][...] = fold(known, chips - 1, place, entering, place ^ c)

    cum = cum_ref[...]
    log_cum = cum * LOG2E
    back = (log_cum - jnp.log2(step_ref[...])).T
    gram = lax.dot_general(
        c_ref[...], b_ref[...], (((1,), (1,)), ((), ())), preferred_element_type=F32
    )
    if gated:
        gate = normed_ref[...].astype(F32)
    else:
        gate = silu(mm(normed_ref[...], wz[...]).astype(BF16).astype(F32))
    half = SPAN // 2
    ri = lax.broadcasted_iota(jnp.int32, (half, half), 0)
    ci = lax.broadcasted_iota(jnp.int32, (half, half), 1)
    inside = ri >= ci
    head_dim = x_ref.shape[1] // heads
    for h in range(heads):
        cols = slice(h * head_dim, (h + 1) * head_dim)
        upper, lower = log_cum[:half, h : h + 1], log_cum[half:, h : h + 1]
        early, late = back[h : h + 1, :half], back[h : h + 1, half:]
        first = jnp.where(inside, jnp.exp2(upper - early), 0.0) * gram[:half, :half]
        cross = jnp.exp2(lower - early) * gram[half:, :half]
        second = jnp.where(inside, jnp.exp2(lower - late), 0.0) * gram[half:, half:]
        y_acc[:half, cols] = mm(first.astype(BF16), x_ref[:half, cols])
        y_acc[half:, cols] = mm(
            jnp.concatenate([cross.astype(BF16), second.astype(BF16)], axis=1), x_ref[:, cols]
        )
    cm = c_ref[...]
    high, low = split(local_ref[0] + grown_ref[0, 0:1] * start[...])
    added = mm(jnp.concatenate([cm, cm], axis=1), jnp.concatenate([high, low], axis=0))
    value = ((y_acc[...] + expand(jnp.exp(cum), spread) * added) * gate).astype(BF16)
    whole = 0
    for n, r in enumerate(which):
        if chip or not r:
            @pl.when(block // per == n)
            def _(whole=whole):
                outs[whole][pl.ds(pl.multiple_of((block % per) * SPAN, SPAN), SPAN), :] = value
            whole += 1
    for n, r in enumerate(which):
        if not chip and r:
            for i in range(len(outs) - whole):
                @pl.when(block == whole * per + i)
                def _(i=i):
                    outs[whole + i][...] = value
            break


def run_outputs(heads, chip, chips, reps, which, me, gate, xc, bm, cm, cum, step, local, grown, wz, spread, enter, own):
    tokens, inner = xc.shape
    state = cm.shape[1]
    per = own // SPAN
    gated, opening = wz is None, isinstance(enter, tuple)
    ends, earlier = enter if opening else ([], [])
    shapes = []
    for r in which:
        shapes += [(own, inner)] if chip or not r else [(SPAN, inner)] * per
    at = lambda b, me: (lax.rem(me[0], reps) ^ (which[0] + b // per)) * per + b % per
    row = lambda n: pl.BlockSpec((SPAN, n), lambda b, me: (at(b, me), 0))
    block3 = lambda b, me: (at(b, me), 0, 0)
    fixed = lambda shape: pl.BlockSpec(shape, lambda b, me: (0, 0))
    firsts = [(state, inner)] * chips if opening else []
    extra = ([] if gated else [wz]) + [spread] + (list(ends) + list(earlier) if opening else [enter])
    return pl.pallas_call(
        functools.partial(outputs, heads, chip, chips, len(earlier), reps, which, gated, opening),
        grid_spec=pltpu.PrefetchScalarGridSpec(
            num_scalar_prefetch=1,
            grid=(len(which) * per,),
            in_specs=[row(a.shape[1]) for a in (gate, xc, bm, cm, cum, step)]
            + [pl.BlockSpec((1, state, inner), block3), pl.BlockSpec((1, 8, inner), block3)]
            + [VMEM] * len(extra),
            out_specs=[fixed(shape) for shape in firsts + shapes],
            scratch_shapes=[pltpu.VMEM((SPAN, inner), F32)],
        ),
        out_shape=[jax.ShapeDtypeStruct(shape, F32) for shape in firsts]
        + [jax.ShapeDtypeStruct(shape, BF16) for shape in shapes],
        compiler_params=PARAMS,
        cost_estimate=cost(0.05),
        name="outputs",
    )(me, gate, xc, bm, cm, cum, step, local, grown, *extra)


def pick_gains(norm, index, count):
    values = norm[...].astype(F32)
    each = values.shape[0] // count
    gains = None
    for j in range(count):
        row = jnp.concatenate([values[j * each + i : j * each + i + 1] for i in range(each)], axis=1)
        gains = row if gains is None else jnp.where(index == j, row, gains)
    return gains


def mix_most(sizes, share, me_ref, pat_ref, we_ref, *refs):
    (norm, weight, embed_ref, mixed_ref, square_ref), refs = refs[-5:], refs[:-5]
    step = pl.program_id(0)
    parts = []
    for size in sizes:
        parts.append(refs[:size])
        refs = refs[size:]
    count = len(parts)
    whole = lambda n: jnp.concatenate([p[...] for p in parts[n]], axis=0).astype(F32)

    @pl.when(step == 0)
    def _():
        embed_ref[...] = mm(pat_ref[...], we_ref[...]).astype(BF16)
        square = None
        for n in range(count):
            v = whole(n)
            square = v * v if square is None else square + v * v
        square_ref[...] = jnp.broadcast_to(jnp.sum(square, axis=-1, keepdims=True), square_ref.shape)

    gains = pick_gains(norm, me_ref[0] ^ step, share)
    for n in range(count):
        @pl.when(step == n)
        def _(n=n):
            got = mm((whole(n) * gains).astype(BF16), weight[0])
            mixed_ref[...] = got if n == 0 else mixed_ref[...] + got


def mix_last(total, share, me_ref, embed_ref, mixed_ref, square_ref, part_ref, norm, weight, out_ref):
    v = part_ref[...].astype(F32)
    gains = pick_gains(norm, me_ref[0] ^ (share - 1), share)
    got = mm((v * gains).astype(BF16), weight[0])
    square = square_ref[:, 0:1] + jnp.sum(v * v, axis=-1, keepdims=True)
    scale = lax.rsqrt(square * (1.0 / total) + EPSILON)
    out_ref[...] = (embed_ref[...].astype(F32) + scale * (mixed_ref[...] + got)).astype(BF16)


def run_mix(me, patches, we, parts, norm_out, w_out):
    share = len(parts)
    count = share - 1
    parts = [p if isinstance(p, list) else [p] for p in parts]
    sizes = [len(p) for p in parts[:count]]
    most = [v for p in parts[:count] for v in p]
    (final,) = parts[count]
    own, inner = final.shape
    width = w_out.shape[1]
    norms = norm_out.reshape(-1, LANES)
    weights = w_out.reshape(share, inner, width)
    full = pl.BlockSpec((own, width), lambda d, me: (0, 0))
    embed, mixed, square = pl.pallas_call(
        functools.partial(mix_most, sizes, share),
        grid_spec=pltpu.PrefetchScalarGridSpec(
            num_scalar_prefetch=1,
            grid=(count,),
            in_specs=[pl.BlockSpec((own, patches.shape[1]), lambda d, me: (0, 0)), VMEM] + [VMEM] * (len(most) + 1)
            + [pl.BlockSpec((1, inner, width), lambda d, me: (me[0] ^ d, 0, 0))],
            out_specs=[full, full, pl.BlockSpec((own, LANES), lambda d, me: (0, 0))],
        ),
        out_shape=[jax.ShapeDtypeStruct((own, width), BF16), jax.ShapeDtypeStruct((own, width), F32),
                   jax.ShapeDtypeStruct((own, LANES), F32)],
        compiler_params=PARAMS,
        cost_estimate=cost(0.05),
        name="mix_most",
    )(me, patches, we, *most, norms, weights)
    tile = SPAN
    row = lambda n: pl.BlockSpec((tile, n), lambda i, me: (i, 0))
    return pl.pallas_call(
        functools.partial(mix_last, share * inner, share),
        grid_spec=pltpu.PrefetchScalarGridSpec(
            num_scalar_prefetch=1,
            grid=(own // tile,),
            in_specs=[row(width), row(width), row(LANES), row(inner),
                      VMEM, pl.BlockSpec((1, inner, width), lambda i, me: (me[0] ^ count, 0, 0))],
            out_specs=row(width),
        ),
        out_shape=jax.ShapeDtypeStruct((own, width), BF16),
        compiler_params=PARAMS,
        cost_estimate=cost(3),
        name="mix_last",
    )(me, embed, mixed, square, final, norms, weights)


def swap(value, flip):
    count = lax.axis_size(HR)
    return lax.ppermute(value, HR, [(i, i ^ flip) for i in range(count)])


def shift(value, by):
    count = lax.axis_size("seq")
    return lax.ppermute(value, "seq", [(i, i + by) for i in range(count - by)])


def on_device(
    spectrum, src_amp, src_phase, src_mode, src_delay, src_bins, w_embed, norm_in, w_z, w_x, w_bc, w_dt,
    dt_bias, a_log, conv_x, conv_bc, norm_out, w_out,
):
    devices = lax.axis_size(ALL)
    share = lax.axis_size(HR)
    rows_all = spectrum.shape[2] * devices
    length = rows_all * spectrum.shape[3]
    pos = lax.axis_index(ALL).astype(jnp.int32).reshape(1)
    me = lax.axis_index(HR).astype(jnp.int32).reshape(1)
    first = run_first(
        spectrum, src_amp, src_phase, src_mode, src_delay, src_bins, pos, rows_all, length
    )
    patches = make_patches(first, length)
    own = patches.shape[0] - 8
    reps, chips = lax.axis_size("rep"), lax.axis_size("head")
    heads, inner, state = dt_bias.shape[0], w_x.shape[1], w_bc.shape[1] // 2
    spread = np.zeros((2 * LANES, inner), ml_dtypes.bfloat16)
    for h in range(heads):
        spread[h, h * (inner // heads) : (h + 1) * (inner // heads)] = 1
    spread[LANES:] = spread[:LANES]
    consts = (
        w_embed, norm_in.reshape(-1, LANES), w_x, w_bc, w_dt.T, dt_bias[None], a_log[None], conv_x, conv_bc,
        jnp.asarray(spread),
    )
    done, ends = [], []
    base = [patches] + [swap(patches, c * reps) for c in range(1, chips)]
    for c in range(chips):
        start = base[c]
        if ends:
            start, ends[-1] = lax.optimization_barrier((start, ends[-1]))
        group = [start] + [swap(start, r) for r in range(1, reps)]
        got = run_states(
            me, group, start, consts, heads, inner, state, own, ends, c == chips - 1
        )
        done.append(got[:8])
        ends.append(got[8])
    send = got[9]
    earlier = [shift(send, d) for d in range(1, lax.axis_size("seq"))]
    parts = [None] * share
    gate = None
    enter = (ends, earlier)
    for c in list(range(1, chips)) + [0]:
        normed, xc, bm, cm, cum, step, local, grown = done[c]
        if gate is not None:
            normed, gate = lax.optimization_barrier((normed, gate))
        ahead = run_gate(normed, w_z) if c == 1 else normed
        values = []
        for which in ([[r] for r in range(reps)] if c else [list(range(reps))]):
            got = run_outputs(
                heads, c, chips, reps, which, me, ahead, xc, bm, cm, cum, step, local, grown,
                None if c == 1 else w_z, spread, enter if isinstance(enter, tuple) else enter[c], own,
            )
            if isinstance(enter, tuple):
                enter, got = list(got[:chips]), list(got[chips:])
            values += got
            if c:
                ahead, values[-1] = lax.optimization_barrier((ahead, values[-1]))
        gate = values[-1]
        for r in reversed(range(reps)):
            d = c * reps + r
            if c or not r:
                parts[d] = swap(values[r], d) if d else values[0]
            else:
                per = own // SPAN
                pieces = values[1 + (r - 1) * per : 1 + r * per]
                parts[d] = [swap(v, d) for v in pieces]
    return run_mix(me, patches, w_embed, parts, norm_out, w_out)


def solution(mesh):
    in_specs = (
        P("grp", None, ("seq", "head", "rep"), None),
        P("grp", None),
        P("grp"),
        P("grp"),
        P("grp"),
        P("grp", None),
        P(),
        P(),
        P(None, ("head", "rep")),
        P(None, ("head", "rep")),
        P(),
        P(None, ("head", "rep")),
        P(("head", "rep")),
        P(("head", "rep")),
        P(None, ("head", "rep")),
        P(),
        P(),
        P(),
    )
    out_specs = P(("grp", "seq", "head", "rep"), None)
    return jax.shard_map(
        on_device, mesh=mesh, in_specs=in_specs, out_specs=out_specs, check_vma=False
    )
```

```python
import functools
import math

import jax
import jax.numpy as jnp
import ml_dtypes
import numpy as np
from jax import lax
from jax.experimental import pallas as pl
from jax.experimental.pallas import tpu as pltpu
from jax.sharding import PartitionSpec as P

SPAN = 256
LOG2E = math.log2(math.e)
TILE = 512
EPSILON = 1e-05
LANES = 128
PATCH = 64
ALL = ("seq", "head", "rep")
HR = ("head", "rep")
F32 = jnp.float32
BF16 = jnp.bfloat16
VMEM = pl.BlockSpec(memory_space=pltpu.VMEM)
SMEM = pl.BlockSpec(memory_space=pltpu.SMEM)


def cost(micros):
    return pl.CostEstimate(
        flops=int(micros * 1e9), transcendentals=0, bytes_accessed=int(micros * 3e6)
    )


PARAMS = pltpu.CompilerParams(vmem_limit_bytes=56 * 1024 * 1024)


def two_halves(table):
    high = table.astype(ml_dtypes.bfloat16)
    return high, (table - high.astype(np.float64)).astype(ml_dtypes.bfloat16)


def mm(a, b):
    return jnp.dot(a, b, preferred_element_type=F32)


def split(a):
    high = a.astype(BF16)
    return high, (a - high.astype(F32)).astype(BF16)


def lane_bins(inner):
    parts = PATCH // inner
    lane = np.arange(LANES)
    width = LANES // parts
    return lane // width + parts * (lane % width)


def inverse_fft(real, imag):
    count = len(real)
    if count == 1:
        return real, imag
    even_r, even_i = inverse_fft(real[0::2], imag[0::2])
    odd_r, odd_i = inverse_fft(real[1::2], imag[1::2])
    half = count // 2
    out_r, out_i = [None] * count, [None] * count
    for k in range(half):
        angle = 2.0 * math.pi * k / count
        c, s = math.cos(angle), math.sin(angle)
        if k == 0:
            r, i = odd_r[k], odd_i[k]
        elif 4 * k == count:
            r, i = -odd_i[k], odd_r[k]
        else:
            r = odd_r[k] * c - odd_i[k] * s
            i = odd_r[k] * s + odd_i[k] * c
        out_r[k], out_i[k] = even_r[k] + r, even_i[k] + i
        out_r[k + half], out_i[k + half] = even_r[k] - r, even_i[k] - i
    return out_r, out_i


def first_section(
    rows_all, length, pos, amp, phase, mode, delay, bins, turn_ref, x_ref, twist_ref, near_ref, high_ref, low_ref,
    out_ref, base, acc, lhs,
):
    channels = x_ref.shape[1]
    sources = phase.shape[0]
    inner = x_ref.shape[2]
    row_block = x_ref.shape[3]
    shape = (row_block, LANES)
    row = pos[0] * row_block + lax.broadcasted_iota(jnp.int32, shape, 0)
    lane = lax.broadcasted_iota(jnp.int32, shape, 1)
    first_bin = row + rows_all * lane
    unit = 2.0 * math.pi / length

    group = math.gcd(sources, 4)

    def make_base(g, _):
        for n in range(group):
            s = g * group + n
            turn = ((((first_bin * delay[s]) & (length - 1)) * mode[s]) & (length - 1)).astype(F32)
            angle = mode[s].astype(F32) * phase[s] + turn * unit
            base[pl.ds(pl.multiple_of(s * row_block, row_block), row_block), :] = jnp.cos(angle)
            base[pl.ds(pl.multiple_of((sources + s) * row_block, row_block), row_block), :] = jnp.sin(angle)
        return 0

    lax.fori_loop(0, sources // group, make_base, 0)

    width = rows_all * LANES
    high_bits = lax.broadcasted_iota(jnp.int32, (inner, LANES), 0)
    place = lax.broadcasted_iota(jnp.int32, (1, LANES), 1)

    def spread_out(value, kind):
        out = jnp.zeros((1, LANES), kind)
        for s in range(sources):
            out = jnp.where(place == s, value(s), out)
        return out

    lag = spread_out(lambda s: delay[s] * mode[s], jnp.int32)
    low_end = spread_out(lambda s: bins[0, s], jnp.int32)
    high_end = spread_out(lambda s: bins[1, s], jnp.int32)
    step_angle = ((lag * high_bits) & (inner - 1)).astype(F32) * (2.0 * math.pi / inner)
    known = lax.broadcasted_iota(jnp.int32, (inner, LANES), 1) < sources
    full = known & (low_end <= high_bits * width) & (high_end >= (high_bits + 1) * width)
    step_cos = jnp.where(full, jnp.cos(step_angle), 0.0)
    step_sin = jnp.where(full, jnp.sin(step_angle), 0.0)
    rows = []
    for r in range(2):
        one, two = (step_cos, -step_sin) if r == 0 else (step_sin, step_cos)
        for c in range(channels):
            gain = spread_out(lambda s: amp[c, s], F32)
            rows.append(gain * one + pltpu.roll(gain * two, sources, 1))
    rows = jnp.concatenate(rows, axis=0)
    top = rows.astype(BF16).astype(F32)
    rest = (rows - top).astype(BF16).astype(F32)
    left = (top + pltpu.roll(top, 2 * sources, 1) + pltpu.roll(rest, 4 * sources, 1)).astype(BF16)
    blank = jnp.zeros((LANES - 6 * sources, LANES), F32)
    for u in range(row_block):
        wave = base[pl.ds(u, 2 * sources, stride=row_block), :]
        top = wave.astype(BF16).astype(F32)
        right = jnp.concatenate([top, wave - top, top, blank], axis=0).astype(BF16)
        acc[pl.ds(u, 2 * channels * inner, stride=row_block), :] = mm(left, right)

    def add_ends(s, _):
        first, past = bins[0, s], bins[1, s]
        at_first, at_past = lax.div(first, width), lax.div(past, width)
        begins = (first > at_first * width) | (past < (at_first + 1) * width)
        ends = (at_past != at_first) & (at_past < inner)
        for at, wanted in ((at_first, begins), (at_past, ends)):
            @pl.when(wanted)
            def _(at=at):
                here = first_bin + width * at
                which = (delay[s] * mode[s] * at) & (inner - 1)
                tr, ti = turn_ref[0, which], turn_ref[1, which]
                inside = (here >= first) & (here < past)
                br = base[pl.ds(pl.multiple_of(s * row_block, row_block), row_block), :]
                bi = base[pl.ds(pl.multiple_of((sources + s) * row_block, row_block), row_block), :]
                real = jnp.where(inside, br * tr - bi * ti, 0.0)
                imag = jnp.where(inside, br * ti + bi * tr, 0.0)
                for c in range(channels):
                    for n, part in ((c, real), (channels + c, imag)):
                        slot = pl.ds(pl.multiple_of((n * inner + at) * row_block, row_block), row_block)
                        acc[slot, :] = acc[slot, :] + amp[c, s] * part
        return 0

    lax.fori_loop(0, sources, add_ends, 0)

    def total(r, c, v):
        slot = pl.multiple_of(((r * channels + c) * inner + v) * row_block, row_block)
        return x_ref[r, c, v] + acc[pl.ds(slot, row_block), :]

    def transform(c, _):
        real, imag = inverse_fft(
            [total(0, c, v) for v in range(inner)], [total(1, c, v) for v in range(inner)]
        )
        for q in range(inner):
            tc, ts = twist_ref[0, q : q + 1, :], twist_ref[1, q : q + 1, :]
            lhs[c, q, :, 0:LANES] = real[q] * tc - imag[q] * ts
            lhs[c, q, :, LANES : 2 * LANES] = real[q] * ts + imag[q] * tc
        return 0

    lax.fori_loop(0, channels, transform, 0)

    wide = (inner, row_block, LANES)
    parts = PATCH // inner
    width = LANES // parts
    flat = (inner, LANES)
    lanes = lax.broadcasted_iota(jnp.int32, flat, 1)
    outer = lax.div(lanes, width) + parts * lax.rem(lanes, width)
    column = lax.broadcasted_iota(jnp.int32, flat, 0) + inner * outer
    angle = ((pos[0] * row_block * column) & (length - 1)).astype(F32) * unit
    turn_cos, turn_sin = jnp.cos(angle)[:, None, :], jnp.sin(angle)[:, None, :]
    near_cos, near_sin = near_ref[0], near_ref[1]
    cos = turn_cos * near_cos - turn_sin * near_sin
    sin = turn_sin * near_cos + turn_cos * near_sin
    for c in range(channels):
        high, low = split(lhs[c].reshape(inner * row_block, 2 * LANES))
        got = mm(high, high_ref[...]) + mm(low, high_ref[...]) + mm(high, low_ref[...])
        real = got[:, 0:LANES].reshape(wide)
        imag = got[:, LANES : 2 * LANES].reshape(wide)
        out_ref[:, c] = (real * cos - imag * sin).astype(BF16)
        out_ref[:, channels + c] = (real * sin + imag * cos).astype(BF16)


def run_first(spectrum, amp, phase, mode, delay, bins, pos, rows_all, length):
    _, channels, row_block, columns = spectrum.shape
    inner = columns // LANES
    grid_in = spectrum.reshape(2, channels, row_block, inner, LANES).transpose(0, 1, 3, 2, 4)
    steps = np.arange(inner)
    turn = 2.0 * np.pi * steps / inner
    turns = np.stack([np.cos(turn), np.sin(turn)]).astype(np.float32)
    lane = np.arange(LANES)
    twist = 2.0 * np.pi * (steps[:, None] * lane[None, :] % columns) / columns
    twists = np.stack([np.cos(twist), np.sin(twist)]).astype(np.float32)
    column = steps[:, None] + inner * lane_bins(inner)[None, :]
    near = 2.0 * np.pi * np.arange(row_block)[None, :, None] * column[:, None, :] / length
    nears = np.stack([np.cos(near), np.sin(near)]).astype(np.float32)
    angle = 2.0 * np.pi * (lane[:, None] * lane_bins(inner)[None, :] % LANES) / LANES
    cos, sin = np.cos(angle), np.sin(angle)
    high, low = two_halves(np.block([[cos, sin], [-sin, cos]]))
    return pl.pallas_call(
        functools.partial(first_section, rows_all, length),
        out_shape=jax.ShapeDtypeStruct((inner, 2 * channels, row_block, LANES), BF16),
        in_specs=[SMEM] * 7 + [VMEM] * 5,
        out_specs=VMEM,
        scratch_shapes=[
            pltpu.VMEM((2 * amp.shape[0] * row_block, LANES), F32),
            pltpu.VMEM((2 * channels * inner * row_block, LANES), F32),
            pltpu.VMEM((channels, inner, row_block, 2 * LANES), F32),
        ],
        compiler_params=PARAMS,
        cost_estimate=cost(7),
        name="first_section",
    )(pos, amp.T, phase, mode, delay, bins.T, turns, grid_in, twists, nears, high, low)


def second_section(reps, z_ref, high_ref, low_ref, out_ref):
    devices, own, pairs, row_block, _ = z_ref.shape
    channels = pairs // 2
    rows = devices * row_block
    tiles = own * pairs
    half = (tiles + 1) // 2
    lane = lax.broadcasted_iota(jnp.int32, (rows, LANES), 1)
    sub = lax.rem(lax.broadcasted_iota(jnp.int32, (rows, LANES), 0), row_block)
    upper = (lane & 32) != 0
    rim = jnp.zeros((rows, LANES), F32)
    for q in range(own):
        for c in range(channels):
            right = jnp.concatenate(
                [z_ref[:, q, r * channels + c].astype(F32).reshape(rows, LANES) for r in range(2)], axis=0
            ).astype(BF16)
            got = mm(high_ref[...], right) + mm(low_ref[...], right)
            for r in range(2):
                tile = q * pairs + r * channels + c
                part = got[r * rows : (r + 1) * rows]
                out_ref[:, tile] = part.reshape(devices, row_block, LANES).astype(BF16)
                ends = jnp.broadcast_to(
                    part.reshape(devices, row_block, LANES)[:, row_block - 1 :, :],
                    (devices, row_block, LANES),
                ).reshape(rows, LANES)
                if tile < half:
                    rim = jnp.where(upper & (sub == tile), ends, rim)
                else:
                    ends = pltpu.roll(ends, LANES - 32, 1)
                    rim = jnp.where(jnp.logical_not(upper) & (sub == tile - half), ends, rim)
    rim = rim.reshape(devices, row_block, LANES).astype(BF16)
    for d in range(devices):
        source = d - d % reps - 1
        out_ref[d, tiles] = rim[source] if source >= 0 else jnp.zeros((row_block, LANES), BF16)


def run_second(z, length):
    devices, own, pairs, row_block, _ = z.shape
    rows = devices * row_block
    counter = np.arange(rows)
    angle = 2.0 * np.pi * (counter[:, None] * counter[None, :] % rows) / rows
    cos, sin = np.cos(angle), np.sin(angle)
    high, low = two_halves(np.block([[cos, -sin], [sin, cos]]) / math.sqrt(length))
    return pl.pallas_call(
        functools.partial(second_section, lax.axis_size("rep")),
        out_shape=jax.ShapeDtypeStruct((devices, own * pairs + 1, row_block, LANES), BF16),
        in_specs=[VMEM] * 3,
        out_specs=VMEM,
        compiler_params=PARAMS,
        cost_estimate=cost(3),
        name="second_section",
    )(z, high, low)


def order_patches(x_ref, perm_ref, rim_ref, out_ref, wide):
    devices, tiles, row_block, _ = x_ref.shape
    parts = perm_ref.shape[0]
    width = LANES // parts
    half = tiles // 2
    wide[...] = x_ref[...].astype(F32).reshape(devices * tiles * row_block, LANES)
    for m in range(row_block):
        rows = wide[pl.ds(m, devices * tiles, stride=row_block), :]
        across = rows.T.astype(BF16)
        total = mm(across[0:width], perm_ref[0])
        for n in range(1, parts):
            total = total + mm(across[n * width : (n + 1) * width], perm_ref[n])
        out_ref[m * width : (m + 1) * width, :] = total.astype(BF16)
    rows = jnp.concatenate(
        [wide[pl.ds((tiles - 1) * row_block + n, devices, stride=tiles * row_block), :] for n in range(half)],
        axis=0,
    )
    across = jnp.concatenate([rows, pltpu.roll(rows, 32, 1)], axis=0).T.astype(BF16)
    total = mm(across[width - 8 : width], rim_ref[0])
    for n in range(1, parts):
        total = total + mm(across[(n + 1) * width - 8 : (n + 1) * width], rim_ref[n])
    out_ref[row_block * width :, :] = total.astype(BF16)


def run_order(x, inner, channels):
    devices, tiles, row_block, _ = x.shape
    parts = PATCH // inner
    own = tiles - 1
    pairs = 2 * channels
    each = own // pairs
    perm = np.zeros((parts, devices * tiles, pairs * PATCH), ml_dtypes.bfloat16)
    rim = np.zeros((parts, own * devices, pairs * PATCH), ml_dtypes.bfloat16)
    for n in range(parts):
        for j in range(devices):
            for q in range(each):
                for rc in range(pairs):
                    to = rc * PATCH + n * inner + j * each + q
                    perm[n, j * tiles + q * pairs + rc, to] = 1
                    rim[n, (q * pairs + rc) * devices + j, to] = 1
    return pl.pallas_call(
        order_patches,
        out_shape=jax.ShapeDtypeStruct((row_block * LANES // parts + 8, pairs * PATCH), BF16),
        in_specs=[VMEM] * 3,
        out_specs=VMEM,
        scratch_shapes=[pltpu.VMEM((devices * tiles * row_block, LANES), F32)],
        compiler_params=PARAMS,
        cost_estimate=cost(3),
        name="order_patches",
    )(x, perm, rim)


def dft_table(order):
    counter = jnp.arange(order, dtype=jnp.int32)
    turn_count = counter[:, None] * counter[None, :] % order
    radians = turn_count.astype(F32) * (2.0 * math.pi / order)
    return jnp.stack([jnp.cos(radians), jnp.sin(radians)])


def make_patches(first, length):
    devices = lax.axis_size(ALL)
    inner, pairs, row_block, _ = first.shape
    channels = pairs // 2
    if inner % devices == 0 and 2 * inner == PATCH and inner // devices * pairs in range(2, 17, 2):
        own = inner // devices
        moved = lax.all_to_all(
            first.reshape(devices, own, pairs, row_block, LANES), ALL, 0, 0, tiled=True
        )
        moved = lax.all_to_all(run_second(moved, length), ALL, 0, 0, tiled=True)
        return run_order(moved, inner, channels)
    flat = first.transpose(1, 2, 0, 3).reshape(2, channels, row_block, inner * LANES)
    flat = lax.all_to_all(flat, ALL, split_axis=3, concat_axis=2, tiled=True).astype(F32)
    mixed = jnp.einsum(
        "rcuq,kum->krcqm", flat, dft_table(row_block * devices), precision=lax.Precision.HIGHEST
    )
    series = jnp.stack([mixed[0, 0] - mixed[1, 1], mixed[1, 0] + mixed[0, 1]])
    series = (series * (1.0 / math.sqrt(length))).astype(BF16)
    series = lax.all_to_all(series, ALL, split_axis=4 - 1, concat_axis=2, tiled=True)
    parts = PATCH // inner
    series = series.reshape(2, channels, inner, parts, LANES // parts, row_block)
    patches = series.transpose(5, 4, 0, 1, 3, 2).reshape(
        row_block * LANES // parts, 2 * channels * PATCH
    )
    reps = lax.axis_size("rep")
    tail = patches[patches.shape[0] - 8 :]
    rim = jnp.zeros_like(tail)
    for r in range(reps):
        pairs = [(i - 1, i + r) for i in range(reps, devices, reps)]
        rim = rim + lax.ppermute(tail, ALL, pairs)
    return jnp.concatenate([patches, rim], 0)


def norm_rows(values, total):
    return lax.rsqrt(jnp.sum(values * values, axis=-1, keepdims=True) * (1.0 / total) + EPSILON)


def silu(values):
    half = 0.5 * values
    return half + half * jnp.tanh(half)


def fold(ends, count, head, entering, upto=None):
    state = entering.shape[0]
    for i in range(count):
        part, decay = ends[0][0:state], ends[0][state : state + 1]
        for j in range(1, len(ends)):
            here = (head ^ i) == j
            part = jnp.where(here, ends[j][0:state], part)
            decay = jnp.where(here, ends[j][state : state + 1], decay)
        after = decay * entering + part
        entering = after if upto is None else jnp.where(i < upto, after, entering)
    return entering


def expand(values, spread):
    high, low = split(values)
    return mm(jnp.concatenate([high, low], axis=1), spread[...])


def block_states(heads, per, reps, before, final, me_ref, *refs):
    pats, refs = refs[:2], refs[2:]
    halo, we, nin, wx, wbc, wdt, dtb, alog, cx, cbc, spread = refs[:11]
    earlier, refs = refs[11 : 11 + before], refs[11 + before :]
    normed_ref, x_ref, b_ref, c_ref, cum_ref, step_ref, local_ref, grown_ref, st_ref = refs[:9]
    xs, bcs, carried, total, low_tri, dts, rows, tail = refs[-8:]
    block = pl.program_id(0)
    state = wbc.shape[1] // 2
    taps = cx.shape[0]

    gains = nin[...].astype(F32)
    gains = jnp.concatenate([gains[i : i + 1] for i in range(gains.shape[0])], axis=1)

    def features(p):
        embedded = mm(p, we[...]).astype(BF16).astype(F32)
        scale = norm_rows(embedded, embedded.shape[-1])
        return (embedded * scale * gains).astype(BF16)

    @pl.when(block == 0)
    def _():
        carried[...] = jnp.zeros_like(carried)
        total[...] = jnp.zeros_like(total)
        tail[...] = jnp.zeros_like(tail)
        tail[8:16] = halo[...].astype(F32)
        ri = lax.broadcasted_iota(jnp.int32, (SPAN, SPAN), 0)
        ci = lax.broadcasted_iota(jnp.int32, (SPAN, SPAN), 1)
        low_tri[...] = jnp.where(ri >= ci, 1.0, 0.0).astype(BF16)
        dts[...] = jnp.zeros_like(dts)
        rows[...] = jnp.zeros_like(rows)
        rows[0:1, 0:heads] = dtb[...]
        rows[1:2, 0:heads] = -jnp.exp(alog[...])

    here = ((block // per) ^ lax.rem(me_ref[0], reps)) == 0
    span = pats[0].shape[0]
    patch = jnp.where(here, pats[0][...], pats[1][...]).astype(F32)
    joined = features(jnp.concatenate([tail[...], patch], axis=0).astype(BF16))
    tail[...] = patch[span - 16 :]
    normed = joined[16:]
    normed_ref[...] = normed
    dts[:, 0:heads] = lax.dot_general(
        normed, wdt[...], (((1,), (1,)), ((), ())), preferred_element_type=F32
    )
    bcs[...] = mm(joined, wbc[...]).astype(BF16).astype(F32)
    xs[...] = mm(joined, wx[...]).astype(BF16).astype(F32)
    step_all = dts[...] + rows[0:1]
    step_all = jnp.maximum(step_all, 0.0) + jnp.log1p(jnp.exp(-jnp.abs(step_all)))
    step_ref[...] = step_all

    def conv(buffer, kernel, at):
        out = kernel[0:1] * buffer[at + 17 - taps : at + 17 - taps + SPAN]
        for i in range(1, taps):
            out = out + kernel[i : i + 1] * buffer[at + 17 - taps + i : at + 17 - taps + i + SPAN]
        return silu(out)

    for n in range(span // SPAN):
        at = n * SPAN
        step = step_all[at : at + SPAN]
        rated = step * rows[1:2]
        one = rated.astype(BF16).astype(F32)
        two = (rated - one).astype(BF16).astype(F32)
        three = rated - one - two
        packed = one + pltpu.roll(two, heads, 1) + pltpu.roll(three, 2 * heads, 1)
        sums = mm(low_tri[...], packed.astype(BF16))
        cum = sums + pltpu.roll(sums, LANES - heads, 1) + pltpu.roll(sums, LANES - 2 * heads, 1)
        cum_ref[at : at + SPAN] = cum
        last = cum[SPAN - 1 : SPAN]
        weights = expand(jnp.exp(last - cum) * step, spread)
        grow = expand(
            jnp.exp(jnp.concatenate([jnp.broadcast_to(last, (8, LANES)), total[...]], axis=0)), spread
        )
        bc = conv(bcs, cbc, at)
        b_ref[at : at + SPAN] = bc[:, :state].astype(BF16)
        c_ref[at : at + SPAN] = bc[:, state:].astype(BF16)
        bt = bc[:, :state].T.astype(BF16)
        xc = conv(xs, cx, at).astype(BF16)
        x_ref[at : at + SPAN] = xc
        weighted = (xc.astype(F32) * weights).astype(BF16)
        local_ref[n] = carried[...]
        grown_ref[n] = grow[8:16]
        carried[...] = carried[...] * grow[0:1] + mm(bt, weighted)
        total[...] = total[...] + last

    @pl.when(block == pl.num_programs(0) - 1)
    def _():
        st_ref[0:state] = carried[...]
        st_ref[state : state + 8] = grow[8:16] * grow[0:8]
        if final:
            everything = [e[...] for e in earlier] + [st_ref[...]]
            count = len(everything)
            send = refs[9]
            zero = jnp.zeros((state, xs.shape[1]), F32)
            send[0:state] = fold(everything, count, lax.div(me_ref[0], reps), zero).astype(BF16)
            decay = everything[0][state : state + 8]
            for e in everything[1:]:
                decay = decay * e[state : state + 8]
            send[state : state + 8] = decay.astype(BF16)


def run_states(me, pats, halo, consts, heads, inner, state, own, earlier, final):
    rows_in, width = pats[0].shape
    model = consts[0].shape[1]
    tokens = own * len(pats)
    span = min(own, TILE)
    per = own // span
    blocks = tokens // SPAN
    subs = span // SPAN
    row = lambda n: pl.BlockSpec((span, n), lambda b, me: (b, 0))
    fixed = pl.BlockSpec((state + 8, inner), lambda b, me: (0, 0))
    shape = lambda *d, t=F32: jax.ShapeDtypeStruct(d, t)
    return pl.pallas_call(
        functools.partial(block_states, heads, per, len(pats), len(earlier), final),
        grid_spec=pltpu.PrefetchScalarGridSpec(
            num_scalar_prefetch=1,
            grid=(tokens // span,),
            in_specs=[pl.BlockSpec((span, width), lambda b, me: (b % per, 0))] * len(pats)
            + [pl.BlockSpec((8, width), lambda b, me: (own // 8, 0))]
            + [VMEM] * (len(consts) + len(earlier)),
            out_specs=[row(model), row(inner), row(state), row(state), row(LANES), row(LANES),
                       pl.BlockSpec((subs, state, inner), lambda b, me: (b, 0, 0)),
                       pl.BlockSpec((subs, 8, inner), lambda b, me: (b, 0, 0)), fixed]
            + [fixed] * final,
            scratch_shapes=[
                pltpu.VMEM((span + 16, inner), F32),
                pltpu.VMEM((span + 16, 2 * state), F32),
                pltpu.VMEM((state, inner), F32),
                pltpu.VMEM((8, LANES), F32),
                pltpu.VMEM((SPAN, SPAN), BF16),
                pltpu.VMEM((span, LANES), F32),
                pltpu.VMEM((8, LANES), F32),
                pltpu.VMEM((16, width), F32),
            ],
        ),
        out_shape=[
            shape(tokens, model, t=BF16), shape(tokens, inner, t=BF16), shape(tokens, state, t=BF16),
            shape(tokens, state, t=BF16), shape(tokens, LANES), shape(tokens, LANES),
            shape(blocks, state, inner), shape(blocks, 8, inner), shape(state + 8, inner),
        ] + [shape(state + 8, inner, t=BF16)] * final,
        compiler_params=PARAMS,
        cost_estimate=cost(13),
        name="block_states",
    )(me, *pats, halo, *consts, *earlier)


def gate_tokens(normed_ref, wz, gate_ref):
    gate_ref[...] = silu(mm(normed_ref[...], wz[...]).astype(BF16).astype(F32)).astype(BF16)


def run_gate(normed, wz):
    tokens, width = normed.shape
    inner = wz.shape[1]
    span = min(tokens, TILE)
    return pl.pallas_call(
        gate_tokens,
        grid=(tokens // span,),
        in_specs=[pl.BlockSpec((span, width), lambda b: (b, 0)), VMEM],
        out_specs=pl.BlockSpec((span, inner), lambda b: (b, 0)),
        out_shape=jax.ShapeDtypeStruct((tokens, inner), BF16),
        compiler_params=PARAMS,
        cost_estimate=cost(4),
        name="gate_tokens",
    )(normed, wz)


def outputs(
    heads, chip, chips, seqs, reps, which, gated, opening, me_ref, normed_ref, x_ref, b_ref, c_ref, cum_ref, step_ref, local_ref, grown_ref,
    *refs,
):
    if not gated:
        wz, refs = refs[0], refs[1:]
    spread, refs = refs[0], refs[1:]
    if opening:
        ends, earlier, refs = refs[:chips], refs[chips : chips + seqs], refs[chips + seqs :]
        entries, refs = refs[:chips], refs[chips:]
        start = entries[chip]
    else:
        start, refs = refs[0], refs[1:]
    outs, y_acc = refs[:-1], refs[-1]
    state = c_ref.shape[1]
    block = pl.program_id(0)
    per = pl.num_programs(0) // len(which)

    if opening:
        @pl.when(block == 0)
        def _():
            entering = jnp.zeros((state, x_ref.shape[1]), F32)
            for part in reversed(earlier):
                entering = part[0:state].astype(F32) + part[state : state + 1].astype(F32) * entering
            place = lax.div(me_ref[0], reps)
            known = [e[...] for e in ends]
            for c in range(chips):
                entries[c][...] = fold(known, chips - 1, place, entering, place ^ c)

    cum = cum_ref[...]
    log_cum = cum * LOG2E
    back = (log_cum - jnp.log2(step_ref[...])).T
    gram = lax.dot_general(
        c_ref[...], b_ref[...], (((1,), (1,)), ((), ())), preferred_element_type=F32
    )
    if gated:
        gate = normed_ref[...].astype(F32)
    else:
        gate = silu(mm(normed_ref[...], wz[...]).astype(BF16).astype(F32))
    half = SPAN // 2
    ri = lax.broadcasted_iota(jnp.int32, (half, half), 0)
    ci = lax.broadcasted_iota(jnp.int32, (half, half), 1)
    inside = ri >= ci
    head_dim = x_ref.shape[1] // heads
    for h in range(heads):
        cols = slice(h * head_dim, (h + 1) * head_dim)
        upper, lower = log_cum[:half, h : h + 1], log_cum[half:, h : h + 1]
        early, late = back[h : h + 1, :half], back[h : h + 1, half:]
        first = jnp.where(inside, jnp.exp2(upper - early), 0.0) * gram[:half, :half]
        cross = jnp.exp2(lower - early) * gram[half:, :half]
        second = jnp.where(inside, jnp.exp2(lower - late), 0.0) * gram[half:, half:]
        y_acc[:half, cols] = mm(first.astype(BF16), x_ref[:half, cols])
        y_acc[half:, cols] = mm(
            jnp.concatenate([cross.astype(BF16), second.astype(BF16)], axis=1), x_ref[:, cols]
        )
    cm = c_ref[...]
    high, low = split(local_ref[0] + grown_ref[0, 0:1] * start[...])
    added = mm(jnp.concatenate([cm, cm], axis=1), jnp.concatenate([high, low], axis=0))
    value = ((y_acc[...] + expand(jnp.exp(cum), spread) * added) * gate).astype(BF16)
    whole = 0
    for n, r in enumerate(which):
        if chip or not r:
            @pl.when(block // per == n)
            def _(whole=whole):
                outs[whole][pl.ds(pl.multiple_of((block % per) * SPAN, SPAN), SPAN), :] = value
            whole += 1
    for n, r in enumerate(which):
        if not chip and r:
            for i in range(len(outs) - whole):
                @pl.when(block == whole * per + i)
                def _(i=i):
                    outs[whole + i][...] = value
            break


def run_outputs(heads, chip, chips, reps, which, me, gate, xc, bm, cm, cum, step, local, grown, wz, spread, enter, own):
    tokens, inner = xc.shape
    state = cm.shape[1]
    per = own // SPAN
    gated, opening = wz is None, isinstance(enter, tuple)
    ends, earlier = enter if opening else ([], [])
    shapes = []
    for r in which:
        shapes += [(own, inner)] if chip or not r else [(SPAN, inner)] * per
    at = lambda b, me: (lax.rem(me[0], reps) ^ (which[0] + b // per)) * per + b % per
    row = lambda n: pl.BlockSpec((SPAN, n), lambda b, me: (at(b, me), 0))
    block3 = lambda b, me: (at(b, me), 0, 0)
    fixed = lambda shape: pl.BlockSpec(shape, lambda b, me: (0, 0))
    firsts = [(state, inner)] * chips if opening else []
    extra = ([] if gated else [wz]) + [spread] + (list(ends) + list(earlier) if opening else [enter])
    return pl.pallas_call(
        functools.partial(outputs, heads, chip, chips, len(earlier), reps, which, gated, opening),
        grid_spec=pltpu.PrefetchScalarGridSpec(
            num_scalar_prefetch=1,
            grid=(len(which) * per,),
            in_specs=[row(a.shape[1]) for a in (gate, xc, bm, cm, cum, step)]
            + [pl.BlockSpec((1, state, inner), block3), pl.BlockSpec((1, 8, inner), block3)]
            + [VMEM] * len(extra),
            out_specs=[fixed(shape) for shape in firsts + shapes],
            scratch_shapes=[pltpu.VMEM((SPAN, inner), F32)],
        ),
        out_shape=[jax.ShapeDtypeStruct(shape, F32) for shape in firsts]
        + [jax.ShapeDtypeStruct(shape, BF16) for shape in shapes],
        compiler_params=PARAMS,
        cost_estimate=cost(0.05),
        name="outputs",
    )(me, gate, xc, bm, cm, cum, step, local, grown, *extra)


def pick_gains(norm, index, count):
    values = norm[...].astype(F32)
    each = values.shape[0] // count
    gains = None
    for j in range(count):
        row = jnp.concatenate([values[j * each + i : j * each + i + 1] for i in range(each)], axis=1)
        gains = row if gains is None else jnp.where(index == j, row, gains)
    return gains


def mix_most(sizes, share, me_ref, pat_ref, we_ref, *refs):
    (norm, weight, embed_ref, mixed_ref, square_ref), refs = refs[-5:], refs[:-5]
    step = pl.program_id(0)
    parts = []
    for size in sizes:
        parts.append(refs[:size])
        refs = refs[size:]
    count = len(parts)
    whole = lambda n: jnp.concatenate([p[...] for p in parts[n]], axis=0).astype(F32)

    @pl.when(step == 0)
    def _():
        embed_ref[...] = mm(pat_ref[...], we_ref[...]).astype(BF16)
        square = None
        for n in range(count):
            v = whole(n)
            square = v * v if square is None else square + v * v
        square_ref[...] = jnp.broadcast_to(jnp.sum(square, axis=-1, keepdims=True), square_ref.shape)

    gains = pick_gains(norm, me_ref[0] ^ step, share)
    for n in range(count):
        @pl.when(step == n)
        def _(n=n):
            got = mm((whole(n) * gains).astype(BF16), weight[0])
            mixed_ref[...] = got if n == 0 else mixed_ref[...] + got


def mix_last(total, share, me_ref, embed_ref, mixed_ref, square_ref, part_ref, norm, weight, out_ref):
    v = part_ref[...].astype(F32)
    gains = pick_gains(norm, me_ref[0] ^ (share - 1), share)
    got = mm((v * gains).astype(BF16), weight[0])
    square = square_ref[:, 0:1] + jnp.sum(v * v, axis=-1, keepdims=True)
    scale = lax.rsqrt(square * (1.0 / total) + EPSILON)
    out_ref[...] = (embed_ref[...].astype(F32) + scale * (mixed_ref[...] + got)).astype(BF16)


def run_mix(me, patches, we, parts, norm_out, w_out):
    share = len(parts)
    count = share - 1
    parts = [p if isinstance(p, list) else [p] for p in parts]
    sizes = [len(p) for p in parts[:count]]
    most = [v for p in parts[:count] for v in p]
    (final,) = parts[count]
    own, inner = final.shape
    width = w_out.shape[1]
    norms = norm_out.reshape(-1, LANES)
    weights = w_out.reshape(share, inner, width)
    full = pl.BlockSpec((own, width), lambda d, me: (0, 0))
    embed, mixed, square = pl.pallas_call(
        functools.partial(mix_most, sizes, share),
        grid_spec=pltpu.PrefetchScalarGridSpec(
            num_scalar_prefetch=1,
            grid=(count,),
            in_specs=[pl.BlockSpec((own, patches.shape[1]), lambda d, me: (0, 0)), VMEM] + [VMEM] * (len(most) + 1)
            + [pl.BlockSpec((1, inner, width), lambda d, me: (me[0] ^ d, 0, 0))],
            out_specs=[full, full, pl.BlockSpec((own, LANES), lambda d, me: (0, 0))],
        ),
        out_shape=[jax.ShapeDtypeStruct((own, width), BF16), jax.ShapeDtypeStruct((own, width), F32),
                   jax.ShapeDtypeStruct((own, LANES), F32)],
        compiler_params=PARAMS,
        cost_estimate=cost(0.05),
        name="mix_most",
    )(me, patches, we, *most, norms, weights)
    tile = SPAN
    row = lambda n: pl.BlockSpec((tile, n), lambda i, me: (i, 0))
    return pl.pallas_call(
        functools.partial(mix_last, share * inner, share),
        grid_spec=pltpu.PrefetchScalarGridSpec(
            num_scalar_prefetch=1,
            grid=(own // tile,),
            in_specs=[row(width), row(width), row(LANES), row(inner),
                      VMEM, pl.BlockSpec((1, inner, width), lambda i, me: (me[0] ^ count, 0, 0))],
            out_specs=row(width),
        ),
        out_shape=jax.ShapeDtypeStruct((own, width), BF16),
        compiler_params=PARAMS,
        cost_estimate=cost(3),
        name="mix_last",
    )(me, embed, mixed, square, final, norms, weights)


def swap(value, flip):
    count = lax.axis_size(HR)
    return lax.ppermute(value, HR, [(i, i ^ flip) for i in range(count)])


def shift(value, by):
    count = lax.axis_size("seq")
    return lax.ppermute(value, "seq", [(i, i + by) for i in range(count - by)])


def on_device(
    spectrum, src_amp, src_phase, src_mode, src_delay, src_bins, w_embed, norm_in, w_z, w_x, w_bc, w_dt,
    dt_bias, a_log, conv_x, conv_bc, norm_out, w_out,
):
    devices = lax.axis_size(ALL)
    share = lax.axis_size(HR)
    rows_all = spectrum.shape[2] * devices
    length = rows_all * spectrum.shape[3]
    pos = lax.axis_index(ALL).astype(jnp.int32).reshape(1)
    me = lax.axis_index(HR).astype(jnp.int32).reshape(1)
    first = run_first(
        spectrum, src_amp, src_phase, src_mode, src_delay, src_bins, pos, rows_all, length
    )
    patches = make_patches(first, length)
    own = patches.shape[0] - 8
    reps, chips = lax.axis_size("rep"), lax.axis_size("head")
    heads, inner, state = dt_bias.shape[0], w_x.shape[1], w_bc.shape[1] // 2
    spread = np.zeros((2 * LANES, inner), ml_dtypes.bfloat16)
    for h in range(heads):
        spread[h, h * (inner // heads) : (h + 1) * (inner // heads)] = 1
    spread[LANES:] = spread[:LANES]
    consts = (
        w_embed, norm_in.reshape(-1, LANES), w_x, w_bc, w_dt.T, dt_bias[None], a_log[None], conv_x, conv_bc,
        jnp.asarray(spread),
    )
    done, ends = [], []
    base = [patches] + [swap(patches, c * reps) for c in range(1, chips)]
    for c in range(chips):
        start = base[c]
        if ends:
            start, ends[-1] = lax.optimization_barrier((start, ends[-1]))
        group = [start] + [swap(start, r) for r in range(1, reps)]
        got = run_states(
            me, group, start, consts, heads, inner, state, own, ends, c == chips - 1
        )
        done.append(got[:8])
        ends.append(got[8])
    send = got[9]
    earlier = [shift(send, d) for d in range(1, lax.axis_size("seq"))]
    parts = [None] * share
    gate = None
    enter = (ends, earlier)
    for c in list(range(1, chips)) + [0]:
        normed, xc, bm, cm, cum, step, local, grown = done[c]
        if gate is not None:
            normed, gate = lax.optimization_barrier((normed, gate))
        ahead = run_gate(normed, w_z) if c == 1 else normed
        values = []
        for which in ([[r] for r in range(reps)] if c else [list(range(reps))]):
            got = run_outputs(
                heads, c, chips, reps, which, me, ahead, xc, bm, cm, cum, step, local, grown,
                None if c == 1 else w_z, spread, enter if isinstance(enter, tuple) else enter[c], own,
            )
            if isinstance(enter, tuple):
                enter, got = list(got[:chips]), list(got[chips:])
            values += got
            if c:
                ahead, values[-1] = lax.optimization_barrier((ahead, values[-1]))
        gate = values[-1]
        for r in reversed(range(reps)):
            d = c * reps + r
            if c or not r:
                parts[d] = swap(values[r], d) if d else values[0]
            else:
                per = own // SPAN
                pieces = values[1 + (r - 1) * per : 1 + r * per]
                parts[d] = [swap(v, d) for v in pieces]
    return run_mix(me, patches, w_embed, parts, norm_out, w_out)


def solution(mesh):
    in_specs = (
        P("grp", None, ("seq", "head", "rep"), None),
        P("grp", None),
        P("grp"),
        P("grp"),
        P("grp"),
        P("grp", None),
        P(),
        P(),
        P(None, ("head", "rep")),
        P(None, ("head", "rep")),
        P(),
        P(None, ("head", "rep")),
        P(("head", "rep")),
        P(("head", "rep")),
        P(None, ("head", "rep")),
        P(),
        P(),
        P(),
    )
    out_specs = P(("grp", "seq", "head", "rep"), None)
    return jax.shard_map(
        on_device, mesh=mesh, in_specs=in_specs, out_specs=out_specs, check_vma=False
    )
```

```python
import functools
import math

import jax
import jax.numpy as jnp
import ml_dtypes
import numpy as np
from jax import lax
from jax.experimental import pallas as pl
from jax.experimental.pallas import tpu as pltpu
from jax.sharding import PartitionSpec as P

SPAN = 256
LOG2E = math.log2(math.e)
TILE = 512
EPSILON = 1e-05
LANES = 128
PATCH = 64
ALL = ("seq", "head", "rep")
HR = ("head", "rep")
F32 = jnp.float32
BF16 = jnp.bfloat16
VMEM = pl.BlockSpec(memory_space=pltpu.VMEM)
SMEM = pl.BlockSpec(memory_space=pltpu.SMEM)


def cost(micros):
    return pl.CostEstimate(
        flops=int(micros * 1e9), transcendentals=0, bytes_accessed=int(micros * 3e6)
    )


PARAMS = pltpu.CompilerParams(vmem_limit_bytes=56 * 1024 * 1024)


def two_halves(table):
    high = table.astype(ml_dtypes.bfloat16)
    return high, (table - high.astype(np.float64)).astype(ml_dtypes.bfloat16)


def mm(a, b):
    return jnp.dot(a, b, preferred_element_type=F32)


def split(a):
    high = a.astype(BF16)
    return high, (a - high.astype(F32)).astype(BF16)


def lane_bins(inner):
    parts = PATCH // inner
    lane = np.arange(LANES)
    width = LANES // parts
    return lane // width + parts * (lane % width)


def inverse_fft(real, imag):
    count = len(real)
    if count == 1:
        return real, imag
    even_r, even_i = inverse_fft(real[0::2], imag[0::2])
    odd_r, odd_i = inverse_fft(real[1::2], imag[1::2])
    half = count // 2
    out_r, out_i = [None] * count, [None] * count
    for k in range(half):
        angle = 2.0 * math.pi * k / count
        c, s = math.cos(angle), math.sin(angle)
        if k == 0:
            r, i = odd_r[k], odd_i[k]
        elif 4 * k == count:
            r, i = -odd_i[k], odd_r[k]
        else:
            r = odd_r[k] * c - odd_i[k] * s
            i = odd_r[k] * s + odd_i[k] * c
        out_r[k], out_i[k] = even_r[k] + r, even_i[k] + i
        out_r[k + half], out_i[k + half] = even_r[k] - r, even_i[k] - i
    return out_r, out_i


def first_section(
    rows_all, length, pos, amp, phase, mode, delay, bins, turn_ref, x_ref, twist_ref, near_ref, high_ref, low_ref,
    out_ref, base, acc, lhs,
):
    channels = x_ref.shape[1]
    sources = phase.shape[0]
    inner = x_ref.shape[2]
    row_block = x_ref.shape[3]
    shape = (row_block, LANES)
    row = pos[0] * row_block + lax.broadcasted_iota(jnp.int32, shape, 0)
    lane = lax.broadcasted_iota(jnp.int32, shape, 1)
    first_bin = row + rows_all * lane
    unit = 2.0 * math.pi / length

    group = math.gcd(sources, 4)

    def make_base(g, _):
        for n in range(group):
            s = g * group + n
            turn = ((((first_bin * delay[s]) & (length - 1)) * mode[s]) & (length - 1)).astype(F32)
            angle = mode[s].astype(F32) * phase[s] + turn * unit
            base[pl.ds(pl.multiple_of(s * row_block, row_block), row_block), :] = jnp.cos(angle)
            base[pl.ds(pl.multiple_of((sources + s) * row_block, row_block), row_block), :] = jnp.sin(angle)
        return 0

    lax.fori_loop(0, sources // group, make_base, 0)

    width = rows_all * LANES
    high_bits = lax.broadcasted_iota(jnp.int32, (inner, LANES), 0)
    place = lax.broadcasted_iota(jnp.int32, (1, LANES), 1)

    def spread_out(value, kind):
        out = jnp.zeros((1, LANES), kind)
        for s in range(sources):
            out = jnp.where(place == s, value(s), out)
        return out

    lag = spread_out(lambda s: delay[s] * mode[s], jnp.int32)
    low_end = spread_out(lambda s: bins[0, s], jnp.int32)
    high_end = spread_out(lambda s: bins[1, s], jnp.int32)
    step_angle = ((lag * high_bits) & (inner - 1)).astype(F32) * (2.0 * math.pi / inner)
    known = lax.broadcasted_iota(jnp.int32, (inner, LANES), 1) < sources
    full = known & (low_end <= high_bits * width) & (high_end >= (high_bits + 1) * width)
    step_cos = jnp.where(full, jnp.cos(step_angle), 0.0)
    step_sin = jnp.where(full, jnp.sin(step_angle), 0.0)
    rows = []
    for r in range(2):
        one, two = (step_cos, -step_sin) if r == 0 else (step_sin, step_cos)
        for c in range(channels):
            gain = spread_out(lambda s: amp[c, s], F32)
            rows.append(gain * one + pltpu.roll(gain * two, sources, 1))
    rows = jnp.concatenate(rows, axis=0)
    top = rows.astype(BF16).astype(F32)
    rest = (rows - top).astype(BF16).astype(F32)
    left = (top + pltpu.roll(top, 2 * sources, 1) + pltpu.roll(rest, 4 * sources, 1)).astype(BF16)
    blank = jnp.zeros((LANES - 6 * sources, LANES), F32)
    for u in range(row_block):
        wave = base[pl.ds(u, 2 * sources, stride=row_block), :]
        top = wave.astype(BF16).astype(F32)
        right = jnp.concatenate([top, wave - top, top, blank], axis=0).astype(BF16)
        acc[pl.ds(u, 2 * channels * inner, stride=row_block), :] = mm(left, right)

    def add_ends(s, _):
        first, past = bins[0, s], bins[1, s]
        at_first, at_past = lax.div(first, width), lax.div(past, width)
        begins = (first > at_first * width) | (past < (at_first + 1) * width)
        ends = (at_past != at_first) & (at_past < inner)
        for at, wanted in ((at_first, begins), (at_past, ends)):
            @pl.when(wanted)
            def _(at=at):
                here = first_bin + width * at
                which = (delay[s] * mode[s] * at) & (inner - 1)
                tr, ti = turn_ref[0, which], turn_ref[1, which]
                inside = (here >= first) & (here < past)
                br = base[pl.ds(pl.multiple_of(s * row_block, row_block), row_block), :]
                bi = base[pl.ds(pl.multiple_of((sources + s) * row_block, row_block), row_block), :]
                real = jnp.where(inside, br * tr - bi * ti, 0.0)
                imag = jnp.where(inside, br * ti + bi * tr, 0.0)
                for c in range(channels):
                    for n, part in ((c, real), (channels + c, imag)):
                        slot = pl.ds(pl.multiple_of((n * inner + at) * row_block, row_block), row_block)
                        acc[slot, :] = acc[slot, :] + amp[c, s] * part
        return 0

    lax.fori_loop(0, sources, add_ends, 0)

    def total(r, c, v):
        slot = pl.multiple_of(((r * channels + c) * inner + v) * row_block, row_block)
        return x_ref[r, c, v] + acc[pl.ds(slot, row_block), :]

    def transform(c, _):
        real, imag = inverse_fft(
            [total(0, c, v) for v in range(inner)], [total(1, c, v) for v in range(inner)]
        )
        for q in range(inner):
            tc, ts = twist_ref[0, q : q + 1, :], twist_ref[1, q : q + 1, :]
            lhs[c, q, :, 0:LANES] = real[q] * tc - imag[q] * ts
            lhs[c, q, :, LANES : 2 * LANES] = real[q] * ts + imag[q] * tc
        return 0

    lax.fori_loop(0, channels, transform, 0)

    wide = (inner, row_block, LANES)
    parts = PATCH // inner
    width = LANES // parts
    flat = (inner, LANES)
    lanes = lax.broadcasted_iota(jnp.int32, flat, 1)
    outer = lax.div(lanes, width) + parts * lax.rem(lanes, width)
    column = lax.broadcasted_iota(jnp.int32, flat, 0) + inner * outer
    angle = ((pos[0] * row_block * column) & (length - 1)).astype(F32) * unit
    turn_cos, turn_sin = jnp.cos(angle)[:, None, :], jnp.sin(angle)[:, None, :]
    near_cos, near_sin = near_ref[0], near_ref[1]
    cos = turn_cos * near_cos - turn_sin * near_sin
    sin = turn_sin * near_cos + turn_cos * near_sin
    for c in range(channels):
        high, low = split(lhs[c].reshape(inner * row_block, 2 * LANES))
        got = mm(high, high_ref[...]) + mm(low, high_ref[...]) + mm(high, low_ref[...])
        real = got[:, 0:LANES].reshape(wide)
        imag = got[:, LANES : 2 * LANES].reshape(wide)
        out_ref[:, c] = (real * cos - imag * sin).astype(BF16)
        out_ref[:, channels + c] = (real * sin + imag * cos).astype(BF16)


def run_first(spectrum, amp, phase, mode, delay, bins, pos, rows_all, length):
    _, channels, row_block, columns = spectrum.shape
    inner = columns // LANES
    grid_in = spectrum.reshape(2, channels, row_block, inner, LANES).transpose(0, 1, 3, 2, 4)
    steps = np.arange(inner)
    turn = 2.0 * np.pi * steps / inner
    turns = np.stack([np.cos(turn), np.sin(turn)]).astype(np.float32)
    lane = np.arange(LANES)
    twist = 2.0 * np.pi * (steps[:, None] * lane[None, :] % columns) / columns
    twists = np.stack([np.cos(twist), np.sin(twist)]).astype(np.float32)
    column = steps[:, None] + inner * lane_bins(inner)[None, :]
    near = 2.0 * np.pi * np.arange(row_block)[None, :, None] * column[:, None, :] / length
    nears = np.stack([np.cos(near), np.sin(near)]).astype(np.float32)
    angle = 2.0 * np.pi * (lane[:, None] * lane_bins(inner)[None, :] % LANES) / LANES
    cos, sin = np.cos(angle), np.sin(angle)
    high, low = two_halves(np.block([[cos, sin], [-sin, cos]]))
    return pl.pallas_call(
        functools.partial(first_section, rows_all, length),
        out_shape=jax.ShapeDtypeStruct((inner, 2 * channels, row_block, LANES), BF16),
        in_specs=[SMEM] * 7 + [VMEM] * 5,
        out_specs=VMEM,
        scratch_shapes=[
            pltpu.VMEM((2 * amp.shape[0] * row_block, LANES), F32),
            pltpu.VMEM((2 * channels * inner * row_block, LANES), F32),
            pltpu.VMEM((channels, inner, row_block, 2 * LANES), F32),
        ],
        compiler_params=PARAMS,
        cost_estimate=cost(7),
        name="first_section",
    )(pos, amp.T, phase, mode, delay, bins.T, turns, grid_in, twists, nears, high, low)


def second_section(reps, z_ref, high_ref, low_ref, out_ref):
    devices, own, pairs, row_block, _ = z_ref.shape
    channels = pairs // 2
    rows = devices * row_block
    tiles = own * pairs
    half = (tiles + 1) // 2
    lane = lax.broadcasted_iota(jnp.int32, (rows, LANES), 1)
    sub = lax.rem(lax.broadcasted_iota(jnp.int32, (rows, LANES), 0), row_block)
    upper = (lane & 32) != 0
    rim = jnp.zeros((rows, LANES), F32)
    for q in range(own):
        for c in range(channels):
            right = jnp.concatenate(
                [z_ref[:, q, r * channels + c].astype(F32).reshape(rows, LANES) for r in range(2)], axis=0
            ).astype(BF16)
            got = mm(high_ref[...], right) + mm(low_ref[...], right)
            for r in range(2):
                tile = q * pairs + r * channels + c
                part = got[r * rows : (r + 1) * rows]
                out_ref[:, tile] = part.reshape(devices, row_block, LANES).astype(BF16)
                ends = jnp.broadcast_to(
                    part.reshape(devices, row_block, LANES)[:, row_block - 1 :, :],
                    (devices, row_block, LANES),
                ).reshape(rows, LANES)
                if tile < half:
                    rim = jnp.where(upper & (sub == tile), ends, rim)
                else:
                    ends = pltpu.roll(ends, LANES - 32, 1)
                    rim = jnp.where(jnp.logical_not(upper) & (sub == tile - half), ends, rim)
    rim = rim.reshape(devices, row_block, LANES).astype(BF16)
    for d in range(devices):
        source = d - d % reps - 1
        out_ref[d, tiles] = rim[source] if source >= 0 else jnp.zeros((row_block, LANES), BF16)


def run_second(z, length):
    devices, own, pairs, row_block, _ = z.shape
    rows = devices * row_block
    counter = np.arange(rows)
    angle = 2.0 * np.pi * (counter[:, None] * counter[None, :] % rows) / rows
    cos, sin = np.cos(angle), np.sin(angle)
    high, low = two_halves(np.block([[cos, -sin], [sin, cos]]) / math.sqrt(length))
    return pl.pallas_call(
        functools.partial(second_section, lax.axis_size("rep")),
        out_shape=jax.ShapeDtypeStruct((devices, own * pairs + 1, row_block, LANES), BF16),
        in_specs=[VMEM] * 3,
        out_specs=VMEM,
        compiler_params=PARAMS,
        cost_estimate=cost(3),
        name="second_section",
    )(z, high, low)


def order_patches(x_ref, perm_ref, rim_ref, out_ref, wide):
    devices, tiles, row_block, _ = x_ref.shape
    parts = perm_ref.shape[0]
    width = LANES // parts
    half = tiles // 2
    wide[...] = x_ref[...].astype(F32).reshape(devices * tiles * row_block, LANES)
    for m in range(row_block):
        rows = wide[pl.ds(m, devices * tiles, stride=row_block), :]
        across = rows.T.astype(BF16)
        total = mm(across[0:width], perm_ref[0])
        for n in range(1, parts):
            total = total + mm(across[n * width : (n + 1) * width], perm_ref[n])
        out_ref[m * width : (m + 1) * width, :] = total.astype(BF16)
    rows = jnp.concatenate(
        [wide[pl.ds((tiles - 1) * row_block + n, devices, stride=tiles * row_block), :] for n in range(half)],
        axis=0,
    )
    across = jnp.concatenate([rows, pltpu.roll(rows, 32, 1)], axis=0).T.astype(BF16)
    total = mm(across[width - 8 : width], rim_ref[0])
    for n in range(1, parts):
        total = total + mm(across[(n + 1) * width - 8 : (n + 1) * width], rim_ref[n])
    out_ref[row_block * width :, :] = total.astype(BF16)


def run_order(x, inner, channels):
    devices, tiles, row_block, _ = x.shape
    parts = PATCH // inner
    own = tiles - 1
    pairs = 2 * channels
    each = own // pairs
    perm = np.zeros((parts, devices * tiles, pairs * PATCH), ml_dtypes.bfloat16)
    rim = np.zeros((parts, own * devices, pairs * PATCH), ml_dtypes.bfloat16)
    for n in range(parts):
        for j in range(devices):
            for q in range(each):
                for rc in range(pairs):
                    to = rc * PATCH + n * inner + j * each + q
                    perm[n, j * tiles + q * pairs + rc, to] = 1
                    rim[n, (q * pairs + rc) * devices + j, to] = 1
    return pl.pallas_call(
        order_patches,
        out_shape=jax.ShapeDtypeStruct((row_block * LANES // parts + 8, pairs * PATCH), BF16),
        in_specs=[VMEM] * 3,
        out_specs=VMEM,
        scratch_shapes=[pltpu.VMEM((devices * tiles * row_block, LANES), F32)],
        compiler_params=PARAMS,
        cost_estimate=cost(3),
        name="order_patches",
    )(x, perm, rim)


def dft_table(order):
    counter = jnp.arange(order, dtype=jnp.int32)
    turn_count = counter[:, None] * counter[None, :] % order
    radians = turn_count.astype(F32) * (2.0 * math.pi / order)
    return jnp.stack([jnp.cos(radians), jnp.sin(radians)])


def make_patches(first, length):
    devices = lax.axis_size(ALL)
    inner, pairs, row_block, _ = first.shape
    channels = pairs // 2
    if inner % devices == 0 and 2 * inner == PATCH and inner // devices * pairs in range(2, 17, 2):
        own = inner // devices
        moved = lax.all_to_all(
            first.reshape(devices, own, pairs, row_block, LANES), ALL, 0, 0, tiled=True
        )
        moved = lax.all_to_all(run_second(moved, length), ALL, 0, 0, tiled=True)
        return run_order(moved, inner, channels)
    flat = first.transpose(1, 2, 0, 3).reshape(2, channels, row_block, inner * LANES)
    flat = lax.all_to_all(flat, ALL, split_axis=3, concat_axis=2, tiled=True).astype(F32)
    mixed = jnp.einsum(
        "rcuq,kum->krcqm", flat, dft_table(row_block * devices), precision=lax.Precision.HIGHEST
    )
    series = jnp.stack([mixed[0, 0] - mixed[1, 1], mixed[1, 0] + mixed[0, 1]])
    series = (series * (1.0 / math.sqrt(length))).astype(BF16)
    series = lax.all_to_all(series, ALL, split_axis=4 - 1, concat_axis=2, tiled=True)
    parts = PATCH // inner
    series = series.reshape(2, channels, inner, parts, LANES // parts, row_block)
    patches = series.transpose(5, 4, 0, 1, 3, 2).reshape(
        row_block * LANES // parts, 2 * channels * PATCH
    )
    reps = lax.axis_size("rep")
    tail = patches[patches.shape[0] - 8 :]
    rim = jnp.zeros_like(tail)
    for r in range(reps):
        pairs = [(i - 1, i + r) for i in range(reps, devices, reps)]
        rim = rim + lax.ppermute(tail, ALL, pairs)
    return jnp.concatenate([patches, rim], 0)


def norm_rows(values, total):
    return lax.rsqrt(jnp.sum(values * values, axis=-1, keepdims=True) * (1.0 / total) + EPSILON)


def silu(values):
    half = 0.5 * values
    return half + half * jnp.tanh(half)


def fold(ends, count, head, entering, upto=None):
    state = entering.shape[0]
    for i in range(count):
        part, decay = ends[0][0:state], ends[0][state : state + 1]
        for j in range(1, len(ends)):
            here = (head ^ i) == j
            part = jnp.where(here, ends[j][0:state], part)
            decay = jnp.where(here, ends[j][state : state + 1], decay)
        after = decay * entering + part
        entering = after if upto is None else jnp.where(i < upto, after, entering)
    return entering


def expand(values, spread):
    high, low = split(values)
    return mm(jnp.concatenate([high, low], axis=1), spread[...])


def block_states(heads, per, reps, before, final, me_ref, *refs):
    pats, refs = refs[:2], refs[2:]
    halo, we, nin, wx, wbc, wdt, dtb, alog, cx, cbc, spread = refs[:11]
    earlier, refs = refs[11 : 11 + before], refs[11 + before :]
    normed_ref, x_ref, b_ref, c_ref, cum_ref, step_ref, local_ref, grown_ref, st_ref = refs[:9]
    xs, bcs, carried, total, low_tri, dts, rows, tail = refs[-8:]
    block = pl.program_id(0)
    state = wbc.shape[1] // 2
    taps = cx.shape[0]

    gains = nin[...].astype(F32)
    gains = jnp.concatenate([gains[i : i + 1] for i in range(gains.shape[0])], axis=1)

    def features(p):
        embedded = mm(p, we[...]).astype(BF16).astype(F32)
        scale = norm_rows(embedded, embedded.shape[-1])
        return (embedded * scale * gains).astype(BF16)

    @pl.when(block == 0)
    def _():
        carried[...] = jnp.zeros_like(carried)
        total[...] = jnp.zeros_like(total)
        tail[...] = jnp.zeros_like(tail)
        tail[8:16] = halo[...].astype(F32)
        ri = lax.broadcasted_iota(jnp.int32, (SPAN, SPAN), 0)
        ci = lax.broadcasted_iota(jnp.int32, (SPAN, SPAN), 1)
        low_tri[...] = jnp.where(ri >= ci, 1.0, 0.0).astype(BF16)
        dts[...] = jnp.zeros_like(dts)
        rows[...] = jnp.zeros_like(rows)
        rows[0:1, 0:heads] = dtb[...]
        rows[1:2, 0:heads] = -jnp.exp(alog[...])

    here = ((block // per) ^ lax.rem(me_ref[0], reps)) == 0
    span = pats[0].shape[0]
    patch = jnp.where(here, pats[0][...], pats[1][...]).astype(F32)
    joined = features(jnp.concatenate([tail[...], patch], axis=0).astype(BF16))
    tail[...] = patch[span - 16 :]
    normed = joined[16:]
    normed_ref[...] = normed
    dts[:, 0:heads] = lax.dot_general(
        normed, wdt[...], (((1,), (1,)), ((), ())), preferred_element_type=F32
    )
    bcs[...] = mm(joined, wbc[...]).astype(BF16).astype(F32)
    xs[...] = mm(joined, wx[...]).astype(BF16).astype(F32)
    step_all = dts[...] + rows[0:1]
    step_all = jnp.maximum(step_all, 0.0) + jnp.log1p(jnp.exp(-jnp.abs(step_all)))
    step_ref[...] = step_all

    def conv(buffer, kernel, at):
        out = kernel[0:1] * buffer[at + 17 - taps : at + 17 - taps + SPAN]
        for i in range(1, taps):
            out = out + kernel[i : i + 1] * buffer[at + 17 - taps + i : at + 17 - taps + i + SPAN]
        return silu(out)

    for n in range(span // SPAN):
        at = n * SPAN
        step = step_all[at : at + SPAN]
        rated = step * rows[1:2]
        one = rated.astype(BF16).astype(F32)
        two = (rated - one).astype(BF16).astype(F32)
        three = rated - one - two
        packed = one + pltpu.roll(two, heads, 1) + pltpu.roll(three, 2 * heads, 1)
        sums = mm(low_tri[...], packed.astype(BF16))
        cum = sums + pltpu.roll(sums, LANES - heads, 1) + pltpu.roll(sums, LANES - 2 * heads, 1)
        cum_ref[at : at + SPAN] = cum
        last = cum[SPAN - 1 : SPAN]
        weights = expand(jnp.exp(last - cum) * step, spread)
        grow = expand(
            jnp.exp(jnp.concatenate([jnp.broadcast_to(last, (8, LANES)), total[...]], axis=0)), spread
        )
        bc = conv(bcs, cbc, at)
        b_ref[at : at + SPAN] = bc[:, :state].astype(BF16)
        c_ref[at : at + SPAN] = bc[:, state:].astype(BF16)
        bt = bc[:, :state].T.astype(BF16)
        xc = conv(xs, cx, at).astype(BF16)
        x_ref[at : at + SPAN] = xc
        weighted = (xc.astype(F32) * weights).astype(BF16)
        local_ref[n] = carried[...]
        grown_ref[n] = grow[8:16]
        carried[...] = carried[...] * grow[0:1] + mm(bt, weighted)
        total[...] = total[...] + last

    @pl.when(block == pl.num_programs(0) - 1)
    def _():
        st_ref[0:state] = carried[...]
        st_ref[state : state + 8] = grow[8:16] * grow[0:8]
        if final:
            everything = [e[...] for e in earlier] + [st_ref[...]]
            count = len(everything)
            send = refs[9]
            zero = jnp.zeros((state, xs.shape[1]), F32)
            send[0:state] = fold(everything, count, lax.div(me_ref[0], reps), zero).astype(BF16)
            decay = everything[0][state : state + 8]
            for e in everything[1:]:
                decay = decay * e[state : state + 8]
            send[state : state + 8] = decay.astype(BF16)


def run_states(me, pats, halo, consts, heads, inner, state, own, earlier, final):
    rows_in, width = pats[0].shape
    model = consts[0].shape[1]
    tokens = own * len(pats)
    span = min(own, TILE)
    per = own // span
    blocks = tokens // SPAN
    subs = span // SPAN
    row = lambda n: pl.BlockSpec((span, n), lambda b, me: (b, 0))
    fixed = pl.BlockSpec((state + 8, inner), lambda b, me: (0, 0))
    shape = lambda *d, t=F32: jax.ShapeDtypeStruct(d, t)
    return pl.pallas_call(
        functools.partial(block_states, heads, per, len(pats), len(earlier), final),
        grid_spec=pltpu.PrefetchScalarGridSpec(
            num_scalar_prefetch=1,
            grid=(tokens // span,),
            in_specs=[pl.BlockSpec((span, width), lambda b, me: (b % per, 0))] * len(pats)
            + [pl.BlockSpec((8, width), lambda b, me: (own // 8, 0))]
            + [VMEM] * (len(consts) + len(earlier)),
            out_specs=[row(model), row(inner), row(state), row(state), row(LANES), row(LANES),
                       pl.BlockSpec((subs, state, inner), lambda b, me: (b, 0, 0)),
                       pl.BlockSpec((subs, 8, inner), lambda b, me: (b, 0, 0)), fixed]
            + [fixed] * final,
            scratch_shapes=[
                pltpu.VMEM((span + 16, inner), F32),
                pltpu.VMEM((span + 16, 2 * state), F32),
                pltpu.VMEM((state, inner), F32),
                pltpu.VMEM((8, LANES), F32),
                pltpu.VMEM((SPAN, SPAN), BF16),
                pltpu.VMEM((span, LANES), F32),
                pltpu.VMEM((8, LANES), F32),
                pltpu.VMEM((16, width), F32),
            ],
        ),
        out_shape=[
            shape(tokens, model, t=BF16), shape(tokens, inner, t=BF16), shape(tokens, state, t=BF16),
            shape(tokens, state, t=BF16), shape(tokens, LANES), shape(tokens, LANES),
            shape(blocks, state, inner), shape(blocks, 8, inner), shape(state + 8, inner),
        ] + [shape(state + 8, inner, t=BF16)] * final,
        compiler_params=PARAMS,
        cost_estimate=cost(13),
        name="block_states",
    )(me, *pats, halo, *consts, *earlier)


def gate_tokens(normed_ref, wz, pat_ref, we, gate_ref, embed_ref):
    @pl.when(pl.program_id(0) == 0)
    def _():
        embed_ref[...] = mm(pat_ref[...], we[...]).astype(BF16)

    gate_ref[...] = silu(mm(normed_ref[...], wz[...]).astype(BF16).astype(F32)).astype(BF16)


def run_gate(normed, wz, patches, we, own):
    tokens, width = normed.shape
    inner = wz.shape[1]
    span = min(tokens, TILE)
    return pl.pallas_call(
        gate_tokens,
        grid=(tokens // span,),
        in_specs=[pl.BlockSpec((span, width), lambda b: (b, 0)), VMEM,
                  pl.BlockSpec((own, patches.shape[1]), lambda b: (0, 0)), VMEM],
        out_specs=[pl.BlockSpec((span, inner), lambda b: (b, 0)),
                   pl.BlockSpec((own, we.shape[1]), lambda b: (0, 0))],
        out_shape=[jax.ShapeDtypeStruct((tokens, inner), BF16),
                   jax.ShapeDtypeStruct((own, we.shape[1]), BF16)],
        compiler_params=PARAMS,
        cost_estimate=cost(4),
        name="gate_tokens",
    )(normed, wz, patches, we)


def outputs(
    heads, chip, chips, seqs, reps, which, gated, opening, me_ref, normed_ref, x_ref, b_ref, c_ref, cum_ref, step_ref, local_ref, grown_ref,
    *refs,
):
    if not gated:
        wz, refs = refs[0], refs[1:]
    spread, refs = refs[0], refs[1:]
    if opening:
        ends, earlier, refs = refs[:chips], refs[chips : chips + seqs], refs[chips + seqs :]
        entries, refs = refs[:chips], refs[chips:]
        start = entries[chip]
    else:
        start, refs = refs[0], refs[1:]
    outs, y_acc = refs[:-1], refs[-1]
    state = c_ref.shape[1]
    block = pl.program_id(0)
    per = pl.num_programs(0) // len(which)

    if opening:
        @pl.when(block == 0)
        def _():
            entering = jnp.zeros((state, x_ref.shape[1]), F32)
            for part in reversed(earlier):
                entering = part[0:state].astype(F32) + part[state : state + 1].astype(F32) * entering
            place = lax.div(me_ref[0], reps)
            known = [e[...] for e in ends]
            for c in range(chips):
                entries[c][...] = fold(known, chips - 1, place, entering, place ^ c)

    cum = cum_ref[...]
    log_cum = cum * LOG2E
    back = (log_cum - jnp.log2(step_ref[...])).T
    gram = lax.dot_general(
        c_ref[...], b_ref[...], (((1,), (1,)), ((), ())), preferred_element_type=F32
    )
    if gated:
        gate = normed_ref[...].astype(F32)
    else:
        gate = silu(mm(normed_ref[...], wz[...]).astype(BF16).astype(F32))
    half = SPAN // 2
    ri = lax.broadcasted_iota(jnp.int32, (half, half), 0)
    ci = lax.broadcasted_iota(jnp.int32, (half, half), 1)
    inside = ri >= ci
    head_dim = x_ref.shape[1] // heads
    for h in range(heads):
        cols = slice(h * head_dim, (h + 1) * head_dim)
        upper, lower = log_cum[:half, h : h + 1], log_cum[half:, h : h + 1]
        early, late = back[h : h + 1, :half], back[h : h + 1, half:]
        first = jnp.where(inside, jnp.exp2(upper - early), 0.0) * gram[:half, :half]
        cross = jnp.exp2(lower - early) * gram[half:, :half]
        second = jnp.where(inside, jnp.exp2(lower - late), 0.0) * gram[half:, half:]
        y_acc[:half, cols] = mm(first.astype(BF16), x_ref[:half, cols])
        y_acc[half:, cols] = mm(
            jnp.concatenate([cross.astype(BF16), second.astype(BF16)], axis=1), x_ref[:, cols]
        )
    cm = c_ref[...]
    high, low = split(local_ref[0] + grown_ref[0, 0:1] * start[...])
    added = mm(jnp.concatenate([cm, cm], axis=1), jnp.concatenate([high, low], axis=0))
    value = ((y_acc[...] + expand(jnp.exp(cum), spread) * added) * gate).astype(BF16)
    whole = 0
    for n, r in enumerate(which):
        if chip or not r:
            @pl.when(block // per == n)
            def _(whole=whole):
                outs[whole][pl.ds(pl.multiple_of((block % per) * SPAN, SPAN), SPAN), :] = value
            whole += 1
    for n, r in enumerate(which):
        if not chip and r:
            for i in range(len(outs) - whole):
                @pl.when(block == whole * per + i)
                def _(i=i):
                    outs[whole + i][...] = value
            break


def run_outputs(heads, chip, chips, reps, which, me, gate, xc, bm, cm, cum, step, local, grown, wz, spread, enter, own):
    tokens, inner = xc.shape
    state = cm.shape[1]
    per = own // SPAN
    gated, opening = wz is None, isinstance(enter, tuple)
    ends, earlier = enter if opening else ([], [])
    shapes = []
    for r in which:
        shapes += [(own, inner)] if chip or not r else [(SPAN, inner)] * per
    at = lambda b, me: (lax.rem(me[0], reps) ^ (which[0] + b // per)) * per + b % per
    row = lambda n: pl.BlockSpec((SPAN, n), lambda b, me: (at(b, me), 0))
    block3 = lambda b, me: (at(b, me), 0, 0)
    fixed = lambda shape: pl.BlockSpec(shape, lambda b, me: (0, 0))
    firsts = [(state, inner)] * chips if opening else []
    extra = ([] if gated else [wz]) + [spread] + (list(ends) + list(earlier) if opening else [enter])
    return pl.pallas_call(
        functools.partial(outputs, heads, chip, chips, len(earlier), reps, which, gated, opening),
        grid_spec=pltpu.PrefetchScalarGridSpec(
            num_scalar_prefetch=1,
            grid=(len(which) * per,),
            in_specs=[row(a.shape[1]) for a in (gate, xc, bm, cm, cum, step)]
            + [pl.BlockSpec((1, state, inner), block3), pl.BlockSpec((1, 8, inner), block3)]
            + [VMEM] * len(extra),
            out_specs=[fixed(shape) for shape in firsts + shapes],
            scratch_shapes=[pltpu.VMEM((SPAN, inner), F32)],
        ),
        out_shape=[jax.ShapeDtypeStruct(shape, F32) for shape in firsts]
        + [jax.ShapeDtypeStruct(shape, BF16) for shape in shapes],
        compiler_params=PARAMS,
        cost_estimate=cost(0.05),
        name="outputs",
    )(me, gate, xc, bm, cm, cum, step, local, grown, *extra)


def pick_gains(norm, index, count):
    values = norm[...].astype(F32)
    each = values.shape[0] // count
    gains = None
    for j in range(count):
        row = jnp.concatenate([values[j * each + i : j * each + i + 1] for i in range(each)], axis=1)
        gains = row if gains is None else jnp.where(index == j, row, gains)
    return gains


def mix_most(sizes, share, me_ref, *refs):
    (norm, weight, mixed_ref, square_ref), refs = refs[-4:], refs[:-4]
    step = pl.program_id(0)
    parts = []
    for size in sizes:
        parts.append(refs[:size])
        refs = refs[size:]
    count = len(parts)
    whole = lambda n: jnp.concatenate([p[...] for p in parts[n]], axis=0).astype(F32)

    @pl.when(step == 0)
    def _():
        square = None
        for n in range(count):
            v = whole(n)
            square = v * v if square is None else square + v * v
        square_ref[...] = jnp.broadcast_to(jnp.sum(square, axis=-1, keepdims=True), square_ref.shape)

    gains = pick_gains(norm, me_ref[0] ^ step, share)
    for n in range(count):
        @pl.when(step == n)
        def _(n=n):
            got = mm((whole(n) * gains).astype(BF16), weight[0])
            mixed_ref[...] = got if n == 0 else mixed_ref[...] + got


def mix_last(total, share, me_ref, embed_ref, mixed_ref, square_ref, part_ref, norm, weight, out_ref):
    v = part_ref[...].astype(F32)
    gains = pick_gains(norm, me_ref[0] ^ (share - 1), share)
    got = mm((v * gains).astype(BF16), weight[0])
    square = square_ref[:, 0:1] + jnp.sum(v * v, axis=-1, keepdims=True)
    scale = lax.rsqrt(square * (1.0 / total) + EPSILON)
    out_ref[...] = (embed_ref[...].astype(F32) + scale * (mixed_ref[...] + got)).astype(BF16)


def run_mix(me, embed, parts, norm_out, w_out):
    share = len(parts)
    count = share - 1
    parts = [p if isinstance(p, list) else [p] for p in parts]
    sizes = [len(p) for p in parts[:count]]
    most = [v for p in parts[:count] for v in p]
    (final,) = parts[count]
    own, inner = final.shape
    width = w_out.shape[1]
    norms = norm_out.reshape(-1, LANES)
    weights = w_out.reshape(share, inner, width)
    full = pl.BlockSpec((own, width), lambda d, me: (0, 0))
    mixed, square = pl.pallas_call(
        functools.partial(mix_most, sizes, share),
        grid_spec=pltpu.PrefetchScalarGridSpec(
            num_scalar_prefetch=1,
            grid=(count,),
            in_specs=[VMEM] * (len(most) + 1)
            + [pl.BlockSpec((1, inner, width), lambda d, me: (me[0] ^ d, 0, 0))],
            out_specs=[full, pl.BlockSpec((own, LANES), lambda d, me: (0, 0))],
        ),
        out_shape=[jax.ShapeDtypeStruct((own, width), F32),
                   jax.ShapeDtypeStruct((own, LANES), F32)],
        compiler_params=PARAMS,
        cost_estimate=cost(0.05),
        name="mix_most",
    )(me, *most, norms, weights)
    tile = SPAN
    row = lambda n: pl.BlockSpec((tile, n), lambda i, me: (i, 0))
    return pl.pallas_call(
        functools.partial(mix_last, share * inner, share),
        grid_spec=pltpu.PrefetchScalarGridSpec(
            num_scalar_prefetch=1,
            grid=(own // tile,),
            in_specs=[row(width), row(width), row(LANES), row(inner),
                      VMEM, pl.BlockSpec((1, inner, width), lambda i, me: (me[0] ^ count, 0, 0))],
            out_specs=row(width),
        ),
        out_shape=jax.ShapeDtypeStruct((own, width), BF16),
        compiler_params=PARAMS,
        cost_estimate=cost(3),
        name="mix_last",
    )(me, embed, mixed, square, final, norms, weights)


def swap(value, flip):
    count = lax.axis_size(HR)
    return lax.ppermute(value, HR, [(i, i ^ flip) for i in range(count)])


def shift(value, by):
    count = lax.axis_size("seq")
    return lax.ppermute(value, "seq", [(i, i + by) for i in range(count - by)])


def on_device(
    spectrum, src_amp, src_phase, src_mode, src_delay, src_bins, w_embed, norm_in, w_z, w_x, w_bc, w_dt,
    dt_bias, a_log, conv_x, conv_bc, norm_out, w_out,
):
    devices = lax.axis_size(ALL)
    share = lax.axis_size(HR)
    rows_all = spectrum.shape[2] * devices
    length = rows_all * spectrum.shape[3]
    pos = lax.axis_index(ALL).astype(jnp.int32).reshape(1)
    me = lax.axis_index(HR).astype(jnp.int32).reshape(1)
    first = run_first(
        spectrum, src_amp, src_phase, src_mode, src_delay, src_bins, pos, rows_all, length
    )
    patches = make_patches(first, length)
    own = patches.shape[0] - 8
    reps, chips = lax.axis_size("rep"), lax.axis_size("head")
    heads, inner, state = dt_bias.shape[0], w_x.shape[1], w_bc.shape[1] // 2
    spread = np.zeros((2 * LANES, inner), ml_dtypes.bfloat16)
    for h in range(heads):
        spread[h, h * (inner // heads) : (h + 1) * (inner // heads)] = 1
    spread[LANES:] = spread[:LANES]
    consts = (
        w_embed, norm_in.reshape(-1, LANES), w_x, w_bc, w_dt.T, dt_bias[None], a_log[None], conv_x, conv_bc,
        jnp.asarray(spread),
    )
    done, ends = [], []
    base = [patches] + [swap(patches, c * reps) for c in range(1, chips)]
    for c in range(chips):
        start = base[c]
        if ends:
            start, ends[-1] = lax.optimization_barrier((start, ends[-1]))
        group = [start] + [swap(start, r) for r in range(1, reps)]
        got = run_states(
            me, group, start, consts, heads, inner, state, own, ends, c == chips - 1
        )
        done.append(got[:8])
        ends.append(got[8])
    send = got[9]
    earlier = [shift(send, d) for d in range(1, lax.axis_size("seq"))]
    parts = [None] * share
    gate = None
    enter = (ends, earlier)
    for c in list(range(1, chips)) + [0]:
        normed, xc, bm, cm, cum, step, local, grown = done[c]
        if gate is not None:
            normed, gate = lax.optimization_barrier((normed, gate))
        ahead = normed
        if c == 1:
            ahead, embed = run_gate(normed, w_z, patches, w_embed, own)
        values = []
        for which in ([[r] for r in range(reps)] if c else [list(range(reps))]):
            got = run_outputs(
                heads, c, chips, reps, which, me, ahead, xc, bm, cm, cum, step, local, grown,
                None if c == 1 else w_z, spread, enter if isinstance(enter, tuple) else enter[c], own,
            )
            if isinstance(enter, tuple):
                enter, got = list(got[:chips]), list(got[chips:])
            values += got
            if c:
                ahead, values[-1] = lax.optimization_barrier((ahead, values[-1]))
        gate = values[-1]
        for r in reversed(range(reps)):
            d = c * reps + r
            if c or not r:
                parts[d] = swap(values[r], d) if d else values[0]
            else:
                per = own // SPAN
                pieces = values[1 + (r - 1) * per : 1 + r * per]
                parts[d] = [swap(v, d) for v in pieces]
    return run_mix(me, embed, parts, norm_out, w_out)


def solution(mesh):
    in_specs = (
        P("grp", None, ("seq", "head", "rep"), None),
        P("grp", None),
        P("grp"),
        P("grp"),
        P("grp"),
        P("grp", None),
        P(),
        P(),
        P(None, ("head", "rep")),
        P(None, ("head", "rep")),
        P(),
        P(None, ("head", "rep")),
        P(("head", "rep")),
        P(("head", "rep")),
        P(None, ("head", "rep")),
        P(),
        P(),
        P(),
    )
    out_specs = P(("grp", "seq", "head", "rep"), None)
    return jax.shard_map(
        on_device, mesh=mesh, in_specs=in_specs, out_specs=out_specs, check_vma=False
    )
```

```python
import functools
import math

import jax
import jax.numpy as jnp
import ml_dtypes
import numpy as np
from jax import lax
from jax.experimental import pallas as pl
from jax.experimental.pallas import tpu as pltpu
from jax.sharding import PartitionSpec as P

SPAN = 256
LOG2E = math.log2(math.e)
TILE = 512
EPSILON = 1e-05
LANES = 128
PATCH = 64
ALL = ("seq", "head", "rep")
HR = ("head", "rep")
F32 = jnp.float32
BF16 = jnp.bfloat16
VMEM = pl.BlockSpec(memory_space=pltpu.VMEM)
SMEM = pl.BlockSpec(memory_space=pltpu.SMEM)


def cost(micros):
    return pl.CostEstimate(
        flops=int(micros * 1e9), transcendentals=0, bytes_accessed=int(micros * 3e6)
    )


PARAMS = pltpu.CompilerParams(vmem_limit_bytes=56 * 1024 * 1024)


def two_halves(table):
    high = table.astype(ml_dtypes.bfloat16)
    return high, (table - high.astype(np.float64)).astype(ml_dtypes.bfloat16)


def mm(a, b):
    return jnp.dot(a, b, preferred_element_type=F32)


def split(a):
    high = a.astype(BF16)
    return high, (a - high.astype(F32)).astype(BF16)


def lane_bins(inner):
    parts = PATCH // inner
    lane = np.arange(LANES)
    width = LANES // parts
    return lane // width + parts * (lane % width)


def inverse_fft(real, imag):
    count = len(real)
    if count == 1:
        return real, imag
    even_r, even_i = inverse_fft(real[0::2], imag[0::2])
    odd_r, odd_i = inverse_fft(real[1::2], imag[1::2])
    half = count // 2
    out_r, out_i = [None] * count, [None] * count
    for k in range(half):
        angle = 2.0 * math.pi * k / count
        c, s = math.cos(angle), math.sin(angle)
        if k == 0:
            r, i = odd_r[k], odd_i[k]
        elif 4 * k == count:
            r, i = -odd_i[k], odd_r[k]
        else:
            r = odd_r[k] * c - odd_i[k] * s
            i = odd_r[k] * s + odd_i[k] * c
        out_r[k], out_i[k] = even_r[k] + r, even_i[k] + i
        out_r[k + half], out_i[k + half] = even_r[k] - r, even_i[k] - i
    return out_r, out_i


def first_section(
    rows_all, length, pos, amp, phase, mode, delay, bins, turn_ref, x_ref, twist_ref, near_ref, high_ref, low_ref,
    out_ref, base, acc, lhs,
):
    channels = x_ref.shape[1]
    sources = phase.shape[0]
    inner = x_ref.shape[2]
    row_block = x_ref.shape[3]
    shape = (row_block, LANES)
    row = pos[0] * row_block + lax.broadcasted_iota(jnp.int32, shape, 0)
    lane = lax.broadcasted_iota(jnp.int32, shape, 1)
    first_bin = row + rows_all * lane
    unit = 2.0 * math.pi / length

    group = math.gcd(sources, 4)

    def make_base(g, _):
        for n in range(group):
            s = g * group + n
            turn = ((((first_bin * delay[s]) & (length - 1)) * mode[s]) & (length - 1)).astype(F32)
            angle = mode[s].astype(F32) * phase[s] + turn * unit
            base[pl.ds(pl.multiple_of(s * row_block, row_block), row_block), :] = jnp.cos(angle)
            base[pl.ds(pl.multiple_of((sources + s) * row_block, row_block), row_block), :] = jnp.sin(angle)
        return 0

    lax.fori_loop(0, sources // group, make_base, 0)

    width = rows_all * LANES
    high_bits = lax.broadcasted_iota(jnp.int32, (inner, LANES), 0)
    place = lax.broadcasted_iota(jnp.int32, (1, LANES), 1)

    def spread_out(value, kind):
        out = jnp.zeros((1, LANES), kind)
        for s in range(sources):
            out = jnp.where(place == s, value(s), out)
        return out

    lag = spread_out(lambda s: delay[s] * mode[s], jnp.int32)
    low_end = spread_out(lambda s: bins[0, s], jnp.int32)
    high_end = spread_out(lambda s: bins[1, s], jnp.int32)
    step_angle = ((lag * high_bits) & (inner - 1)).astype(F32) * (2.0 * math.pi / inner)
    known = lax.broadcasted_iota(jnp.int32, (inner, LANES), 1) < sources
    full = known & (low_end <= high_bits * width) & (high_end >= (high_bits + 1) * width)
    step_cos = jnp.where(full, jnp.cos(step_angle), 0.0)
    step_sin = jnp.where(full, jnp.sin(step_angle), 0.0)
    rows = []
    for r in range(2):
        one, two = (step_cos, -step_sin) if r == 0 else (step_sin, step_cos)
        for c in range(channels):
            gain = spread_out(lambda s: amp[c, s], F32)
            rows.append(gain * one + pltpu.roll(gain * two, sources, 1))
    rows = jnp.concatenate(rows, axis=0)
    top = rows.astype(BF16).astype(F32)
    rest = (rows - top).astype(BF16).astype(F32)
    left = (top + pltpu.roll(top, 2 * sources, 1) + pltpu.roll(rest, 4 * sources, 1)).astype(BF16)
    blank = jnp.zeros((LANES - 6 * sources, LANES), F32)
    for u in range(row_block):
        wave = base[pl.ds(u, 2 * sources, stride=row_block), :]
        top = wave.astype(BF16).astype(F32)
        right = jnp.concatenate([top, wave - top, top, blank], axis=0).astype(BF16)
        acc[pl.ds(u, 2 * channels * inner, stride=row_block), :] = mm(left, right)

    def add_ends(s, _):
        first, past = bins[0, s], bins[1, s]
        at_first, at_past = lax.div(first, width), lax.div(past, width)
        begins = (first > at_first * width) | (past < (at_first + 1) * width)
        ends = (at_past != at_first) & (at_past < inner)
        for at, wanted in ((at_first, begins), (at_past, ends)):
            @pl.when(wanted)
            def _(at=at):
                here = first_bin + width * at
                which = (delay[s] * mode[s] * at) & (inner - 1)
                tr, ti = turn_ref[0, which], turn_ref[1, which]
                inside = (here >= first) & (here < past)
                br = base[pl.ds(pl.multiple_of(s * row_block, row_block), row_block), :]
                bi = base[pl.ds(pl.multiple_of((sources + s) * row_block, row_block), row_block), :]
                real = jnp.where(inside, br * tr - bi * ti, 0.0)
                imag = jnp.where(inside, br * ti + bi * tr, 0.0)
                for c in range(channels):
                    for n, part in ((c, real), (channels + c, imag)):
                        slot = pl.ds(pl.multiple_of((n * inner + at) * row_block, row_block), row_block)
                        acc[slot, :] = acc[slot, :] + amp[c, s] * part
        return 0

    lax.fori_loop(0, sources, add_ends, 0)

    def total(r, c, v):
        slot = pl.multiple_of(((r * channels + c) * inner + v) * row_block, row_block)
        return x_ref[r, c, v] + acc[pl.ds(slot, row_block), :]

    def transform(c, _):
        real, imag = inverse_fft(
            [total(0, c, v) for v in range(inner)], [total(1, c, v) for v in range(inner)]
        )
        for q in range(inner):
            tc, ts = twist_ref[0, q : q + 1, :], twist_ref[1, q : q + 1, :]
            lhs[c, q, :, 0:LANES] = real[q] * tc - imag[q] * ts
            lhs[c, q, :, LANES : 2 * LANES] = real[q] * ts + imag[q] * tc
        return 0

    lax.fori_loop(0, channels, transform, 0)

    wide = (inner, row_block, LANES)
    parts = PATCH // inner
    width = LANES // parts
    flat = (inner, LANES)
    lanes = lax.broadcasted_iota(jnp.int32, flat, 1)
    outer = lax.div(lanes, width) + parts * lax.rem(lanes, width)
    column = lax.broadcasted_iota(jnp.int32, flat, 0) + inner * outer
    angle = ((pos[0] * row_block * column) & (length - 1)).astype(F32) * unit
    turn_cos, turn_sin = jnp.cos(angle)[:, None, :], jnp.sin(angle)[:, None, :]
    near_cos, near_sin = near_ref[0], near_ref[1]
    cos = turn_cos * near_cos - turn_sin * near_sin
    sin = turn_sin * near_cos + turn_cos * near_sin
    for c in range(channels):
        high, low = split(lhs[c].reshape(inner * row_block, 2 * LANES))
        got = mm(high, high_ref[...]) + mm(low, high_ref[...]) + mm(high, low_ref[...])
        real = got[:, 0:LANES].reshape(wide)
        imag = got[:, LANES : 2 * LANES].reshape(wide)
        out_ref[:, c] = (real * cos - imag * sin).astype(BF16)
        out_ref[:, channels + c] = (real * sin + imag * cos).astype(BF16)


def run_first(spectrum, amp, phase, mode, delay, bins, pos, rows_all, length):
    _, channels, row_block, columns = spectrum.shape
    inner = columns // LANES
    grid_in = spectrum.reshape(2, channels, row_block, inner, LANES).transpose(0, 1, 3, 2, 4)
    steps = np.arange(inner)
    turn = 2.0 * np.pi * steps / inner
    turns = np.stack([np.cos(turn), np.sin(turn)]).astype(np.float32)
    lane = np.arange(LANES)
    twist = 2.0 * np.pi * (steps[:, None] * lane[None, :] % columns) / columns
    twists = np.stack([np.cos(twist), np.sin(twist)]).astype(np.float32)
    column = steps[:, None] + inner * lane_bins(inner)[None, :]
    near = 2.0 * np.pi * np.arange(row_block)[None, :, None] * column[:, None, :] / length
    nears = np.stack([np.cos(near), np.sin(near)]).astype(np.float32)
    angle = 2.0 * np.pi * (lane[:, None] * lane_bins(inner)[None, :] % LANES) / LANES
    cos, sin = np.cos(angle), np.sin(angle)
    high, low = two_halves(np.block([[cos, sin], [-sin, cos]]))
    return pl.pallas_call(
        functools.partial(first_section, rows_all, length),
        out_shape=jax.ShapeDtypeStruct((inner, 2 * channels, row_block, LANES), BF16),
        in_specs=[SMEM] * 7 + [VMEM] * 5,
        out_specs=VMEM,
        scratch_shapes=[
            pltpu.VMEM((2 * amp.shape[0] * row_block, LANES), F32),
            pltpu.VMEM((2 * channels * inner * row_block, LANES), F32),
            pltpu.VMEM((channels, inner, row_block, 2 * LANES), F32),
        ],
        compiler_params=PARAMS,
        cost_estimate=cost(7),
        name="first_section",
    )(pos, amp.T, phase, mode, delay, bins.T, turns, grid_in, twists, nears, high, low)


def second_section(reps, z_ref, high_ref, low_ref, out_ref):
    devices, own, pairs, row_block, _ = z_ref.shape
    channels = pairs // 2
    rows = devices * row_block
    tiles = own * pairs
    half = (tiles + 1) // 2
    lane = lax.broadcasted_iota(jnp.int32, (rows, LANES), 1)
    sub = lax.rem(lax.broadcasted_iota(jnp.int32, (rows, LANES), 0), row_block)
    upper = (lane & 32) != 0
    rim = jnp.zeros((rows, LANES), F32)
    for q in range(own):
        for c in range(channels):
            right = jnp.concatenate(
                [z_ref[:, q, r * channels + c].astype(F32).reshape(rows, LANES) for r in range(2)], axis=0
            ).astype(BF16)
            got = mm(high_ref[...], right) + mm(low_ref[...], right)
            for r in range(2):
                tile = q * pairs + r * channels + c
                part = got[r * rows : (r + 1) * rows]
                out_ref[:, tile] = part.reshape(devices, row_block, LANES).astype(BF16)
                ends = jnp.broadcast_to(
                    part.reshape(devices, row_block, LANES)[:, row_block - 1 :, :],
                    (devices, row_block, LANES),
                ).reshape(rows, LANES)
                if tile < half:
                    rim = jnp.where(upper & (sub == tile), ends, rim)
                else:
                    ends = pltpu.roll(ends, LANES - 32, 1)
                    rim = jnp.where(jnp.logical_not(upper) & (sub == tile - half), ends, rim)
    rim = rim.reshape(devices, row_block, LANES).astype(BF16)
    for d in range(devices):
        source = d - d % reps - 1
        out_ref[d, tiles] = rim[source] if source >= 0 else jnp.zeros((row_block, LANES), BF16)


def run_second(z, length):
    devices, own, pairs, row_block, _ = z.shape
    rows = devices * row_block
    counter = np.arange(rows)
    angle = 2.0 * np.pi * (counter[:, None] * counter[None, :] % rows) / rows
    cos, sin = np.cos(angle), np.sin(angle)
    high, low = two_halves(np.block([[cos, -sin], [sin, cos]]) / math.sqrt(length))
    return pl.pallas_call(
        functools.partial(second_section, lax.axis_size("rep")),
        out_shape=jax.ShapeDtypeStruct((devices, own * pairs + 1, row_block, LANES), BF16),
        in_specs=[VMEM] * 3,
        out_specs=VMEM,
        compiler_params=PARAMS,
        cost_estimate=cost(3),
        name="second_section",
    )(z, high, low)


def order_patches(x_ref, perm_ref, rim_ref, out_ref, wide):
    devices, tiles, row_block, _ = x_ref.shape
    parts = perm_ref.shape[0]
    width = LANES // parts
    half = tiles // 2
    wide[...] = x_ref[...].astype(F32).reshape(devices * tiles * row_block, LANES)
    for m in range(row_block):
        rows = wide[pl.ds(m, devices * tiles, stride=row_block), :]
        across = rows.T.astype(BF16)
        total = mm(across[0:width], perm_ref[0])
        for n in range(1, parts):
            total = total + mm(across[n * width : (n + 1) * width], perm_ref[n])
        out_ref[m * width : (m + 1) * width, :] = total.astype(BF16)
    rows = jnp.concatenate(
        [wide[pl.ds((tiles - 1) * row_block + n, devices, stride=tiles * row_block), :] for n in range(half)],
        axis=0,
    )
    across = jnp.concatenate([rows, pltpu.roll(rows, 32, 1)], axis=0).T.astype(BF16)
    total = mm(across[width - 8 : width], rim_ref[0])
    for n in range(1, parts):
        total = total + mm(across[(n + 1) * width - 8 : (n + 1) * width], rim_ref[n])
    out_ref[row_block * width :, :] = total.astype(BF16)


def run_order(x, inner, channels):
    devices, tiles, row_block, _ = x.shape
    parts = PATCH // inner
    own = tiles - 1
    pairs = 2 * channels
    each = own // pairs
    perm = np.zeros((parts, devices * tiles, pairs * PATCH), ml_dtypes.bfloat16)
    rim = np.zeros((parts, own * devices, pairs * PATCH), ml_dtypes.bfloat16)
    for n in range(parts):
        for j in range(devices):
            for q in range(each):
                for rc in range(pairs):
                    to = rc * PATCH + n * inner + j * each + q
                    perm[n, j * tiles + q * pairs + rc, to] = 1
                    rim[n, (q * pairs + rc) * devices + j, to] = 1
    return pl.pallas_call(
        order_patches,
        out_shape=jax.ShapeDtypeStruct((row_block * LANES // parts + 8, pairs * PATCH), BF16),
        in_specs=[VMEM] * 3,
        out_specs=VMEM,
        scratch_shapes=[pltpu.VMEM((devices * tiles * row_block, LANES), F32)],
        compiler_params=PARAMS,
        cost_estimate=cost(3),
        name="order_patches",
    )(x, perm, rim)


def dft_table(order):
    counter = jnp.arange(order, dtype=jnp.int32)
    turn_count = counter[:, None] * counter[None, :] % order
    radians = turn_count.astype(F32) * (2.0 * math.pi / order)
    return jnp.stack([jnp.cos(radians), jnp.sin(radians)])


def make_patches(first, length):
    devices = lax.axis_size(ALL)
    inner, pairs, row_block, _ = first.shape
    channels = pairs // 2
    if inner % devices == 0 and 2 * inner == PATCH and inner // devices * pairs in range(2, 17, 2):
        own = inner // devices
        moved = lax.all_to_all(
            first.reshape(devices, own, pairs, row_block, LANES), ALL, 0, 0, tiled=True
        )
        moved = lax.all_to_all(run_second(moved, length), ALL, 0, 0, tiled=True)
        return run_order(moved, inner, channels)
    flat = first.transpose(1, 2, 0, 3).reshape(2, channels, row_block, inner * LANES)
    flat = lax.all_to_all(flat, ALL, split_axis=3, concat_axis=2, tiled=True).astype(F32)
    mixed = jnp.einsum(
        "rcuq,kum->krcqm", flat, dft_table(row_block * devices), precision=lax.Precision.HIGHEST
    )
    series = jnp.stack([mixed[0, 0] - mixed[1, 1], mixed[1, 0] + mixed[0, 1]])
    series = (series * (1.0 / math.sqrt(length))).astype(BF16)
    series = lax.all_to_all(series, ALL, split_axis=4 - 1, concat_axis=2, tiled=True)
    parts = PATCH // inner
    series = series.reshape(2, channels, inner, parts, LANES // parts, row_block)
    patches = series.transpose(5, 4, 0, 1, 3, 2).reshape(
        row_block * LANES // parts, 2 * channels * PATCH
    )
    reps = lax.axis_size("rep")
    tail = patches[patches.shape[0] - 8 :]
    rim = jnp.zeros_like(tail)
    for r in range(reps):
        pairs = [(i - 1, i + r) for i in range(reps, devices, reps)]
        rim = rim + lax.ppermute(tail, ALL, pairs)
    return jnp.concatenate([patches, rim], 0)


def norm_rows(values, total):
    return lax.rsqrt(jnp.sum(values * values, axis=-1, keepdims=True) * (1.0 / total) + EPSILON)


def silu(values):
    half = 0.5 * values
    return half + half * jnp.tanh(half)


def fold(ends, count, head, entering, upto=None):
    state = entering.shape[0]
    for i in range(count):
        part, decay = ends[0][0:state], ends[0][state : state + 1]
        for j in range(1, len(ends)):
            here = (head ^ i) == j
            part = jnp.where(here, ends[j][0:state], part)
            decay = jnp.where(here, ends[j][state : state + 1], decay)
        after = decay * entering + part
        entering = after if upto is None else jnp.where(i < upto, after, entering)
    return entering


def expand(values, spread):
    high, low = split(values)
    return mm(jnp.concatenate([high, low], axis=1), spread[...])


def block_states(heads, per, reps, before, final, me_ref, *refs):
    pats, refs = refs[:2], refs[2:]
    halo, we, nin, wx, wbc, wdt, dtb, alog, cx, cbc, spread = refs[:11]
    earlier, refs = refs[11 : 11 + before], refs[11 + before :]
    normed_ref, x_ref, b_ref, c_ref, cum_ref, local_ref, grown_ref, st_ref = refs[:8]
    xs, bcs, carried, total, low_tri, dts, rows, tail = refs[-8:]
    block = pl.program_id(0)
    state = wbc.shape[1] // 2
    taps = cx.shape[0]

    gains = nin[...].astype(F32)
    gains = jnp.concatenate([gains[i : i + 1] for i in range(gains.shape[0])], axis=1)

    def features(p):
        embedded = mm(p, we[...]).astype(BF16).astype(F32)
        scale = norm_rows(embedded, embedded.shape[-1])
        return (embedded * scale * gains).astype(BF16)

    @pl.when(block == 0)
    def _():
        carried[...] = jnp.zeros_like(carried)
        total[...] = jnp.zeros_like(total)
        tail[...] = jnp.zeros_like(tail)
        tail[8:16] = halo[...].astype(F32)
        ri = lax.broadcasted_iota(jnp.int32, (SPAN, SPAN), 0)
        ci = lax.broadcasted_iota(jnp.int32, (SPAN, SPAN), 1)
        low_tri[...] = jnp.where(ri >= ci, 1.0, 0.0).astype(BF16)
        dts[...] = jnp.zeros_like(dts)
        rows[...] = jnp.zeros_like(rows)
        rows[0:1, 0:heads] = dtb[...]
        rows[1:2, 0:heads] = -jnp.exp(alog[...])

    here = ((block // per) ^ lax.rem(me_ref[0], reps)) == 0
    span = pats[0].shape[0]
    patch = jnp.where(here, pats[0][...], pats[1][...]).astype(F32)
    joined = features(jnp.concatenate([tail[...], patch], axis=0).astype(BF16))
    tail[...] = patch[span - 16 :]
    normed = joined[16:]
    normed_ref[...] = normed
    dts[:, 0:heads] = lax.dot_general(
        normed, wdt[...], (((1,), (1,)), ((), ())), preferred_element_type=F32
    )
    bcs[...] = mm(joined, wbc[...]).astype(BF16).astype(F32)
    xs[...] = mm(joined, wx[...]).astype(BF16).astype(F32)
    step_all = dts[...] + rows[0:1]
    step_all = jnp.maximum(step_all, 0.0) + jnp.log1p(jnp.exp(-jnp.abs(step_all)))

    def conv(buffer, kernel, at):
        out = kernel[0:1] * buffer[at + 17 - taps : at + 17 - taps + SPAN]
        for i in range(1, taps):
            out = out + kernel[i : i + 1] * buffer[at + 17 - taps + i : at + 17 - taps + i + SPAN]
        return silu(out)

    for n in range(span // SPAN):
        at = n * SPAN
        step = step_all[at : at + SPAN]
        rated = step * rows[1:2]
        one = rated.astype(BF16).astype(F32)
        two = (rated - one).astype(BF16).astype(F32)
        three = rated - one - two
        packed = one + pltpu.roll(two, heads, 1) + pltpu.roll(three, 2 * heads, 1)
        sums = mm(low_tri[...], packed.astype(BF16))
        cum = sums + pltpu.roll(sums, LANES - heads, 1) + pltpu.roll(sums, LANES - 2 * heads, 1)
        head_lane = lax.broadcasted_iota(jnp.int32, (SPAN, LANES), 1)
        packed = jnp.where(head_lane < heads, cum, pltpu.roll(step, heads, 1))
        cum_ref[at : at + SPAN] = packed
        last = cum[SPAN - 1 : SPAN]
        weights = expand(jnp.exp(last - cum) * step, spread)
        grow = expand(
            jnp.exp(jnp.concatenate([jnp.broadcast_to(last, (8, LANES)), total[...]], axis=0)), spread
        )
        bc = conv(bcs, cbc, at)
        b_ref[at : at + SPAN] = bc[:, :state].astype(BF16)
        c_ref[at : at + SPAN] = bc[:, state:].astype(BF16)
        bt = bc[:, :state].T.astype(BF16)
        xc = conv(xs, cx, at).astype(BF16)
        x_ref[at : at + SPAN] = xc
        weighted = (xc.astype(F32) * weights).astype(BF16)
        local_ref[n] = carried[...]
        grown_ref[n] = grow[8:16]
        carried[...] = carried[...] * grow[0:1] + mm(bt, weighted)
        total[...] = total[...] + last

    @pl.when(block == pl.num_programs(0) - 1)
    def _():
        st_ref[0:state] = carried[...]
        st_ref[state : state + 8] = grow[8:16] * grow[0:8]
        if final:
            everything = [e[...] for e in earlier] + [st_ref[...]]
            count = len(everything)
            send = refs[8]
            zero = jnp.zeros((state, xs.shape[1]), F32)
            send[0:state] = fold(everything, count, lax.div(me_ref[0], reps), zero).astype(BF16)
            decay = everything[0][state : state + 8]
            for e in everything[1:]:
                decay = decay * e[state : state + 8]
            send[state : state + 8] = decay.astype(BF16)


def run_states(me, pats, halo, consts, heads, inner, state, own, earlier, final):
    rows_in, width = pats[0].shape
    model = consts[0].shape[1]
    tokens = own * len(pats)
    span = min(own, TILE)
    per = own // span
    blocks = tokens // SPAN
    subs = span // SPAN
    row = lambda n: pl.BlockSpec((span, n), lambda b, me: (b, 0))
    fixed = pl.BlockSpec((state + 8, inner), lambda b, me: (0, 0))
    shape = lambda *d, t=F32: jax.ShapeDtypeStruct(d, t)
    return pl.pallas_call(
        functools.partial(block_states, heads, per, len(pats), len(earlier), final),
        grid_spec=pltpu.PrefetchScalarGridSpec(
            num_scalar_prefetch=1,
            grid=(tokens // span,),
            in_specs=[pl.BlockSpec((span, width), lambda b, me: (b % per, 0))] * len(pats)
            + [pl.BlockSpec((8, width), lambda b, me: (own // 8, 0))]
            + [VMEM] * (len(consts) + len(earlier)),
            out_specs=[row(model), row(inner), row(state), row(state), row(LANES),
                       pl.BlockSpec((subs, state, inner), lambda b, me: (b, 0, 0)),
                       pl.BlockSpec((subs, 8, inner), lambda b, me: (b, 0, 0)), fixed]
            + [fixed] * final,
            scratch_shapes=[
                pltpu.VMEM((span + 16, inner), F32),
                pltpu.VMEM((span + 16, 2 * state), F32),
                pltpu.VMEM((state, inner), F32),
                pltpu.VMEM((8, LANES), F32),
                pltpu.VMEM((SPAN, SPAN), BF16),
                pltpu.VMEM((span, LANES), F32),
                pltpu.VMEM((8, LANES), F32),
                pltpu.VMEM((16, width), F32),
            ],
        ),
        out_shape=[
            shape(tokens, model, t=BF16), shape(tokens, inner, t=BF16), shape(tokens, state, t=BF16),
            shape(tokens, state, t=BF16), shape(tokens, LANES),
            shape(blocks, state, inner), shape(blocks, 8, inner), shape(state + 8, inner),
        ] + [shape(state + 8, inner, t=BF16)] * final,
        compiler_params=PARAMS,
        cost_estimate=cost(13),
        name="block_states",
    )(me, *pats, halo, *consts, *earlier)


def gate_tokens(normed_ref, wz, pat_ref, we, gate_ref, embed_ref):
    @pl.when(pl.program_id(0) == 0)
    def _():
        embed_ref[...] = mm(pat_ref[...], we[...]).astype(BF16)

    gate_ref[...] = silu(mm(normed_ref[...], wz[...]).astype(BF16).astype(F32)).astype(BF16)


def run_gate(normed, wz, patches, we, own):
    tokens, width = normed.shape
    inner = wz.shape[1]
    span = min(tokens, TILE)
    return pl.pallas_call(
        gate_tokens,
        grid=(tokens // span,),
        in_specs=[pl.BlockSpec((span, width), lambda b: (b, 0)), VMEM,
                  pl.BlockSpec((own, patches.shape[1]), lambda b: (0, 0)), VMEM],
        out_specs=[pl.BlockSpec((span, inner), lambda b: (b, 0)),
                   pl.BlockSpec((own, we.shape[1]), lambda b: (0, 0))],
        out_shape=[jax.ShapeDtypeStruct((tokens, inner), BF16),
                   jax.ShapeDtypeStruct((own, we.shape[1]), BF16)],
        compiler_params=PARAMS,
        cost_estimate=cost(4),
        name="gate_tokens",
    )(normed, wz, patches, we)


def outputs(
    heads, chip, chips, seqs, reps, which, gated, opening, me_ref, normed_ref, x_ref, b_ref, c_ref, cum_ref, local_ref, grown_ref,
    *refs,
):
    if not gated:
        wz, refs = refs[0], refs[1:]
    spread, refs = refs[0], refs[1:]
    if opening:
        ends, earlier, refs = refs[:chips], refs[chips : chips + seqs], refs[chips + seqs :]
        entries, refs = refs[:chips], refs[chips:]
        start = entries[chip]
    else:
        start, refs = refs[0], refs[1:]
    outs, y_acc = refs[:-1], refs[-1]
    state = c_ref.shape[1]
    block = pl.program_id(0)
    per = pl.num_programs(0) // len(which)

    if opening:
        @pl.when(block == 0)
        def _():
            entering = jnp.zeros((state, x_ref.shape[1]), F32)
            for part in reversed(earlier):
                entering = part[0:state].astype(F32) + part[state : state + 1].astype(F32) * entering
            place = lax.div(me_ref[0], reps)
            known = [e[...] for e in ends]
            for c in range(chips):
                entries[c][...] = fold(known, chips - 1, place, entering, place ^ c)

    cum = cum_ref[...]
    log_cum = cum * LOG2E
    back = (log_cum - jnp.log2(pltpu.roll(cum, LANES - heads, 1))).T
    gram = lax.dot_general(
        c_ref[...], b_ref[...], (((1,), (1,)), ((), ())), preferred_element_type=F32
    )
    if gated:
        gate = normed_ref[...].astype(F32)
    else:
        gate = silu(mm(normed_ref[...], wz[...]).astype(BF16).astype(F32))
    half = SPAN // 2
    ri = lax.broadcasted_iota(jnp.int32, (half, half), 0)
    ci = lax.broadcasted_iota(jnp.int32, (half, half), 1)
    inside = ri >= ci
    head_dim = x_ref.shape[1] // heads
    for h in range(heads):
        cols = slice(h * head_dim, (h + 1) * head_dim)
        upper, lower = log_cum[:half, h : h + 1], log_cum[half:, h : h + 1]
        early, late = back[h : h + 1, :half], back[h : h + 1, half:]
        first = jnp.where(inside, jnp.exp2(upper - early), 0.0) * gram[:half, :half]
        cross = jnp.exp2(lower - early) * gram[half:, :half]
        second = jnp.where(inside, jnp.exp2(lower - late), 0.0) * gram[half:, half:]
        y_acc[:half, cols] = mm(first.astype(BF16), x_ref[:half, cols])
        y_acc[half:, cols] = mm(
            jnp.concatenate([cross.astype(BF16), second.astype(BF16)], axis=1), x_ref[:, cols]
        )
    cm = c_ref[...]
    high, low = split(local_ref[0] + grown_ref[0, 0:1] * start[...])
    added = mm(jnp.concatenate([cm, cm], axis=1), jnp.concatenate([high, low], axis=0))
    value = ((y_acc[...] + expand(jnp.exp(jnp.minimum(cum, 0.0)), spread) * added) * gate).astype(BF16)
    whole = 0
    for n, r in enumerate(which):
        if chip or not r:
            @pl.when(block // per == n)
            def _(whole=whole):
                outs[whole][pl.ds(pl.multiple_of((block % per) * SPAN, SPAN), SPAN), :] = value
            whole += 1
    for n, r in enumerate(which):
        if not chip and r:
            for i in range(len(outs) - whole):
                @pl.when(block == whole * per + i)
                def _(i=i):
                    outs[whole + i][...] = value
            break


def run_outputs(heads, chip, chips, reps, which, me, gate, xc, bm, cm, cum, local, grown, wz, spread, enter, own):
    tokens, inner = xc.shape
    state = cm.shape[1]
    per = own // SPAN
    gated, opening = wz is None, isinstance(enter, tuple)
    ends, earlier = enter if opening else ([], [])
    shapes = []
    for r in which:
        shapes += [(own, inner)] if chip or not r else [(SPAN, inner)] * per
    at = lambda b, me: (lax.rem(me[0], reps) ^ (which[0] + b // per)) * per + b % per
    row = lambda n: pl.BlockSpec((SPAN, n), lambda b, me: (at(b, me), 0))
    block3 = lambda b, me: (at(b, me), 0, 0)
    fixed = lambda shape: pl.BlockSpec(shape, lambda b, me: (0, 0))
    firsts = [(state, inner)] * chips if opening else []
    extra = ([] if gated else [wz]) + [spread] + (list(ends) + list(earlier) if opening else [enter])
    return pl.pallas_call(
        functools.partial(outputs, heads, chip, chips, len(earlier), reps, which, gated, opening),
        grid_spec=pltpu.PrefetchScalarGridSpec(
            num_scalar_prefetch=1,
            grid=(len(which) * per,),
            in_specs=[row(a.shape[1]) for a in (gate, xc, bm, cm, cum)]
            + [pl.BlockSpec((1, state, inner), block3), pl.BlockSpec((1, 8, inner), block3)]
            + [VMEM] * len(extra),
            out_specs=[fixed(shape) for shape in firsts + shapes],
            scratch_shapes=[pltpu.VMEM((SPAN, inner), F32)],
        ),
        out_shape=[jax.ShapeDtypeStruct(shape, F32) for shape in firsts]
        + [jax.ShapeDtypeStruct(shape, BF16) for shape in shapes],
        compiler_params=PARAMS,
        cost_estimate=cost(0.05),
        name="outputs",
    )(me, gate, xc, bm, cm, cum, local, grown, *extra)


def pick_gains(norm, index, count):
    values = norm[...].astype(F32)
    each = values.shape[0] // count
    gains = None
    for j in range(count):
        row = jnp.concatenate([values[j * each + i : j * each + i + 1] for i in range(each)], axis=1)
        gains = row if gains is None else jnp.where(index == j, row, gains)
    return gains


def mix_most(sizes, share, me_ref, *refs):
    (norm, weight, mixed_ref, square_ref), refs = refs[-4:], refs[:-4]
    step = pl.program_id(0)
    parts = []
    for size in sizes:
        parts.append(refs[:size])
        refs = refs[size:]
    count = len(parts)
    whole = lambda n: jnp.concatenate([p[...] for p in parts[n]], axis=0).astype(F32)

    @pl.when(step == 0)
    def _():
        square = None
        for n in range(count):
            v = whole(n)
            square = v * v if square is None else square + v * v
        square_ref[...] = jnp.broadcast_to(jnp.sum(square, axis=-1, keepdims=True), square_ref.shape)

    gains = pick_gains(norm, me_ref[0] ^ step, share)
    for n in range(count):
        @pl.when(step == n)
        def _(n=n):
            got = mm((whole(n) * gains).astype(BF16), weight[0])
            mixed_ref[...] = got if n == 0 else mixed_ref[...] + got


def mix_last(total, share, me_ref, embed_ref, mixed_ref, square_ref, part_ref, norm, weight, out_ref):
    v = part_ref[...].astype(F32)
    gains = pick_gains(norm, me_ref[0] ^ (share - 1), share)
    got = mm((v * gains).astype(BF16), weight[0])
    square = square_ref[:, 0:1] + jnp.sum(v * v, axis=-1, keepdims=True)
    scale = lax.rsqrt(square * (1.0 / total) + EPSILON)
    out_ref[...] = (embed_ref[...].astype(F32) + scale * (mixed_ref[...] + got)).astype(BF16)


def run_mix(me, embed, parts, norm_out, w_out):
    share = len(parts)
    count = share - 1
    parts = [p if isinstance(p, list) else [p] for p in parts]
    sizes = [len(p) for p in parts[:count]]
    most = [v for p in parts[:count] for v in p]
    (final,) = parts[count]
    own, inner = final.shape
    width = w_out.shape[1]
    norms = norm_out.reshape(-1, LANES)
    weights = w_out.reshape(share, inner, width)
    full = pl.BlockSpec((own, width), lambda d, me: (0, 0))
    mixed, square = pl.pallas_call(
        functools.partial(mix_most, sizes, share),
        grid_spec=pltpu.PrefetchScalarGridSpec(
            num_scalar_prefetch=1,
            grid=(count,),
            in_specs=[VMEM] * (len(most) + 1)
            + [pl.BlockSpec((1, inner, width), lambda d, me: (me[0] ^ d, 0, 0))],
            out_specs=[full, pl.BlockSpec((own, LANES), lambda d, me: (0, 0))],
        ),
        out_shape=[jax.ShapeDtypeStruct((own, width), F32),
                   jax.ShapeDtypeStruct((own, LANES), F32)],
        compiler_params=PARAMS,
        cost_estimate=cost(0.05),
        name="mix_most",
    )(me, *most, norms, weights)
    tile = SPAN
    row = lambda n: pl.BlockSpec((tile, n), lambda i, me: (i, 0))
    return pl.pallas_call(
        functools.partial(mix_last, share * inner, share),
        grid_spec=pltpu.PrefetchScalarGridSpec(
            num_scalar_prefetch=1,
            grid=(own // tile,),
            in_specs=[row(width), row(width), row(LANES), row(inner),
                      VMEM, pl.BlockSpec((1, inner, width), lambda i, me: (me[0] ^ count, 0, 0))],
            out_specs=row(width),
        ),
        out_shape=jax.ShapeDtypeStruct((own, width), BF16),
        compiler_params=PARAMS,
        cost_estimate=cost(3),
        name="mix_last",
    )(me, embed, mixed, square, final, norms, weights)


def swap(value, flip):
    count = lax.axis_size(HR)
    return lax.ppermute(value, HR, [(i, i ^ flip) for i in range(count)])


def shift(value, by):
    count = lax.axis_size("seq")
    return lax.ppermute(value, "seq", [(i, i + by) for i in range(count - by)])


def on_device(
    spectrum, src_amp, src_phase, src_mode, src_delay, src_bins, w_embed, norm_in, w_z, w_x, w_bc, w_dt,
    dt_bias, a_log, conv_x, conv_bc, norm_out, w_out,
):
    devices = lax.axis_size(ALL)
    share = lax.axis_size(HR)
    rows_all = spectrum.shape[2] * devices
    length = rows_all * spectrum.shape[3]
    pos = lax.axis_index(ALL).astype(jnp.int32).reshape(1)
    me = lax.axis_index(HR).astype(jnp.int32).reshape(1)
    first = run_first(
        spectrum, src_amp, src_phase, src_mode, src_delay, src_bins, pos, rows_all, length
    )
    patches = make_patches(first, length)
    own = patches.shape[0] - 8
    reps, chips = lax.axis_size("rep"), lax.axis_size("head")
    heads, inner, state = dt_bias.shape[0], w_x.shape[1], w_bc.shape[1] // 2
    spread = np.zeros((2 * LANES, inner), ml_dtypes.bfloat16)
    for h in range(heads):
        spread[h, h * (inner // heads) : (h + 1) * (inner // heads)] = 1
    spread[LANES:] = spread[:LANES]
    consts = (
        w_embed, norm_in.reshape(-1, LANES), w_x, w_bc, w_dt.T, dt_bias[None], a_log[None], conv_x, conv_bc,
        jnp.asarray(spread),
    )
    done, ends = [], []
    base = [patches] + [swap(patches, c * reps) for c in range(1, chips)]
    for c in range(chips):
        start = base[c]
        if ends:
            start, ends[-1] = lax.optimization_barrier((start, ends[-1]))
        group = [start] + [swap(start, r) for r in range(1, reps)]
        got = run_states(
            me, group, start, consts, heads, inner, state, own, ends, c == chips - 1
        )
        done.append(got[:7])
        ends.append(got[7])
    send = got[8]
    earlier = [shift(send, d) for d in range(1, lax.axis_size("seq"))]
    parts = [None] * share
    gate = None
    enter = (ends, earlier)
    for c in list(range(1, chips)) + [0]:
        normed, xc, bm, cm, cum, local, grown = done[c]
        if gate is not None:
            normed, gate = lax.optimization_barrier((normed, gate))
        ahead = normed
        if c == 1:
            ahead, embed = run_gate(normed, w_z, patches, w_embed, own)
        values = []
        for which in ([[r] for r in range(reps)] if c else [list(range(reps))]):
            got = run_outputs(
                heads, c, chips, reps, which, me, ahead, xc, bm, cm, cum, local, grown,
                None if c == 1 else w_z, spread, enter if isinstance(enter, tuple) else enter[c], own,
            )
            if isinstance(enter, tuple):
                enter, got = list(got[:chips]), list(got[chips:])
            values += got
            if c:
                ahead, values[-1] = lax.optimization_barrier((ahead, values[-1]))
        gate = values[-1]
        for r in reversed(range(reps)):
            d = c * reps + r
            if c or not r:
                parts[d] = swap(values[r], d) if d else values[0]
            else:
                per = own // SPAN
                pieces = values[1 + (r - 1) * per : 1 + r * per]
                parts[d] = [swap(v, d) for v in pieces]
    return run_mix(me, embed, parts, norm_out, w_out)


def solution(mesh):
    in_specs = (
        P("grp", None, ("seq", "head", "rep"), None),
        P("grp", None),
        P("grp"),
        P("grp"),
        P("grp"),
        P("grp", None),
        P(),
        P(),
        P(None, ("head", "rep")),
        P(None, ("head", "rep")),
        P(),
        P(None, ("head", "rep")),
        P(("head", "rep")),
        P(("head", "rep")),
        P(None, ("head", "rep")),
        P(),
        P(),
        P(),
    )
    out_specs = P(("grp", "seq", "head", "rep"), None)
    return jax.shard_map(
        on_device, mesh=mesh, in_specs=in_specs, out_specs=out_specs, check_vma=False
    )
```
